32 devices in a mesh: grp: 4 (over y, x), slab: 8 (over z, core).
Axes of the slice: x: 2, y: 2, z: 4, core: 2. Of those that a mesh axis runs over, the one named last changes fastest.
Arguments:
- grain_ids: int32 [2097152], P(('grp', 'slab')), may hold values from 0 to 16383, as said below
- orientation: float32 [4, 2097152], P(None, ('grp', 'slab')), may hold values from -2 to 2, as said below
- stress: float32 [9, 2097152], P(None, ('grp', 'slab')), may hold values from -8 to 8
- owner_blocks: int32 [256], replicated, may hold values from 0 to 255, each once
Outputs:
- grain_table: float32 [13, 16384], P(None, ('grp', 'slab'))
- fluctuation: bfloat16 [13, 2097152], P(None, ('grp', 'slab'))
The draws below stay inside these ranges and needn't reach their ends.
Inputs may be any that keep to these rules, and one draw needn't show every extreme that they name: `grain_ids`: the grain of point x is floor(x / 128) - 1, floor(x / 128) or floor(x / 128) + 1, and both outer cases occur in every draw; ids never fall from one point to the next, and every grain has 16 points or more. `orientation`: the first component of every quaternion is 0.4 or more.
All inputs are finite; a program needn't handle non-finite values.
Results may differ from the reference program's by a relative error of at most 0.012.
The reference program's roundings to bfloat16 on the way (of `lookup`) count: a program that leaves them out, or rounds other values in their place, can miss the bound.
Values may be sent and summed in bfloat16 or wider, within the bound.
No kernel may reach another device: no remote copies, remote signals or barrier semaphores. Data moves between devices by JAX's collectives and lax.ppermute only.
A program may use at most 64 MiB of HBM per device.

```python
import jax
import jax.numpy as jnp
from jax import lax

AVG = 128
BLK = 64
GD = 512
JITTER = 56
POINTS = 2097152
GRAINS = 16384
NBLK = 256


def grain_boundaries(key):
    grain_index = jnp.arange(GRAINS + 1, dtype=jnp.int32)
    jitter = jax.random.randint(jax.random.fold_in(key, 11), (GRAINS + 1,), -JITTER, JITTER + 1, dtype=jnp.int32)
    forced_up = jax.random.randint(jax.random.fold_in(key, 12), (), 1, JITTER + 1, dtype=jnp.int32)
    forced_down = jax.random.randint(jax.random.fold_in(key, 13), (), 1, JITTER + 1, dtype=jnp.int32)
    jitter = jnp.where(grain_index == GD, forced_up, jitter)
    jitter = jnp.where(grain_index == 2 * GD, -forced_down, jitter)
    jitter = jnp.where((grain_index == 0) | (grain_index == GRAINS), 0, jitter)
    return grain_index * AVG + jitter


def grains_of_points(key):
    boundaries = grain_boundaries(key)
    positions = jnp.arange(POINTS, dtype=jnp.int32)
    return (jnp.searchsorted(boundaries, positions, side='right') - 1).astype(jnp.int32)


def draw_grain_ids(key, part):
    return grains_of_points(key)


def draw_orientation(key, part):
    grain_ids = grains_of_points(key)
    grain_first = jax.random.uniform(jax.random.fold_in(key, 21), (GRAINS,), jnp.float32, 0.5, 1.0)
    grain_rest = 0.4 * jax.random.normal(jax.random.fold_in(key, 22), (3, GRAINS), jnp.float32)
    noise_first = jax.random.uniform(jax.random.fold_in(key, 23), (1, POINTS), jnp.float32, -0.1, 0.1)
    noise_rest = 0.15 * jax.random.normal(jax.random.fold_in(key, 24), (3, POINTS), jnp.float32)
    first_row = grain_first[grain_ids][None, :] + noise_first
    other_rows = grain_rest[:, grain_ids] + noise_rest
    return jnp.clip(jnp.concatenate([first_row, other_rows], axis=0), -2.0, 2.0).astype(jnp.float32)


def draw_stress(key, part):
    grain_ids = grains_of_points(key)
    grain_part = jax.random.normal(jax.random.fold_in(key, 31), (9, GRAINS), jnp.float32)
    noise = 0.5 * jax.random.normal(jax.random.fold_in(key, 32), (9, POINTS), jnp.float32)
    return jnp.clip(grain_part[:, grain_ids] + noise, -8.0, 8.0).astype(jnp.float32)


def setup_inputs(seed: int = 0) -> dict:
    splits = jax.random.split(jax.random.key(seed), 5)
    grain_ids = draw_grain_ids(jax.random.fold_in(splits[4], 71), 0)
    orientation = draw_orientation(jax.random.fold_in(splits[4], 71), 0)
    stress = draw_stress(jax.random.fold_in(splits[4], 71), 0)
    owner_blocks = jax.random.permutation(splits[3], NBLK).astype(jnp.int32)
    return {"grain_ids": grain_ids, "orientation": orientation, "stress": stress, "owner_blocks": owner_blocks}


def finish(totals):
    counts = totals[0:1]
    quat_sum = totals[1:5]
    stress_sum = totals[5:14]
    mean_quat = quat_sum / jnp.sqrt(lax.optimization_barrier(jnp.sum(quat_sum * quat_sum, axis=0, keepdims=True)))
    mean_stress = stress_sum / counts
    return jnp.concatenate([mean_quat, mean_stress], axis=0)

def reference(grain_ids, orientation, stress, owner_blocks):
    points = grain_ids.shape[0]
    values = jnp.concatenate([jnp.ones((1, points), jnp.float32), orientation, stress], axis=0)
    totals = jax.ops.segment_sum(values.T, grain_ids, num_segments=GRAINS).T
    finished = finish(totals)
    grain_table = finished.reshape(13, NBLK, BLK)[:, owner_blocks].reshape(13, GRAINS)
    lookup = finished.astype(jnp.bfloat16)
    grain_means = lookup[:, grain_ids].astype(jnp.float32)
    unit_quat = orientation / jnp.sqrt(lax.optimization_barrier(jnp.sum(orientation * orientation, axis=0, keepdims=True)))
    point_part = jnp.concatenate([unit_quat, stress], axis=0)
    fluctuation = (point_part - grain_means).astype(jnp.bfloat16)
    return (grain_table, fluctuation)
```

```python
import functools

import jax
import jax.numpy as jnp
from jax import lax
from jax.experimental import pallas as pl
from jax.experimental.pallas import tpu as pltpu
from jax.sharding import PartitionSpec as P

AVG = 128
AXES = ("grp", "slab")
SUB = 8
WINDOW = 16
ROWS = 16
COUNT = 13
F32 = jnp.float32
BF16 = jnp.bfloat16


def window_sums(ids_ref, orientation, stress, first_tile, first_grain):
    grain_row = lax.broadcasted_iota(jnp.int32, (WINDOW, AVG), 0) + first_grain
    tiles = stress.shape[1] // AVG
    picks = []
    for tile in range(tiles):
        ids = jnp.broadcast_to(ids_ref[pl.ds(first_tile + tile, 1), :], (WINDOW, AVG))
        picks.append((ids == grain_row).astype(F32).astype(BF16))
    selector = jnp.concatenate(picks, axis=1)
    ones = jnp.ones((ROWS - COUNT, stress.shape[1]), F32)
    values = jnp.concatenate([orientation, stress, ones], axis=0)
    high = values.astype(BF16)
    low = (values - high.astype(F32)).astype(BF16)
    dims = (((1,), (1,)), ((), ()))
    return lax.dot_general(
        selector, high, dims, preferred_element_type=F32
    ) + lax.dot_general(selector, low, dims, preferred_element_type=F32)


def rim_kernel(tile_base, ids_lo, ids_hi, q_lo, q_hi, s_lo, s_hi, lower_ref, upper_ref, *, tiles):
    base = tile_base[0]
    low = window_sums(ids_lo, q_lo[...], s_lo[...], 0, base - 1)
    high = window_sums(ids_hi, q_hi[...], s_hi[...], ids_hi.shape[0] - 2, base + tiles - 1)
    square = ((0, AVG - WINDOW), (0, AVG - ROWS))
    lower_ref[...] = jnp.pad(low, square).T[:ROWS]
    upper_ref[...] = jnp.pad(high, square).T[:ROWS]


def sum_kernel(tile_base, ids_ref, q_ref, s_ref, out_ref, acc_ref, carry_ref):
    step = pl.program_id(0)
    tiles = ids_ref.shape[0]

    @pl.when(step == 0)
    def _():
        carry_ref[...] = jnp.zeros_like(carry_ref)

    carry = carry_ref[...]
    for sub in range(tiles // SUB):
        points = slice(sub * SUB * AVG, (sub + 1) * SUB * AVG)
        first = tile_base[0] + step * tiles + sub * SUB - 1
        sums = window_sums(ids_ref, q_ref[:, points], s_ref[:, points], sub * SUB, first)
        row = pl.multiple_of(step * tiles + sub * SUB, SUB)
        acc_ref[pl.ds(row, SUB), :ROWS] = carry + sums[:SUB]
        carry = sums[SUB:]
    carry_ref[...] = carry

    @pl.when(step == pl.num_programs(0) - 1)
    def _():
        total = pl.num_programs(0) * tiles
        acc_ref[pl.ds(pl.multiple_of(total, SUB), SUB), :ROWS] = carry
        for part in range(out_ref.shape[1] // AVG):
            block = acc_ref[part * AVG : (part + 1) * AVG, :]
            out_ref[:, part * AVG : (part + 1) * AVG] = block.T[:ROWS]


def finish_kernel(edge, part_ref, below_ref, above_ref, table_ref, window_ref, *, grains, blk):
    part = part_ref[...]
    lane = lax.broadcasted_iota(jnp.int32, (ROWS, AVG), 1)
    below = jnp.where((lane < 2) & (edge[0] > 0), below_ref[...], 0.0)
    above = jnp.where((lane < 2) & (edge[1] > 0), above_ref[...], 0.0)
    gap = jnp.zeros((ROWS, grains), F32)
    part = part + jnp.concatenate([below, gap], axis=1) + jnp.concatenate([gap, above], axis=1)
    row = lax.broadcasted_iota(jnp.int32, part.shape, 0)
    squares = jnp.sum(jnp.where(row < 4, part * part, 0.0), axis=0, keepdims=True)
    done = jnp.where(row < 4, part / jnp.sqrt(squares), part / part[COUNT : COUNT + 1])
    rounded = done.astype(BF16).astype(F32)
    for index in range(window_ref.shape[0]):
        window_ref[index] = rounded[:, index * blk : index * blk + AVG]
    own = rounded[:, 1 : 1 + grains]
    half = lax.broadcasted_iota(jnp.int32, (8, AVG), 1) < blk
    for pair in range(grains // AVG):
        top = own[:8, pair * AVG : (pair + 1) * AVG]
        low = own[8:, pair * AVG : (pair + 1) * AVG]
        first = jnp.where(half, top, pltpu.roll(low, blk, 1))
        second = jnp.where(half, pltpu.roll(top, blk, 1), low)
        table_ref[2 * pair] = first.astype(BF16)
        table_ref[2 * pair + 1] = second.astype(BF16)


def fluctuation_kernel(tile_base, ids_ref, q_ref, s_ref, window_ref, out_ref, *, blk):
    step = pl.program_id(0)
    tiles = ids_ref.shape[0]
    for tile in range(tiles):
        points = slice(tile * AVG, (tile + 1) * AVG)
        index = tile // blk
        base = tile_base[0] + step * tiles + index * blk - 1
        ids = jnp.broadcast_to(ids_ref[tile : tile + 1, :] - base, (8, AVG))
        means = jnp.concatenate(
            [
                jnp.take_along_axis(window_ref[index, :8], ids, axis=1),
                jnp.take_along_axis(window_ref[index, 8:], ids, axis=1),
            ],
            axis=0,
        )
        q = q_ref[:, points]
        unit = q / jnp.sqrt(jnp.sum(q * q, axis=0, keepdims=True))
        point_part = jnp.concatenate([unit, s_ref[:, points]], axis=0)
        out_ref[:, points] = (point_part - means[:COUNT]).astype(BF16)


def route_kernel(blocks_ref, place, held_ref, out_ref):
    slabs, per_device = out_ref.shape[:2]
    for slab in range(slabs):
        for slot in range(per_device):
            block = blocks_ref[(place[0] * slabs + slab) * per_device + slot]
            group = block // (slabs * per_device)
            out_ref[slab, slot] = held_ref[group, block % per_device]


def place_kernel(blocks_ref, place, got_ref, out_ref, *, blk):
    slabs, per_device = got_ref.shape[:2]
    half = lax.broadcasted_iota(jnp.int32, (8, AVG), 1) < blk

    def pick(slot):
        block = blocks_ref[place[0] * per_device + slot]
        slab = lax.rem(block // per_device, slabs)
        return got_ref[slab, slot].astype(F32)

    for pair in range(per_device // 2):
        first, second = pick(2 * pair), pick(2 * pair + 1)
        lanes = slice(pair * AVG, (pair + 1) * AVG)
        out_ref[:8, lanes] = jnp.where(half, first, pltpu.roll(second, blk, 1))
        low = jnp.where(half, pltpu.roll(first, blk, 1), second)
        out_ref[8:, lanes] = low[: COUNT - 8]


def local(grain_ids, orientation, stress, owner_blocks):
    groups, slabs = lax.axis_size("grp"), lax.axis_size("slab")
    devices = groups * slabs
    group, slab = lax.axis_index("grp"), lax.axis_index("slab")
    device = group * slabs + slab
    points = grain_ids.shape[0]
    tiles = points // AVG
    grains = tiles
    per_device = owner_blocks.shape[0] // devices
    blk = grains // per_device
    step_tiles = min(tiles, blk)
    steps = tiles // step_tiles
    step_points = step_tiles * AVG
    width = grains + AVG

    ids = grain_ids.reshape(tiles, AVG)
    tile_base = (device * tiles).astype(jnp.int32).reshape(1)
    smem = pl.BlockSpec(memory_space=pltpu.SMEM)
    vmem = pl.BlockSpec(memory_space=pltpu.VMEM)

    edge_tiles = 8
    edge_points = 2 * AVG
    last = tiles // edge_tiles - 1
    last_points = points // edge_points - 1
    lower, upper = pl.pallas_call(
        functools.partial(rim_kernel, tiles=tiles),
        out_shape=[jax.ShapeDtypeStruct((ROWS, AVG), F32)] * 2,
        grid=(1,),
        in_specs=[
            smem,
            pl.BlockSpec((edge_tiles, AVG), lambda i: (0, 0)),
            pl.BlockSpec((edge_tiles, AVG), lambda i: (last, 0)),
            pl.BlockSpec((4, edge_points), lambda i: (0, 0)),
            pl.BlockSpec((4, edge_points), lambda i: (0, last_points)),
            pl.BlockSpec((9, edge_points), lambda i: (0, 0)),
            pl.BlockSpec((9, edge_points), lambda i: (0, last_points)),
        ],
        out_specs=[pl.BlockSpec((ROWS, AVG), lambda i: (0, 0))] * 2,
        name="rims",
    )(tile_base, ids, ids, orientation, orientation, stress, stress)

    above = lax.ppermute(lower, AXES, [(d, (d - 1) % devices) for d in range(devices)])
    below = lax.ppermute(upper, AXES, [(d, (d + 1) % devices) for d in range(devices)])

    stream = [
        smem,
        pl.BlockSpec((step_tiles, AVG), lambda i: (i, 0)),
        pl.BlockSpec((4, step_points), lambda i: (0, i)),
        pl.BlockSpec((9, step_points), lambda i: (0, i)),
    ]
    part = pl.pallas_call(
        sum_kernel,
        out_shape=jax.ShapeDtypeStruct((ROWS, width), F32),
        grid=(steps,),
        in_specs=stream,
        out_specs=pl.BlockSpec((ROWS, width), lambda i: (0, 0)),
        scratch_shapes=[pltpu.VMEM((width, AVG), F32), pltpu.VMEM((SUB, ROWS), F32)],
        cost_estimate=pl.CostEstimate(
            flops=64 * points * ROWS, bytes_accessed=4 * points * ROWS, transcendentals=0
        ),
        name="sums",
    )(tile_base, ids, orientation, stress)

    edge = jnp.stack([device, devices - 1 - device]).astype(jnp.int32)
    table, windows = pl.pallas_call(
        functools.partial(finish_kernel, grains=grains, blk=blk),
        out_shape=[
            jax.ShapeDtypeStruct((per_device, 8, AVG), BF16),
            jax.ShapeDtypeStruct((tiles // blk, ROWS, AVG), F32),
        ],
        in_specs=[smem, vmem, vmem, vmem],
        out_specs=[vmem, vmem],
        name="finish",
    )(edge, part, below, above)

    fluctuation = pl.pallas_call(
        functools.partial(fluctuation_kernel, blk=blk),
        out_shape=jax.ShapeDtypeStruct((COUNT, points), BF16),
        grid=(steps,),
        in_specs=stream
        + [pl.BlockSpec((step_tiles // blk, ROWS, AVG), lambda i: (i, 0, 0))],
        out_specs=pl.BlockSpec((COUNT, step_points), lambda i: (0, i)),
        cost_estimate=pl.CostEstimate(
            flops=64 * points * ROWS, bytes_accessed=6 * points * ROWS, transcendentals=0
        ),
        name="fluctuation",
    )(tile_base, ids, orientation, stress, windows)

    held = lax.all_gather(table, "grp", axis=0)
    sent = pl.pallas_call(
        route_kernel,
        out_shape=jax.ShapeDtypeStruct((slabs, per_device, 8, AVG), BF16),
        in_specs=[smem, smem, vmem],
        out_specs=vmem,
        name="route",
    )(owner_blocks, group.astype(jnp.int32).reshape(1), held)
    got = lax.all_to_all(sent, "slab", 0, 0, tiled=True)
    grain_table = pl.pallas_call(
        functools.partial(place_kernel, blk=blk),
        out_shape=jax.ShapeDtypeStruct((COUNT, grains), F32),
        in_specs=[smem, smem, vmem],
        out_specs=vmem,
        name="place",
    )(owner_blocks, device.astype(jnp.int32).reshape(1), got)
    return (grain_table, fluctuation)


def solution(mesh):
    placed = (P(AXES), P(None, AXES), P(None, AXES), P())
    return jax.shard_map(
        local,
        mesh=mesh,
        in_specs=placed,
        out_specs=(P(None, AXES), P(None, AXES)),
        check_vma=False,
    )
```

```python
import functools

import jax
import jax.numpy as jnp
from jax import lax
from jax.experimental import pallas as pl
from jax.experimental.pallas import tpu as pltpu
from jax.sharding import PartitionSpec as P

AVG = 128
AXES = ("grp", "slab")
SUB = 8
WINDOW = 16
ROWS = 16
COUNT = 13
EDGE = 2
F32 = jnp.float32
BF16 = jnp.bfloat16


def window_sums(ids_ref, values, first_tile, first_grain):
    grain_row = lax.broadcasted_iota(jnp.int32, (WINDOW, AVG), 0) + first_grain
    picks = []
    for tile in range(values.shape[1] // AVG):
        ids = jnp.broadcast_to(ids_ref[pl.ds(first_tile + tile, 1), :], (WINDOW, AVG))
        picks.append((ids == grain_row).astype(F32).astype(BF16))
    selector = jnp.concatenate(picks, axis=1)
    high = values.astype(BF16)
    low = (values - high.astype(F32)).astype(BF16)
    dims = (((1,), (1,)), ((), ()))
    return lax.dot_general(
        selector, high, dims, preferred_element_type=F32
    ) + lax.dot_general(selector, low, dims, preferred_element_type=F32)


def finish(total):
    row = lax.broadcasted_iota(jnp.int32, total.shape, 0)
    squares = jnp.sum(jnp.where(row < 4, total * total, 0.0), axis=0, keepdims=True)
    return total / jnp.where(row < 4, jnp.sqrt(squares), total[COUNT : COUNT + 1])


def look_up(top, low, ids):
    ids = jnp.broadcast_to(ids, (8, AVG))
    return jnp.concatenate([jnp.take_along_axis(half, ids, axis=1) for half in (top, low)], axis=0)


def sum_kernel(
    tile_base, ids_hbm, q_hbm, s_hbm, table_ref, window_ref, point_ref, ids_ref, q_ref, s_ref, acc_ref, sems,
    *, chunks, blk,
):
    tiles = ids_hbm.shape[0] // chunks
    points = tiles * AVG
    grains = chunks * tiles

    def copies(chunk):
        rows = pl.ds(pl.multiple_of(chunk * tiles, tiles), tiles)
        lanes = pl.ds(pl.multiple_of(chunk * points, points), points)
        return (
            pltpu.make_async_copy(ids_hbm.at[rows], ids_ref.at[rows], sems.at[0, chunk]),
            pltpu.make_async_copy(q_hbm.at[:, lanes], q_ref.at[:, lanes], sems.at[1, chunk]),
            pltpu.make_async_copy(s_hbm.at[:, lanes], s_ref.at[:, lanes], sems.at[2, chunk]),
        )

    for chunk in range(chunks):
        for copy in copies(chunk):
            copy.start()

    row = lax.broadcasted_iota(jnp.int32, (8, SUB * AVG), 0)
    ones = jnp.ones((ROWS - COUNT, SUB * AVG), F32)

    def step(chunk, carry):
        for copy in copies(chunk):
            copy.wait()
        for sub in range(tiles // SUB):
            tile = pl.multiple_of(chunk * tiles + sub * SUB, SUB)
            lanes = pl.ds(pl.multiple_of(tile * AVG, SUB * AVG), SUB * AVG)
            values = jnp.concatenate([q_ref[:, lanes], s_ref[:, lanes], ones], axis=0)
            sums = window_sums(ids_ref, values, tile, tile_base[0] + tile - 1)
            acc_ref[pl.ds(tile, SUB), :ROWS] = carry + sums[:SUB]
            carry = sums[SUB:]
            top = values[:8]
            squares = jnp.sum(jnp.where(row < 4, top * top, 0.0), axis=0, keepdims=True)
            point_ref[:8, lanes] = top * jnp.where(row < 4, lax.rsqrt(squares), 1.0)
            point_ref[8:, lanes] = values[8:]
        return carry

    carry = lax.fori_loop(0, chunks, step, jnp.zeros((SUB, ROWS), F32))
    acc_ref[grains : grains + SUB, :ROWS] = carry
    part = jnp.concatenate(
        [acc_ref[block * AVG : (block + 1) * AVG, :].T[:ROWS] for block in range(grains // AVG + 1)], axis=1
    )
    rounded = finish(part).astype(BF16).astype(F32)
    for index in range(window_ref.shape[0]):
        window_ref[index] = rounded[:, index * blk : index * blk + AVG]
    own = rounded[:, 1 : 1 + grains]
    half = lax.broadcasted_iota(jnp.int32, (8, AVG), 1) < blk
    for pair in range(grains // AVG):
        top = own[:8, pair * AVG : (pair + 1) * AVG]
        low = own[8:, pair * AVG : (pair + 1) * AVG]
        table_ref[2 * pair] = jnp.where(half, top, pltpu.roll(low, blk, 1)).astype(BF16)
        table_ref[2 * pair + 1] = jnp.where(half, pltpu.roll(top, blk, 1), low).astype(BF16)
    lane = lax.broadcasted_iota(jnp.int32, (ROWS, AVG), 1)
    ends = jnp.where(lane < 2, part[:, :AVG], pltpu.roll(part[:, grains:], 2, 1))
    high = ends.astype(BF16).astype(F32)
    mid = (ends - high).astype(BF16).astype(F32)
    rest = ends - high - mid
    pieces = jnp.where(lane < 4, high, jnp.where(lane < 8, pltpu.roll(mid, 4, 1), pltpu.roll(rest, 8, 1)))
    pieces = jnp.where(lane < 12, pieces, 0.0)
    table_ref[grains // blk] = jnp.where(half, pieces[:8], pltpu.roll(pieces[8:], blk, 1)).astype(BF16)


def fluctuation_kernel(
    tile_base, ids_ref, point_ref, window_ref, out_hbm, edge_ids_ref, edge_point_ref, edge_window_ref, out_ref, sems
):
    windows = window_ref.shape[0]
    total = ids_ref.shape[0]
    tiles = total // windows
    points = tiles * AVG

    def copy(window):
        lanes = pl.ds(pl.multiple_of(window * points, points), points)
        return pltpu.make_async_copy(out_ref.at[:, lanes], out_hbm.at[:, lanes], sems.at[window])

    def step(window, carry):
        base = tile_base[0] + window * tiles - 1
        top, low = window_ref[window, :8], window_ref[window, 8:]
        for index in range(tiles):
            tile = window * tiles + index
            lanes = pl.ds(pl.multiple_of(tile * AVG, AVG), AVG)
            value = point_ref[:, lanes] - look_up(top, low, ids_ref[pl.ds(tile, 1), :] - base)
            out_ref[:, lanes] = value[:COUNT].astype(BF16)
        copy(window).start()
        return carry

    lax.fori_loop(0, windows, step, 0)
    first, last = slice(0, EDGE), slice(total - EDGE, total)
    edge_ids_ref[:EDGE] = ids_ref[first] - (tile_base[0] - 1)
    edge_ids_ref[EDGE:] = ids_ref[last] - (tile_base[0] + total - tiles - 1)
    edge_point_ref[:, : EDGE * AVG] = point_ref[:, : EDGE * AVG]
    edge_point_ref[:, EDGE * AVG :] = point_ref[:, (total - EDGE) * AVG :]
    edge_window_ref[0] = window_ref[0]
    edge_window_ref[1] = window_ref[windows - 1]
    for window in range(windows):
        copy(window).wait()


def route_kernel(blocks_ref, place, *refs):
    *held_refs, out_ref, held_ref = refs
    groups = len(held_refs)
    slabs, slots = out_ref.shape[:2]
    per_device = slots - 1
    for offset, ref in enumerate(held_refs):
        held_ref[partner(place[0], offset, groups)] = ref[...]
    for slab in range(slabs):
        for slot in range(per_device):
            block = blocks_ref[(place[0] * slabs + slab) * per_device + slot]
            out_ref[slab, slot] = held_ref[block // (slabs * per_device), block % per_device]
    step = AVG // 2 // groups
    lane = lax.broadcasted_iota(jnp.int32, (8, AVG), 1) % (AVG // 2)
    ends = jnp.zeros((8, AVG), F32)
    for group in range(groups):
        rolled = pltpu.roll(held_ref[group, per_device].astype(F32), group * step, 1)
        ends = jnp.where((lane >= group * step) & (lane < group * step + 12), rolled, ends)
    for slab in range(slabs):
        out_ref[slab, per_device] = ends.astype(BF16)


def partner(group, offset, groups):
    if groups & (groups - 1) == 0:
        return group ^ offset
    return lax.rem(group + groups - offset, groups)


def place_kernel(
    blocks_ref, place, got_ref, edge_ids_ref, edge_point_ref, edge_window_ref, fluctuation_in, table_ref,
    fluctuation_hbm, edge_ref, sems, *, groups, blk,
):
    del fluctuation_in
    slabs, slots = got_ref.shape[:2]
    per_device = slots - 1
    devices = groups * slabs
    step = AVG // 2 // groups
    device = place[0]
    lane8 = lax.broadcasted_iota(jnp.int32, (8, AVG), 1)
    lane = lax.broadcasted_iota(jnp.int32, (ROWS, AVG), 1)
    half = lane8 < blk

    def ends(owner):
        inside = (owner >= 0) & (owner < devices)
        owner = jnp.clip(owner, 0, devices - 1)
        piece = got_ref[lax.rem(owner, slabs), per_device].astype(F32)
        piece = pltpu.roll(piece, lax.rem(AVG - step * (owner // slabs), AVG), 1)
        piece = piece + pltpu.roll(piece, AVG - 4, 1) + pltpu.roll(piece, AVG - 8, 1)
        piece = jnp.concatenate([piece, pltpu.roll(piece, blk, 1)], axis=0)
        return jnp.where(inside, piece, 0.0)

    def at(value, source, target):
        return pltpu.roll(value, (target - source) % AVG, 1)

    mine, below, above = ends(device), ends(device - 1), ends(device + 1)
    shared = jnp.where(lane < 2, mine + at(below, 2, 0), mine + at(above, 0, 2))
    shared = finish(shared).astype(BF16).astype(F32)
    first = jnp.where(lane < 2, shared, edge_window_ref[0])
    upper = edge_ref.shape[1] // AVG - 2 * EDGE
    last_lane = blk + upper
    last = jnp.where((lane >= last_lane) & (lane < last_lane + 2), at(shared, 2, last_lane), edge_window_ref[1])
    for tile in range(2 * EDGE):
        table = first if tile < EDGE else last
        lanes = slice(tile * AVG, (tile + 1) * AVG)
        value = edge_point_ref[:, lanes] - look_up(table[:8], table[8:], edge_ids_ref[tile : tile + 1, :])
        edge_ref[:, lanes] = value[:COUNT].astype(BF16)
    width = EDGE * AVG
    total = fluctuation_hbm.shape[1]
    copies = (
        pltpu.make_async_copy(edge_ref.at[:, :width], fluctuation_hbm.at[:, :width], sems.at[0]),
        pltpu.make_async_copy(edge_ref.at[:, width:], fluctuation_hbm.at[:, total - width :], sems.at[1]),
    )
    for copy in copies:
        copy.start()

    def pick(slot):
        block = blocks_ref[device * per_device + slot]
        owner, index = block // per_device, lax.rem(block, per_device)
        tile = got_ref[lax.rem(owner, slabs), slot].astype(F32)
        own = ends(owner)
        start = slot % 2 * blk
        low = at(own, 1, start) + at(ends(owner - 1), 3, start)
        high = at(own, 2, start + blk - 1) + at(ends(owner + 1), 0, start + blk - 1)
        is_low = (lane == start) & (index == 0)
        is_high = (lane == start + blk - 1) & (index == per_device - 1)
        return tile, jnp.where(is_low, low, high), is_low | is_high

    for pair in range(per_device // 2):
        (first, first_sums, first_mask), (second, second_sums, second_mask) = pick(2 * pair), pick(2 * pair + 1)
        lanes = slice(pair * AVG, (pair + 1) * AVG)
        top = jnp.where(half, first, pltpu.roll(second, blk, 1))
        low = jnp.where(half, pltpu.roll(first, blk, 1), second)
        repaired = finish(jnp.where(lane < blk, first_sums, second_sums))
        value = jnp.where(first_mask | second_mask, repaired, jnp.concatenate([top, low], axis=0))
        table_ref[:, lanes] = value[:COUNT]
    for copy in copies:
        copy.wait()


def local(grain_ids, orientation, stress, owner_blocks):
    groups, slabs = lax.axis_size("grp"), lax.axis_size("slab")
    group = lax.axis_index("grp")
    device = group * slabs + lax.axis_index("slab")
    points = grain_ids.shape[0]
    tiles = points // AVG
    grains = tiles
    per_device = owner_blocks.shape[0] // (groups * slabs)
    blk = grains // per_device
    slots = per_device + 1

    ids = grain_ids.reshape(tiles, AVG)
    in_hbm = [pltpu.with_memory_space_constraint(x, pltpu.HBM) for x in (ids, orientation, stress)]
    place = device.astype(jnp.int32).reshape(1)
    tile_base = place * tiles
    smem = pl.BlockSpec(memory_space=pltpu.SMEM)
    vmem = pl.BlockSpec(memory_space=pltpu.VMEM)
    hbm = pl.BlockSpec(memory_space=pltpu.HBM)
    params = pltpu.CompilerParams(vmem_limit_bytes=20 << 20)

    chunks = 8
    table, windows, point = pl.pallas_call(
        functools.partial(sum_kernel, chunks=chunks, blk=blk),
        out_shape=[
            jax.ShapeDtypeStruct((slots, 8, AVG), BF16),
            jax.ShapeDtypeStruct((tiles // blk, ROWS, AVG), F32),
            jax.ShapeDtypeStruct((ROWS, points), F32),
        ],
        in_specs=[smem, hbm, hbm, hbm],
        out_specs=[vmem, vmem, vmem],
        scratch_shapes=[
            pltpu.VMEM((tiles, AVG), jnp.int32),
            pltpu.VMEM((4, points), F32),
            pltpu.VMEM((9, points), F32),
            pltpu.VMEM((grains + AVG, AVG), F32),
            pltpu.SemaphoreType.DMA((3, chunks)),
        ],
        compiler_params=params,
        cost_estimate=pl.CostEstimate(
            flops=64 * points * ROWS, bytes_accessed=4 * points * ROWS, transcendentals=0
        ),
        name="sums",
    )(tile_base, *in_hbm)

    held = [table]
    for offset in range(1, groups):
        moves = [(int(partner(g, offset, groups)), g) for g in range(groups)]
        held.append(lax.ppermute(table, "grp", moves))

    fluctuation, edge_ids, edge_point, edge_windows = pl.pallas_call(
        fluctuation_kernel,
        out_shape=[
            jax.ShapeDtypeStruct((COUNT, points), BF16),
            jax.ShapeDtypeStruct((2 * EDGE, AVG), jnp.int32),
            jax.ShapeDtypeStruct((ROWS, 2 * EDGE * AVG), F32),
            jax.ShapeDtypeStruct((2, ROWS, AVG), F32),
        ],
        in_specs=[smem, vmem, vmem, vmem],
        out_specs=[hbm, vmem, vmem, vmem],
        scratch_shapes=[
            pltpu.VMEM((COUNT, points), BF16),
            pltpu.SemaphoreType.DMA((tiles // blk,)),
        ],
        compiler_params=params,
        cost_estimate=pl.CostEstimate(
            flops=64 * points * ROWS, bytes_accessed=6 * points * ROWS, transcendentals=0
        ),
        name="fluctuation",
    )(tile_base, ids, point, windows)

    held, edge_ids = lax.optimization_barrier((held, edge_ids))
    sent = pl.pallas_call(
        route_kernel,
        out_shape=jax.ShapeDtypeStruct((slabs, slots, 8, AVG), BF16),
        in_specs=[smem, smem] + [vmem] * groups,
        out_specs=vmem,
        scratch_shapes=[pltpu.VMEM((groups, slots, 8, AVG), BF16)],
        compiler_params=params,
        name="route",
    )(owner_blocks, group.astype(jnp.int32).reshape(1), *held)
    got = lax.all_to_all(sent, "slab", 0, 0, tiled=True)
    grain_table, fluctuation = pl.pallas_call(
        functools.partial(place_kernel, groups=groups, blk=blk),
        out_shape=[
            jax.ShapeDtypeStruct((COUNT, grains), F32),
            jax.ShapeDtypeStruct((COUNT, points), BF16),
        ],
        in_specs=[smem, smem, vmem, vmem, vmem, vmem, hbm],
        out_specs=[vmem, hbm],
        scratch_shapes=[pltpu.VMEM((COUNT, 2 * EDGE * AVG), BF16), pltpu.SemaphoreType.DMA((2,))],
        input_output_aliases={6: 1},
        compiler_params=params,
        name="place",
    )(owner_blocks, place, got, edge_ids, edge_point, edge_windows, fluctuation)
    return (grain_table, fluctuation)


def solution(mesh):
    placed = (P(AXES), P(None, AXES), P(None, AXES), P())
    return jax.shard_map(
        local,
        mesh=mesh,
        in_specs=placed,
        out_specs=(P(None, AXES), P(None, AXES)),
        check_vma=False,
    )
```

```python
import functools

import jax
import jax.numpy as jnp
from jax import lax
from jax.experimental import pallas as pl
from jax.experimental.pallas import tpu as pltpu
from jax.sharding import PartitionSpec as P

AVG = 128
AXES = ("grp", "slab")
SUB = 8
WINDOW = 16
ROWS = 16
COUNT = 13
CORES = 2
EDGE = 2
F32 = jnp.float32
BF16 = jnp.bfloat16


def window_sums(selector, values):
    high = values.astype(BF16)
    low = (values - high.astype(F32)).astype(BF16)
    dims = (((1,), (1,)), ((), ()))
    return lax.dot_general(
        selector, high, dims, preferred_element_type=F32
    ) + lax.dot_general(selector, low, dims, preferred_element_type=F32)


def finish(total):
    row = lax.broadcasted_iota(jnp.int32, total.shape, 0)
    squares = jnp.sum(jnp.where(row < 4, total * total, 0.0), axis=0, keepdims=True)
    scale = jnp.where(row < 4, jnp.sqrt(squares), total[COUNT : COUNT + 1])
    return total / jnp.where(scale > 0.0, scale, 1.0)


def div_rem(x, n):
    if n & (n - 1) == 0:
        return x >> (n.bit_length() - 1), x & (n - 1)
    return lax.div(x, n), lax.rem(x, n)


def selection(ids_ref, first_tile, tiles, first_grain):
    grain_row = lax.broadcasted_iota(jnp.int32, (WINDOW, AVG), 0) + first_grain
    picks = []
    for tile in range(tiles):
        ids = jnp.broadcast_to(ids_ref[pl.ds(first_tile + tile, 1), :], (WINDOW, AVG))
        picks.append((ids == grain_row).astype(F32).astype(BF16))
    return jnp.concatenate(picks, axis=1)


def sum_kernel(
    tile_base, ids_hbm, q_hbm, s_hbm, table_ref, window_ref, point_ref, ids_ref, q_ref, s_ref, acc_ref, sems,
    *, chunks, blk,
):
    tiles = ids_hbm.shape[0] // chunks
    points = tiles * AVG
    grains = chunks * tiles

    def copies(chunk):
        rows = pl.ds(pl.multiple_of(chunk * tiles, tiles), tiles)
        quads = pl.ds(pl.multiple_of(chunk * tiles * 4, tiles * 4), tiles * 4)
        lanes = pl.ds(pl.multiple_of(chunk * points, points), points)
        return (
            pltpu.make_async_copy(ids_hbm.at[rows], ids_ref.at[rows], sems.at[0, chunk]),
            pltpu.make_async_copy(q_hbm.at[quads], q_ref.at[quads], sems.at[1, chunk]),
            pltpu.make_async_copy(s_hbm.at[:, lanes], s_ref.at[:, lanes], sems.at[2, chunk]),
        )

    for chunk in range(chunks):
        for copy in copies(chunk):
            copy.start()

    quaternion = lax.broadcasted_iota(jnp.int32, (8, AVG), 0) < 4
    ones = jnp.ones((ROWS - COUNT, SUB * AVG), F32)

    def step(chunk, carry):
        for copy in copies(chunk):
            copy.wait()
        for sub in range(tiles // SUB):
            tile = pl.multiple_of(chunk * tiles + sub * SUB, SUB)
            lanes = pl.ds(pl.multiple_of(tile * AVG, SUB * AVG), SUB * AVG)
            quad = pl.multiple_of(tile * 4, 4 * SUB)
            q = jnp.concatenate([q_ref[pl.ds(quad + 4 * t, 4), :] for t in range(SUB)], axis=1)
            values = jnp.concatenate([q, s_ref[:, lanes], ones], axis=0)
            sums = window_sums(selection(ids_ref, tile, SUB, tile_base[0] + tile - 1), values)
            acc_ref[pl.ds(tile, SUB), :ROWS] = carry + sums[:SUB]
            carry = sums[SUB:]
            parts = [q_ref[pl.ds(quad + c, SUB, stride=4), :] for c in range(4)]
            scale = lax.rsqrt(sum(part * part for part in parts))
            scales = [
                jnp.where(quaternion, jnp.broadcast_to(scale[t : t + 1], (8, AVG)), 1.0) for t in range(SUB)
            ]
            point_ref[:8, lanes] = values[:8] * jnp.concatenate(scales, axis=1)
            point_ref[8:, lanes] = values[8:]
        return carry

    carry = lax.fori_loop(0, chunks, step, jnp.zeros((SUB, ROWS), F32))
    acc_ref[grains : grains + SUB, :ROWS] = carry
    part = jnp.concatenate(
        [acc_ref[block * AVG : (block + 1) * AVG, :].T[:ROWS] for block in range(grains // AVG + 1)], axis=1
    )
    rounded = finish(part).astype(BF16).astype(F32)
    for index in range(window_ref.shape[0]):
        window_ref[index] = rounded[:, index * blk : index * blk + AVG]
    own = rounded[:, 1 : 1 + grains]
    half = lax.broadcasted_iota(jnp.int32, (8, AVG), 1) < blk
    for pair in range(grains // AVG):
        top = own[:8, pair * AVG : (pair + 1) * AVG]
        low = own[8:, pair * AVG : (pair + 1) * AVG]
        table_ref[2 * pair] = jnp.where(half, top, pltpu.roll(low, blk, 1)).astype(BF16)
        table_ref[2 * pair + 1] = jnp.where(half, pltpu.roll(top, blk, 1), low).astype(BF16)
    lane = lax.broadcasted_iota(jnp.int32, (ROWS, AVG), 1)
    ends = jnp.where(lane < 2, part[:, :AVG], pltpu.roll(part[:, grains:], 2, 1))
    high = ends.astype(BF16).astype(F32)
    mid = (ends - high).astype(BF16).astype(F32)
    rest = ends - high - mid
    pieces = jnp.where(lane < 4, high, jnp.where(lane < 8, pltpu.roll(mid, 4, 1), pltpu.roll(rest, 8, 1)))
    pieces = jnp.where(lane < 12, pieces, 0.0)
    table_ref[grains // blk] = jnp.where(half, pieces[:8], pltpu.roll(pieces[8:], blk, 1)).astype(BF16)


def fluctuation_kernel(
    tile_base, ids_ref, point_ref, window_ref, out_hbm, edge_ids_ref, edge_point_ref, edge_window_ref, out_ref, sems
):
    windows = window_ref.shape[0]
    total = ids_ref.shape[0]
    tiles = total // windows
    points = tiles * AVG

    def copy(window):
        lanes = pl.ds(pl.multiple_of(window * points, points), points)
        return pltpu.make_async_copy(out_ref.at[:, lanes], out_hbm.at[:, lanes], sems.at[window])

    def step(window, carry):
        table = window_ref[window]
        for sub in range(tiles // SUB):
            tile = pl.multiple_of(window * tiles + sub * SUB, SUB)
            lanes = pl.ds(pl.multiple_of(tile * AVG, SUB * AVG), SUB * AVG)
            near = pltpu.roll(table, (AVG - sub * SUB) % AVG, 1)[:, :WINDOW].astype(BF16)
            picks = selection(ids_ref, tile, SUB, tile_base[0] + tile - 1)
            means = jnp.dot(near, picks, preferred_element_type=F32)
            out_ref[:, lanes] = (point_ref[:, lanes] - means)[:COUNT].astype(BF16)
        copy(window).start()
        return carry

    lax.fori_loop(0, windows, step, 0)
    first, last = slice(0, EDGE), slice(total - EDGE, total)
    edge_ids_ref[:EDGE] = ids_ref[first]
    edge_ids_ref[EDGE:] = ids_ref[last]
    edge_point_ref[:, : EDGE * AVG] = point_ref[:, : EDGE * AVG]
    edge_point_ref[:, EDGE * AVG :] = point_ref[:, (total - EDGE) * AVG :]
    edge_window_ref[0] = window_ref[0]
    edge_window_ref[1] = pltpu.roll(window_ref[windows - 1], AVG - tiles + SUB, 1)
    for window in range(windows):
        copy(window).wait()


def source(me, offset, count):
    if count & (count - 1) == 0:
        return me ^ offset
    return (me + count - offset) % count


def target(me, offset, count):
    if count & (count - 1) == 0:
        return me ^ offset
    return (me + offset) % count


def stack_kernel(place, *refs):
    *held_refs, out_ref = refs
    for offset, ref in enumerate(held_refs):
        out_ref[source(place[0], offset, len(held_refs))] = ref[...]


def route_kernel(blocks_ref, place, mine_ref, other_ref, *refs):
    *out_refs, held_ref = refs
    chips = len(out_refs)
    groups, slots = mine_ref.shape[:2]
    per_device = slots - 1
    slabs = chips * CORES
    group, slab = div_rem(place[0], slabs)
    chip, core = div_rem(slab, CORES)
    held_ref[core] = mine_ref[...]
    held_ref[1 - core] = other_ref[...]
    step = AVG // 2 // groups
    lane = lax.broadcasted_iota(jnp.int32, (8, AVG), 1) & (AVG // 2 - 1)
    for owner_core in range(CORES):
        ends = held_ref[owner_core, 0, per_device].astype(F32)
        for owner_group in range(1, groups):
            rolled = pltpu.roll(held_ref[owner_core, owner_group, per_device].astype(F32), owner_group * step, 1)
            ends = jnp.where(lane >= owner_group * step, rolled, ends)
        for out_ref in out_refs:
            out_ref[per_device + owner_core] = ends.astype(BF16)
    for offset, out_ref in enumerate(out_refs):
        wanted = (group * slabs + target(chip, offset, chips) * CORES + core) * per_device
        for slot in range(per_device):
            owner, index = div_rem(blocks_ref[wanted + slot], per_device)
            owner_group, owner_slab = div_rem(owner, slabs)
            out_ref[slot] = held_ref[div_rem(owner_slab, CORES)[1], owner_group, index]


def place_kernel(blocks_ref, place, *refs, groups, chips, blk):
    (*got_refs, edge_ids_ref, edge_point_ref, edge_window_ref, _, table_ref, fluctuation_hbm, held_ref, ends_ref,
     edge_ref, sems) = refs
    slots = got_refs[0].shape[0]
    per_device = slots - CORES
    slabs = chips * CORES
    devices = groups * slabs
    grains = table_ref.shape[1]
    step = AVG // 2 // groups
    device = place[0]
    chip = div_rem(div_rem(device, slabs)[1], CORES)[0]
    lane = lax.broadcasted_iota(jnp.int32, (8, AVG), 1)
    half = lane < blk

    for offset, ref in enumerate(got_refs):
        owner_chip = source(chip, offset, chips)
        held_ref[owner_chip] = ref[...]
        for core in range(CORES):
            piece = ref[per_device + core].astype(F32)
            piece = piece + pltpu.roll(piece, AVG - 4, 1) + pltpu.roll(piece, AVG - 8, 1)
            ends_ref[owner_chip * CORES + core] = piece

    def ends(owner, column, lane):
        group, slab = div_rem(jnp.clip(owner, 0, devices - 1), slabs)
        moved = pltpu.roll(ends_ref[slab], (lane - column - step * group + 2 * AVG) & (AVG - 1), 1)
        return jnp.where((owner >= 0) & (owner < devices), moved, 0.0)

    def unfold(value):
        return jnp.concatenate([value, pltpu.roll(value, blk, 1)], axis=0)

    lane_half = lane & (blk - 1)
    others = jnp.where(lane_half < 2, ends(device - 1, 2, 0), ends(device + 1, 0, 2))
    shared = finish(unfold(ends(device, 0, 0) + others))
    wide_lane = lax.broadcasted_iota(jnp.int32, (ROWS, AVG), 1)
    first = jnp.where(wide_lane < 2, shared, edge_window_ref[0])
    in_last = (wide_lane >= SUB) & (wide_lane < SUB + 2)
    last = jnp.where(in_last, pltpu.roll(shared, SUB - 2, 1), edge_window_ref[1])
    width = EDGE * AVG
    total = fluctuation_hbm.shape[1]
    first_grain = device * grains - 1
    copies = []
    for end, (table, grain, begin) in enumerate(
        ((first, first_grain, 0), (last, first_grain + grains - SUB, total - width))
    ):
        lanes = slice(end * width, (end + 1) * width)
        picks = selection(edge_ids_ref, end * EDGE, EDGE, grain)
        means = jnp.dot(table[:, :WINDOW].astype(BF16), picks, preferred_element_type=F32)
        edge_ref[:, lanes] = (edge_point_ref[:, lanes] - means)[:COUNT].astype(BF16)
        copies.append(
            pltpu.make_async_copy(
                edge_ref.at[:, lanes], fluctuation_hbm.at[:, begin : begin + width], sems.at[end]
            )
        )
        copies[-1].start()

    tiles, columns = [], []
    sums = jnp.zeros((8, AVG), F32)
    for slot in range(per_device):
        owner, index = div_rem(blocks_ref[device * per_device + slot], per_device)
        owner_chip = div_rem(div_rem(owner, slabs)[1], CORES)[0]
        tiles.append(held_ref[owner_chip, slot].astype(F32))
        low = index == 0
        beside = jnp.where(low, owner - 1, owner + 1)
        both = ends(owner, jnp.where(low, 1, 2), slot) + ends(beside, jnp.where(low, 3, 0), slot)
        sums = jnp.where(lane_half == slot, both, sums)
        columns.append(jnp.where(low, 0, jnp.where(index == per_device - 1, blk - 1, 2 * AVG)))
    repaired = finish(unfold(sums))
    repaired = jnp.where(half, repaired[:8], pltpu.roll(repaired[8:], blk, 1))
    for slot in range(per_device):
        moved = pltpu.roll(repaired, (columns[slot] - slot + AVG) & (AVG - 1), 1)
        tiles[slot] = jnp.where(lane_half == columns[slot], moved, tiles[slot])
    for pair in range(per_device // 2):
        first, second = tiles[2 * pair], tiles[2 * pair + 1]
        lanes = slice(pair * AVG, (pair + 1) * AVG)
        table_ref[:8, lanes] = jnp.where(half, first, pltpu.roll(second, blk, 1))
        table_ref[8:, lanes] = jnp.where(half, pltpu.roll(first, blk, 1), second)[: COUNT - 8]
    for copy in copies:
        copy.wait()


def local(grain_ids, orientation, stress, owner_blocks):
    groups, slabs = lax.axis_size("grp"), lax.axis_size("slab")
    group = lax.axis_index("grp")
    device = group * slabs + lax.axis_index("slab")
    points = grain_ids.shape[0]
    tiles = points // AVG
    grains = tiles
    per_device = owner_blocks.shape[0] // (groups * slabs)
    blk = grains // per_device
    slots = per_device + 1
    chips = slabs // CORES

    ids = grain_ids.reshape(tiles, AVG)
    quads = orientation.reshape(4, tiles, AVG).transpose(1, 0, 2).reshape(4 * tiles, AVG)
    in_hbm = [pltpu.with_memory_space_constraint(x, pltpu.HBM) for x in (ids, quads, stress)]
    place = device.astype(jnp.int32).reshape(1)
    tile_base = place * tiles
    smem = pl.BlockSpec(memory_space=pltpu.SMEM)
    vmem = pl.BlockSpec(memory_space=pltpu.VMEM)
    hbm = pl.BlockSpec(memory_space=pltpu.HBM)
    params = pltpu.CompilerParams(vmem_limit_bytes=20 << 20)

    chunks = 8
    table, windows, point = pl.pallas_call(
        functools.partial(sum_kernel, chunks=chunks, blk=blk),
        out_shape=[
            jax.ShapeDtypeStruct((slots, 8, AVG), BF16),
            jax.ShapeDtypeStruct((tiles // blk, ROWS, AVG), F32),
            jax.ShapeDtypeStruct((ROWS, points), F32),
        ],
        in_specs=[smem, hbm, hbm, hbm],
        out_specs=[vmem, vmem, vmem],
        scratch_shapes=[
            pltpu.VMEM((tiles, AVG), jnp.int32),
            pltpu.VMEM((4 * tiles, AVG), F32),
            pltpu.VMEM((9, points), F32),
            pltpu.VMEM((grains + AVG, AVG), F32),
            pltpu.SemaphoreType.DMA((3, chunks)),
        ],
        compiler_params=params,
        cost_estimate=pl.CostEstimate(
            flops=64 * points * ROWS, bytes_accessed=4 * points * ROWS, transcendentals=0
        ),
        name="sums",
    )(tile_base, *in_hbm)

    held = [table]
    for offset in range(1, groups):
        moves = [(g, int(target(g, offset, groups))) for g in range(groups)]
        held.append(lax.ppermute(table, "grp", moves))

    fluctuation, edge_ids, edge_point, edge_windows = pl.pallas_call(
        fluctuation_kernel,
        out_shape=[
            jax.ShapeDtypeStruct((COUNT, points), BF16),
            jax.ShapeDtypeStruct((2 * EDGE, AVG), jnp.int32),
            jax.ShapeDtypeStruct((ROWS, 2 * EDGE * AVG), F32),
            jax.ShapeDtypeStruct((2, ROWS, AVG), F32),
        ],
        in_specs=[smem, vmem, vmem, vmem],
        out_specs=[hbm, vmem, vmem, vmem],
        scratch_shapes=[
            pltpu.VMEM((COUNT, points), BF16),
            pltpu.SemaphoreType.DMA((tiles // blk,)),
        ],
        compiler_params=params,
        cost_estimate=pl.CostEstimate(
            flops=64 * points * ROWS, bytes_accessed=6 * points * ROWS, transcendentals=0
        ),
        name="fluctuation",
    )(tile_base, ids, point, windows)

    held, edge_ids = lax.optimization_barrier((held, edge_ids))
    mine = pl.pallas_call(
        stack_kernel,
        out_shape=jax.ShapeDtypeStruct((groups, slots, 8, AVG), BF16),
        in_specs=[smem] + [vmem] * groups,
        out_specs=vmem,
        compiler_params=params,
        name="stack",
    )(group.astype(jnp.int32).reshape(1), *held)
    other = lax.ppermute(mine, "slab", [(s, s ^ 1) for s in range(slabs)])
    sent = pl.pallas_call(
        route_kernel,
        out_shape=[jax.ShapeDtypeStruct((per_device + CORES, 8, AVG), BF16)] * chips,
        in_specs=[smem, smem, vmem, vmem],
        out_specs=[vmem] * chips,
        scratch_shapes=[pltpu.VMEM((CORES, groups, slots, 8, AVG), BF16)],
        compiler_params=params,
        name="route",
    )(owner_blocks, place, mine, other)
    got = [sent[0]]
    for offset in range(1, chips):
        moves = [
            (chip * CORES + core, int(target(chip, offset, chips)) * CORES + core)
            for chip in range(chips)
            for core in range(CORES)
        ]
        got.append(lax.ppermute(sent[offset], "slab", moves))
    grain_table, fluctuation = pl.pallas_call(
        functools.partial(place_kernel, groups=groups, chips=chips, blk=blk),
        out_shape=[
            jax.ShapeDtypeStruct((COUNT, grains), F32),
            jax.ShapeDtypeStruct((COUNT, points), BF16),
        ],
        in_specs=[smem, smem] + [vmem] * (chips + 3) + [hbm],
        out_specs=[vmem, hbm],
        scratch_shapes=[
            pltpu.VMEM((chips, per_device + CORES, 8, AVG), BF16),
            pltpu.VMEM((slabs, 8, AVG), F32),
            pltpu.VMEM((COUNT, 2 * EDGE * AVG), BF16),
            pltpu.SemaphoreType.DMA((2,)),
        ],
        input_output_aliases={chips + 5: 1},
        compiler_params=params,
        name="place",
    )(owner_blocks, place, *got, edge_ids, edge_point, edge_windows, fluctuation)
    return (grain_table, fluctuation)


def solution(mesh):
    placed = (P(AXES), P(None, AXES), P(None, AXES), P())
    return jax.shard_map(
        local,
        mesh=mesh,
        in_specs=placed,
        out_specs=(P(None, AXES), P(None, AXES)),
        check_vma=False,
    )
```

```python
import functools

import jax
import jax.numpy as jnp
from jax import lax
from jax.experimental import pallas as pl
from jax.experimental.pallas import tpu as pltpu
from jax.sharding import PartitionSpec as P

AVG = 128
AXES = ("grp", "slab")
SUB = 8
WINDOW = 16
ROWS = 16
COUNT = 13
CORES = 2
EDGE = 2
F32 = jnp.float32
BF16 = jnp.bfloat16


def window_sums(selector, values):
    high = values.astype(BF16)
    low = (values - high.astype(F32)).astype(BF16)
    both = jnp.concatenate([high, low], axis=0)
    return lax.dot_general(selector, both, (((1,), (1,)), ((), ())), preferred_element_type=F32)


def finish(total):
    row = lax.broadcasted_iota(jnp.int32, total.shape, 0)
    squares = jnp.sum(jnp.where(row < 4, total * total, 0.0), axis=0, keepdims=True)
    scale = jnp.where(row < 4, jnp.sqrt(squares), total[COUNT : COUNT + 1])
    return total / jnp.where(scale > 0.0, scale, 1.0)


def device_index():
    return lax.axis_index("grp") * lax.axis_size("slab") + lax.axis_index("slab")


def div_rem(x, n):
    if n & (n - 1) == 0:
        return x >> (n.bit_length() - 1), x & (n - 1)
    return lax.div(x, n), lax.rem(x, n)


def selection(ids_ref, first_tile, tiles, first_grain):
    grain_row = lax.broadcasted_iota(jnp.int32, (WINDOW, AVG), 0) + first_grain
    picks = []
    for tile in range(tiles):
        ids = jnp.broadcast_to(ids_ref[pl.ds(first_tile + tile, 1), :], (WINDOW, AVG))
        picks.append((ids == grain_row).astype(F32).astype(BF16))
    return jnp.concatenate(picks, axis=1)


def sum_kernel(
    ids_hbm, q_hbm, s_hbm, table_ref, window_ref, point_ref, ids_ref, q_ref, s_ref, acc_ref, sems,
    *, chunks, blk,
):
    tiles = ids_hbm.shape[0] // chunks
    points = tiles * AVG
    grains = chunks * tiles
    tile_base = device_index() * grains

    def copies(chunk):
        rows = pl.ds(chunk * tiles, tiles)
        quads = pl.ds(chunk * tiles * 4, tiles * 4)
        lanes = pl.ds(chunk * points, points)
        return (
            pltpu.make_async_copy(ids_hbm.at[rows], ids_ref.at[rows], sems.at[0, chunk]),
            pltpu.make_async_copy(q_hbm.at[quads], q_ref.at[quads], sems.at[1, chunk]),
            pltpu.make_async_copy(s_hbm.at[:, lanes], s_ref.at[:, lanes], sems.at[2, chunk]),
        )

    for chunk in range(chunks):
        for copy in copies(chunk):
            copy.start()

    quaternion = lax.broadcasted_iota(jnp.int32, (8, AVG), 0) < 4
    ones = jnp.ones((ROWS - COUNT, SUB * AVG), F32)

    def step(chunk, carry):
        for copy in copies(chunk):
            copy.wait()
        for sub in range(tiles // SUB):
            tile = chunk * tiles + sub * SUB
            lanes = pl.ds(tile * AVG, SUB * AVG)
            quad = tile * 4
            q = jnp.concatenate([q_ref[pl.ds(quad + 4 * t, 4), :] for t in range(SUB)], axis=1)
            values = jnp.concatenate([q, s_ref[:, lanes], ones], axis=0)
            sums = window_sums(selection(ids_ref, tile, SUB, tile_base + tile - 1), values)
            acc_ref[pl.ds(tile, SUB), : 2 * ROWS] = carry + sums[:SUB]
            carry = sums[SUB:]
            parts = [q_ref[pl.ds(quad + c, SUB, stride=4), :] for c in range(4)]
            scale = lax.rsqrt(sum(part * part for part in parts))
            scales = [
                jnp.where(quaternion, jnp.broadcast_to(scale[t : t + 1], (8, AVG)), 1.0) for t in range(SUB)
            ]
            point_ref[:8, lanes] = values[:8] * jnp.concatenate(scales, axis=1)
            point_ref[8:, lanes] = values[8:]
        return carry

    carry = jnp.zeros((SUB, 2 * ROWS), F32)
    for chunk in range(chunks):
        carry = step(chunk, carry)
    acc_ref[grains : grains + SUB, : 2 * ROWS] = carry
    blocks = [acc_ref[block * AVG : (block + 1) * AVG, :].T for block in range(grains // AVG + 1)]
    part = jnp.concatenate([block[:ROWS] + block[ROWS : 2 * ROWS] for block in blocks], axis=1)
    rounded = finish(part).astype(BF16).astype(F32)
    for index in range(window_ref.shape[0]):
        window_ref[index] = rounded[:, index * blk : index * blk + AVG]
    own = rounded[:, 1 : 1 + grains]
    half = lax.broadcasted_iota(jnp.int32, (8, AVG), 1) < blk
    for pair in range(grains // AVG):
        top = own[:8, pair * AVG : (pair + 1) * AVG]
        low = own[8:, pair * AVG : (pair + 1) * AVG]
        table_ref[2 * pair] = jnp.where(half, top, pltpu.roll(low, blk, 1)).astype(BF16)
        table_ref[2 * pair + 1] = jnp.where(half, pltpu.roll(top, blk, 1), low).astype(BF16)
    lane = lax.broadcasted_iota(jnp.int32, (ROWS, AVG), 1)
    ends = jnp.where(lane < 2, part[:, :AVG], pltpu.roll(part[:, grains:], 2, 1))
    high = ends.astype(BF16).astype(F32)
    mid = (ends - high).astype(BF16).astype(F32)
    rest = ends - high - mid
    pieces = jnp.where(lane < 4, high, jnp.where(lane < 8, pltpu.roll(mid, 4, 1), pltpu.roll(rest, 8, 1)))
    pieces = jnp.where(lane < 12, pieces, 0.0)
    table_ref[grains // blk] = jnp.where(half, pieces[:8], pltpu.roll(pieces[8:], blk, 1)).astype(BF16)


def fluctuation_kernel(
    ids_ref, point_ref, window_ref, out_hbm, edge_ids_ref, edge_point_ref, edge_window_ref, out_ref, sems
):
    windows = window_ref.shape[0]
    total = ids_ref.shape[0]
    tile_base = device_index() * total
    tiles = total // windows
    points = tiles * AVG

    def copy(window):
        lanes = pl.ds(window * points, points)
        return pltpu.make_async_copy(out_ref.at[:, lanes], out_hbm.at[:, lanes], sems.at[window])

    def step(window):
        table = window_ref[window]
        for sub in range(tiles // SUB):
            tile = window * tiles + sub * SUB
            lanes = pl.ds(tile * AVG, SUB * AVG)
            near = pltpu.roll(table, (AVG - sub * SUB) % AVG, 1)[:, :WINDOW].astype(BF16)
            picks = selection(ids_ref, tile, SUB, tile_base + tile - 1)
            means = jnp.dot(near, picks, preferred_element_type=F32)
            out_ref[:, lanes] = (point_ref[:, lanes] - means)[:COUNT].astype(BF16)
        copy(window).start()

    for window in range(windows):
        step(window)
    first, last = slice(0, EDGE), slice(total - EDGE, total)
    edge_ids_ref[:EDGE] = ids_ref[first]
    edge_ids_ref[EDGE:] = ids_ref[last]
    edge_point_ref[:, : EDGE * AVG] = point_ref[:, : EDGE * AVG]
    edge_point_ref[:, EDGE * AVG :] = point_ref[:, (total - EDGE) * AVG :]
    edge_window_ref[0] = window_ref[0]
    edge_window_ref[1] = pltpu.roll(window_ref[windows - 1], AVG - tiles + SUB, 1)
    for window in range(windows):
        copy(window).wait()


def source(me, offset, count):
    if count & (count - 1) == 0:
        return me ^ offset
    return (me + count - offset) % count


def target(me, offset, count):
    if count & (count - 1) == 0:
        return me ^ offset
    return (me + offset) % count


def stack_kernel(*refs):
    *held_refs, out_ref = refs
    for offset, ref in enumerate(held_refs):
        out_ref[source(lax.axis_index("grp"), offset, len(held_refs))] = ref[...]


def route_kernel(blocks_any, mine_ref, other_ref, *refs):
    *out_refs, held_ref, blocks_ref, sem = refs
    copy = pltpu.make_async_copy(blocks_any, blocks_ref, sem)
    copy.start()
    chips = len(out_refs)
    groups, slots = mine_ref.shape[:2]
    per_device = slots - 1
    slabs = chips * CORES
    group = lax.axis_index("grp")
    chip, core = div_rem(lax.axis_index("slab"), CORES)
    held_ref[core] = mine_ref[...]
    held_ref[1 - core] = other_ref[...]
    step = AVG // 2 // groups
    lane = lax.broadcasted_iota(jnp.int32, (8, AVG), 1) & (AVG // 2 - 1)
    for owner_core in range(CORES):
        ends = held_ref[owner_core, 0, per_device].astype(F32)
        for owner_group in range(1, groups):
            rolled = pltpu.roll(held_ref[owner_core, owner_group, per_device].astype(F32), owner_group * step, 1)
            ends = jnp.where(lane >= owner_group * step, rolled, ends)
        for out_ref in out_refs:
            out_ref[per_device + owner_core] = ends.astype(BF16)
    copy.wait()
    for offset, out_ref in enumerate(out_refs):
        wanted = (group * slabs + target(chip, offset, chips) * CORES + core) * per_device
        for slot in range(per_device):
            owner, index = div_rem(blocks_ref[wanted + slot], per_device)
            owner_group, owner_slab = div_rem(owner, slabs)
            out_ref[slot] = held_ref[div_rem(owner_slab, CORES)[1], owner_group, index]


def place_kernel(blocks_any, *refs, groups, chips, blk):
    (*got_refs, edge_ids_ref, edge_point_ref, edge_window_ref, _, table_hbm, fluctuation_hbm, held_ref, ends_ref,
     edge_ref, table_ref, blocks_ref, sems) = refs
    blocks_copy = pltpu.make_async_copy(blocks_any, blocks_ref, sems.at[3])
    blocks_copy.start()
    slots = got_refs[0].shape[0]
    per_device = slots - CORES
    slabs = chips * CORES
    devices = groups * slabs
    grains = table_ref.shape[1]
    step = AVG // 2 // groups
    device = device_index()
    chip = div_rem(lax.axis_index("slab"), CORES)[0]
    lane = lax.broadcasted_iota(jnp.int32, (8, AVG), 1)
    half = lane < blk

    for offset, ref in enumerate(reversed(got_refs)):
        owner_chip = source(chip, offset, chips)
        held_ref[owner_chip] = ref[...]
        for core in range(CORES):
            piece = ref[per_device + core].astype(F32)
            piece = piece + pltpu.roll(piece, AVG - 4, 1) + pltpu.roll(piece, AVG - 8, 1)
            ends_ref[owner_chip * CORES + core] = piece

    def ends(owner, column, lane):
        group, slab = div_rem(jnp.clip(owner, 0, devices - 1), slabs)
        moved = pltpu.roll(ends_ref[slab], (lane - column - step * group + 2 * AVG) & (AVG - 1), 1)
        return jnp.where((owner >= 0) & (owner < devices), moved, 0.0)

    def unfold(value):
        return jnp.concatenate([value, pltpu.roll(value, blk, 1)], axis=0)

    lane_half = lane & (blk - 1)
    others = jnp.where(lane_half < 2, ends(device - 1, 2, 0), ends(device + 1, 0, 2))
    shared = finish(unfold(ends(device, 0, 0) + others))
    wide_lane = lax.broadcasted_iota(jnp.int32, (ROWS, AVG), 1)
    first = jnp.where(wide_lane < 2, shared, edge_window_ref[0])
    in_last = (wide_lane >= SUB) & (wide_lane < SUB + 2)
    last = jnp.where(in_last, pltpu.roll(shared, SUB - 2, 1), edge_window_ref[1])
    width = EDGE * AVG
    total = fluctuation_hbm.shape[1]
    first_grain = device * grains - 1
    copies = []
    for end, (table, grain, begin) in enumerate(
        ((first, first_grain, 0), (last, first_grain + grains - SUB, total - width))
    ):
        lanes = slice(end * width, (end + 1) * width)
        picks = selection(edge_ids_ref, end * EDGE, EDGE, grain)
        means = jnp.dot(table[:, :WINDOW].astype(BF16), picks, preferred_element_type=F32)
        edge_ref[:, lanes] = (edge_point_ref[:, lanes] - means)[:COUNT].astype(BF16)
        copies.append(
            pltpu.make_async_copy(
                edge_ref.at[:, lanes], fluctuation_hbm.at[:, begin : begin + width], sems.at[end]
            )
        )
        copies[-1].start()

    blocks_copy.wait()
    tiles, columns = [], []
    sums = jnp.zeros((8, AVG), F32)
    for slot in range(per_device):
        owner, index = div_rem(blocks_ref[device * per_device + slot], per_device)
        owner_chip = div_rem(div_rem(owner, slabs)[1], CORES)[0]
        tiles.append(held_ref[owner_chip, slot].astype(F32))
        low = index == 0
        beside = jnp.where(low, owner - 1, owner + 1)
        both = ends(owner, jnp.where(low, 1, 2), slot) + ends(beside, jnp.where(low, 3, 0), slot)
        sums = jnp.where(lane_half == slot, both, sums)
        columns.append(jnp.where(low, 0, jnp.where(index == per_device - 1, blk - 1, 2 * AVG)))
    repaired = finish(unfold(sums))
    repaired = jnp.where(half, repaired[:8], pltpu.roll(repaired[8:], blk, 1))
    for slot in range(per_device):
        moved = pltpu.roll(repaired, (columns[slot] - slot + AVG) & (AVG - 1), 1)
        tiles[slot] = jnp.where(lane_half == columns[slot], moved, tiles[slot])
    for pair in range(per_device // 2):
        first, second = tiles[2 * pair], tiles[2 * pair + 1]
        lanes = slice(pair * AVG, (pair + 1) * AVG)
        table_ref[:8, lanes] = jnp.where(half, first, pltpu.roll(second, blk, 1))
        table_ref[8:, lanes] = jnp.where(half, pltpu.roll(first, blk, 1), second)[: COUNT - 8]
    copies.append(pltpu.make_async_copy(table_ref, table_hbm, sems.at[2]))
    copies[-1].start()
    for copy in copies:
        copy.wait()


def local(grain_ids, orientation, stress, owner_blocks):
    groups, slabs = lax.axis_size("grp"), lax.axis_size("slab")
    points = grain_ids.shape[0]
    tiles = points // AVG
    grains = tiles
    per_device = owner_blocks.shape[0] // (groups * slabs)
    blk = grains // per_device
    slots = per_device + 1
    chips = slabs // CORES

    ids = grain_ids.reshape(tiles, AVG)
    quads = orientation.reshape(4, tiles, AVG).transpose(1, 0, 2).reshape(4 * tiles, AVG)
    in_hbm = [pltpu.with_memory_space_constraint(x, pltpu.HBM) for x in (ids, quads, stress)]
    anywhere = pl.BlockSpec(memory_space=pl.ANY)
    vmem = pl.BlockSpec(memory_space=pltpu.VMEM)
    hbm = pl.BlockSpec(memory_space=pltpu.HBM)
    params = pltpu.CompilerParams(vmem_limit_bytes=20 << 20)

    chunks = 8
    table, windows, point = pl.pallas_call(
        functools.partial(sum_kernel, chunks=chunks, blk=blk),
        out_shape=[
            jax.ShapeDtypeStruct((slots, 8, AVG), BF16),
            jax.ShapeDtypeStruct((tiles // blk, ROWS, AVG), F32),
            jax.ShapeDtypeStruct((ROWS, points), F32),
        ],
        in_specs=[hbm, hbm, hbm],
        out_specs=[vmem, vmem, vmem],
        scratch_shapes=[
            pltpu.VMEM((tiles, AVG), jnp.int32),
            pltpu.VMEM((4 * tiles, AVG), F32),
            pltpu.VMEM((9, points), F32),
            pltpu.VMEM((grains + AVG, AVG), F32),
            pltpu.SemaphoreType.DMA((3, chunks)),
        ],
        compiler_params=params,
        cost_estimate=pl.CostEstimate(
            flops=64 * points * ROWS, bytes_accessed=4 * points * ROWS, transcendentals=0
        ),
        name="sums",
    )(*in_hbm)

    held = [table]
    for offset in range(1, groups):
        moves = [(g, int(target(g, offset, groups))) for g in range(groups)]
        held.append(lax.ppermute(table, "grp", moves))

    fluctuation, edge_ids, edge_point, edge_windows = pl.pallas_call(
        fluctuation_kernel,
        out_shape=[
            jax.ShapeDtypeStruct((COUNT, points), BF16),
            jax.ShapeDtypeStruct((2 * EDGE, AVG), jnp.int32),
            jax.ShapeDtypeStruct((ROWS, 2 * EDGE * AVG), F32),
            jax.ShapeDtypeStruct((2, ROWS, AVG), F32),
        ],
        in_specs=[vmem, vmem, vmem],
        out_specs=[hbm, vmem, vmem, vmem],
        scratch_shapes=[
            pltpu.VMEM((COUNT, points), BF16),
            pltpu.SemaphoreType.DMA((tiles // blk,)),
        ],
        compiler_params=params,
        cost_estimate=pl.CostEstimate(
            flops=64 * points * ROWS, bytes_accessed=6 * points * ROWS, transcendentals=0
        ),
        name="fluctuation",
    )(ids, point, windows)

    held, edge_ids = lax.optimization_barrier((held, edge_ids))
    mine = pl.pallas_call(
        stack_kernel,
        out_shape=jax.ShapeDtypeStruct((groups, slots, 8, AVG), BF16),
        in_specs=[vmem] * groups,
        out_specs=vmem,
        compiler_params=params,
        name="stack",
    )(*held)
    other = lax.ppermute(mine, "slab", [(s, s ^ 1) for s in range(slabs)])
    sent = pl.pallas_call(
        route_kernel,
        out_shape=[jax.ShapeDtypeStruct((per_device + CORES, 8, AVG), BF16)] * chips,
        in_specs=[anywhere, vmem, vmem],
        out_specs=[vmem] * chips,
        scratch_shapes=[
            pltpu.VMEM((CORES, groups, slots, 8, AVG), BF16),
            pltpu.SMEM(owner_blocks.shape, jnp.int32),
            pltpu.SemaphoreType.DMA,
        ],
        compiler_params=params,
        name="route",
    )(owner_blocks, mine, other)
    got = [sent[0]]
    for offset in reversed(range(1, chips)):
        moves = [
            (chip * CORES + core, int(target(chip, offset, chips)) * CORES + core)
            for chip in range(chips)
            for core in range(CORES)
        ]
        got.insert(1, lax.ppermute(sent[offset], "slab", moves))
    grain_table, fluctuation = pl.pallas_call(
        functools.partial(place_kernel, groups=groups, chips=chips, blk=blk),
        out_shape=[
            jax.ShapeDtypeStruct((COUNT, grains), F32),
            jax.ShapeDtypeStruct((COUNT, points), BF16),
        ],
        in_specs=[anywhere] + [vmem] * (chips + 3) + [hbm],
        out_specs=[hbm, hbm],
        scratch_shapes=[
            pltpu.VMEM((chips, per_device + CORES, 8, AVG), BF16),
            pltpu.VMEM((slabs, 8, AVG), F32),
            pltpu.VMEM((COUNT, 2 * EDGE * AVG), BF16),
            pltpu.VMEM((COUNT, grains), F32),
            pltpu.SMEM(owner_blocks.shape, jnp.int32),
            pltpu.SemaphoreType.DMA((4,)),
        ],
        input_output_aliases={chips + 4: 1},
        compiler_params=params,
        name="place",
    )(owner_blocks, *reversed(got), edge_ids, edge_point, edge_windows, fluctuation)
    return (grain_table, fluctuation)


def solution(mesh):
    placed = (P(AXES), P(None, AXES), P(None, AXES), P())
    return jax.shard_map(
        local,
        mesh=mesh,
        in_specs=placed,
        out_specs=(P(None, AXES), P(None, AXES)),
        check_vma=False,
    )
```

```python
import functools

import jax
import jax.numpy as jnp
from jax import lax
from jax.experimental import pallas as pl
from jax.experimental.pallas import tpu as pltpu
from jax.sharding import PartitionSpec as P

AVG = 128
AXES = ("grp", "slab")
SUB = 8
WINDOW = 16
ROWS = 16
COUNT = 13
CORES = 2
CUTS = (0, 1, 3, 5, 8)
EDGE = 2
F32 = jnp.float32
BF16 = jnp.bfloat16


def window_sums(selector, values):
    high = values.astype(BF16)
    low = (values - high.astype(F32)).astype(BF16)
    both = jnp.concatenate([high, low], axis=0)
    return lax.dot_general(selector, both, (((1,), (1,)), ((), ())), preferred_element_type=F32)


def finish(total):
    row = lax.broadcasted_iota(jnp.int32, total.shape, 0)
    squares = jnp.sum(jnp.where(row < 4, total * total, 0.0), axis=0, keepdims=True)
    scale = jnp.where(row < 4, jnp.sqrt(squares), total[COUNT : COUNT + 1])
    return total / jnp.where(scale > 0.0, scale, 1.0)


def device_index():
    return lax.axis_index("grp") * lax.axis_size("slab") + lax.axis_index("slab")


def div_rem(x, n):
    if n & (n - 1) == 0:
        return x >> (n.bit_length() - 1), x & (n - 1)
    return lax.div(x, n), lax.rem(x, n)


def selection(ids_ref, first_tile, tiles, first_grain):
    grain_row = lax.broadcasted_iota(jnp.int32, (WINDOW, AVG), 0) + first_grain
    picks = []
    for tile in range(tiles):
        ids = jnp.broadcast_to(ids_ref[pl.ds(first_tile + tile, 1), :], (WINDOW, AVG))
        picks.append((ids == grain_row).astype(F32).astype(BF16))
    return jnp.concatenate(picks, axis=1)


def sum_kernel(
    ids_hbm, q_hbm, s_hbm, table_ref, window_ref, ids_ref, q_ref, s_ref, acc_ref, sems, *, cuts, blk
):
    grains = ids_hbm.shape[0]
    tile_base = device_index() * grains
    chunks = list(zip(cuts[:-1], cuts[1:]))

    def copies(chunk):
        begin, end = chunks[chunk]
        rows, quads = slice(begin, end), slice(4 * begin, 4 * end)
        lanes = slice(begin * AVG, end * AVG)
        return (
            pltpu.make_async_copy(ids_hbm.at[rows], ids_ref.at[rows], sems.at[0, chunk]),
            pltpu.make_async_copy(q_hbm.at[quads], q_ref.at[quads], sems.at[1, chunk]),
            pltpu.make_async_copy(s_hbm.at[:, lanes], s_ref.at[:, lanes], sems.at[2, chunk]),
        )

    for chunk in range(len(chunks)):
        for copy in copies(chunk):
            copy.start()

    ones = jnp.ones((ROWS - COUNT, SUB * AVG), F32)
    carry = jnp.zeros((SUB, 2 * ROWS), F32)
    for chunk, (begin, end) in enumerate(chunks):
        for copy in copies(chunk):
            copy.wait()
        for tile in range(begin, end, SUB):
            values = jnp.concatenate([components(q_ref, s_ref, tile, SUB), ones], axis=0)
            sums = window_sums(selection(ids_ref, tile, SUB, tile_base + tile - 1), values)
            acc_ref[tile : tile + SUB, : 2 * ROWS] = carry + sums[:SUB]
            carry = sums[SUB:]
    acc_ref[grains : grains + SUB, : 2 * ROWS] = carry
    blocks = [acc_ref[block * AVG : (block + 1) * AVG, :].T for block in range(grains // AVG + 1)]
    part = jnp.concatenate([block[:ROWS] + block[ROWS : 2 * ROWS] for block in blocks], axis=1)
    rounded = finish(part).astype(BF16).astype(F32)
    own = rounded[:, 1 : 1 + grains]
    half = lax.broadcasted_iota(jnp.int32, (8, AVG), 1) < blk
    for pair in range(grains // AVG):
        top = own[:8, pair * AVG : (pair + 1) * AVG]
        low = own[8:, pair * AVG : (pair + 1) * AVG]
        table_ref[2 * pair] = jnp.where(half, top, pltpu.roll(low, blk, 1)).astype(BF16)
        table_ref[2 * pair + 1] = jnp.where(half, pltpu.roll(top, blk, 1), low).astype(BF16)
    lane = lax.broadcasted_iota(jnp.int32, (ROWS, AVG), 1)
    ends = jnp.where(lane < 2, part[:, :AVG], pltpu.roll(part[:, grains:], 2, 1))
    high = ends.astype(BF16).astype(F32)
    mid = (ends - high).astype(BF16).astype(F32)
    rest = ends - high - mid
    pieces = jnp.where(lane < 4, high, jnp.where(lane < 8, pltpu.roll(mid, 4, 1), pltpu.roll(rest, 8, 1)))
    pieces = jnp.where(lane < 12, pieces, 0.0)
    table_ref[grains // blk] = jnp.where(half, pieces[:8], pltpu.roll(pieces[8:], blk, 1)).astype(BF16)
    for index in range(window_ref.shape[0]):
        window_ref[index] = rounded[:, index * blk : index * blk + AVG]


def components(q_ref, s_ref, tile, tiles):
    q = [q_ref[4 * t : 4 * t + 4, :] for t in range(tile, tile + tiles)]
    return jnp.concatenate([jnp.concatenate(q, axis=1), s_ref[:, tile * AVG : (tile + tiles) * AVG]], axis=0)


def differences(ids_ref, q_ref, s_ref, table, tile, tiles, first_grain):
    picks = selection(ids_ref, tile, tiles, first_grain)
    means = jnp.dot(table[:, :WINDOW].astype(BF16), picks, preferred_element_type=F32)
    parts = [q_ref[pl.ds(4 * tile + c, tiles, stride=4), :] for c in range(4)]
    scale = lax.rsqrt(sum(part * part for part in parts))
    quaternion = lax.broadcasted_iota(jnp.int32, (8, AVG), 0) < 4
    scales = [jnp.where(quaternion, jnp.broadcast_to(scale[t : t + 1], (8, AVG)), 1.0) for t in range(tiles)]
    values = components(q_ref, s_ref, tile, tiles)
    values = jnp.concatenate([values[:8] * jnp.concatenate(scales, axis=1), values[8:]], axis=0)
    return (values - means[:COUNT]).astype(BF16)


def fluctuation_kernel(ids_ref, q_ref, s_ref, window_ref, *refs, begin, end):
    *_, out_hbm, out_ref, sems = refs
    total = ids_ref.shape[0]
    tile_base = device_index() * total
    tiles = total // window_ref.shape[0]

    def copy(window):
        lanes = slice(window * tiles * AVG, (window + 1) * tiles * AVG)
        local = slice((window - begin) * tiles * AVG, (window - begin + 1) * tiles * AVG)
        return pltpu.make_async_copy(out_ref.at[:, local], out_hbm.at[:, lanes], sems.at[window - begin])

    for window in range(begin, end):
        table = window_ref[window]
        for sub in range(tiles // SUB):
            tile = window * tiles + sub * SUB
            near = pltpu.roll(table, (AVG - sub * SUB) % AVG, 1)
            local = tile - begin * tiles
            out_ref[:, local * AVG : (local + SUB) * AVG] = differences(
                ids_ref, q_ref, s_ref, near, tile, SUB, tile_base + tile - 1
            )
        copy(window).start()
    for window in range(begin, end):
        copy(window).wait()


def stack_kernel(mine_ref, other_ref, out_ref, *, bit):
    upper = (lax.axis_index("grp") // bit) & 1
    out_ref[upper] = mine_ref[...]
    out_ref[1 - upper] = other_ref[...]


def route_kernel(blocks_any, mine_ref, other_ref, *refs):
    *out_refs, held_ref, blocks_ref, sem = refs
    copy = pltpu.make_async_copy(blocks_any, blocks_ref, sem)
    copy.start()
    chips = len(out_refs)
    groups, slots = mine_ref.shape[:2]
    per_device = slots - 1
    slabs = chips * CORES
    group = lax.axis_index("grp")
    chip, core = div_rem(lax.axis_index("slab"), CORES)
    held_ref[core] = mine_ref[...]
    held_ref[1 - core] = other_ref[...]
    step = AVG // 2 // groups
    lane = lax.broadcasted_iota(jnp.int32, (8, AVG), 1) & (AVG // 2 - 1)
    for owner_core in range(CORES):
        ends = held_ref[owner_core, 0, per_device].astype(F32)
        for owner_group in range(1, groups):
            rolled = pltpu.roll(held_ref[owner_core, owner_group, per_device].astype(F32), owner_group * step, 1)
            ends = jnp.where(lane >= owner_group * step, rolled, ends)
        for out_ref in out_refs:
            out_ref[per_device + owner_core] = ends.astype(BF16)
    copy.wait()
    for offset, out_ref in enumerate(out_refs):
        wanted = (group * slabs + (chip ^ offset) * CORES + core) * per_device
        for slot in range(per_device):
            owner, index = div_rem(blocks_ref[wanted + slot], per_device)
            owner_group, owner_slab = div_rem(owner, slabs)
            out_ref[slot] = held_ref[div_rem(owner_slab, CORES)[1], owner_group, index]


def place_kernel(blocks_any, *refs, groups, chips, blk):
    (*got_refs, ids_ref, q_ref, s_ref, window_ref, _, table_hbm, fluctuation_hbm, held_ref, ends_ref,
     edge_ref, table_ref, blocks_ref, sems) = refs
    blocks_copy = pltpu.make_async_copy(blocks_any, blocks_ref, sems.at[3])
    blocks_copy.start()
    slots = got_refs[0].shape[0]
    per_device = slots - CORES
    slabs = chips * CORES
    devices = groups * slabs
    grains = table_ref.shape[1]
    step = AVG // 2 // groups
    device = device_index()
    chip = div_rem(lax.axis_index("slab"), CORES)[0]
    lane = lax.broadcasted_iota(jnp.int32, (8, AVG), 1)
    half = lane < blk

    for offset, ref in enumerate(reversed(got_refs)):
        owner_chip = chip ^ offset
        held_ref[owner_chip] = ref[...]
        for core in range(CORES):
            piece = ref[per_device + core].astype(F32)
            piece = piece + pltpu.roll(piece, AVG - 4, 1) + pltpu.roll(piece, AVG - 8, 1)
            ends_ref[owner_chip * CORES + core] = piece

    def ends(owner, column, lane):
        group, slab = div_rem(jnp.clip(owner, 0, devices - 1), slabs)
        moved = pltpu.roll(ends_ref[slab], (lane - column - step * group + 2 * AVG) & (AVG - 1), 1)
        return jnp.where((owner >= 0) & (owner < devices), moved, 0.0)

    def unfold(value):
        return jnp.concatenate([value, pltpu.roll(value, blk, 1)], axis=0)

    lane_half = lane & (blk - 1)
    others = jnp.where(lane_half < 2, ends(device - 1, 2, 0), ends(device + 1, 0, 2))
    shared = finish(unfold(ends(device, 0, 0) + others))
    wide_lane = lax.broadcasted_iota(jnp.int32, (ROWS, AVG), 1)
    windows = window_ref.shape[0]
    first = jnp.where(wide_lane < 2, shared, window_ref[0])
    in_last = (wide_lane >= SUB) & (wide_lane < SUB + 2)
    last = pltpu.roll(window_ref[windows - 1], AVG - grains // windows + SUB, 1)
    last = jnp.where(in_last, pltpu.roll(shared, SUB - 2, 1), last)
    width = EDGE * AVG
    first_grain = device * grains - 1
    copies = []
    for end, (table, tile, grain) in enumerate(
        ((first, 0, first_grain), (last, grains - EDGE, first_grain + grains - SUB))
    ):
        lanes = slice(end * width, (end + 1) * width)
        edge_ref[:, lanes] = differences(ids_ref, q_ref, s_ref, table, tile, EDGE, grain)
        points = slice(tile * AVG, tile * AVG + width)
        copies.append(pltpu.make_async_copy(edge_ref.at[:, lanes], fluctuation_hbm.at[:, points], sems.at[end]))
        copies[-1].start()

    blocks_copy.wait()
    tiles, columns = [], []
    sums = jnp.zeros((8, AVG), F32)
    for slot in range(per_device):
        owner, index = div_rem(blocks_ref[device * per_device + slot], per_device)
        owner_chip = div_rem(div_rem(owner, slabs)[1], CORES)[0]
        tiles.append(held_ref[owner_chip, slot].astype(F32))
        low = index == 0
        beside = jnp.where(low, owner - 1, owner + 1)
        both = ends(owner, jnp.where(low, 1, 2), slot) + ends(beside, jnp.where(low, 3, 0), slot)
        sums = jnp.where(lane_half == slot, both, sums)
        columns.append(jnp.where(low, 0, jnp.where(index == per_device - 1, blk - 1, 2 * AVG)))
    repaired = finish(unfold(sums))
    repaired = jnp.where(half, repaired[:8], pltpu.roll(repaired[8:], blk, 1))
    for slot in range(per_device):
        moved = pltpu.roll(repaired, (columns[slot] - slot + AVG) & (AVG - 1), 1)
        tiles[slot] = jnp.where(lane_half == columns[slot], moved, tiles[slot])
    for pair in range(per_device // 2):
        first, second = tiles[2 * pair], tiles[2 * pair + 1]
        lanes = slice(pair * AVG, (pair + 1) * AVG)
        table_ref[:8, lanes] = jnp.where(half, first, pltpu.roll(second, blk, 1))
        table_ref[8:, lanes] = jnp.where(half, pltpu.roll(first, blk, 1), second)[: COUNT - 8]
    copies.append(pltpu.make_async_copy(table_ref, table_hbm, sems.at[2]))
    copies[-1].start()
    for copy in copies:
        copy.wait()


def local(grain_ids, orientation, stress, owner_blocks):
    groups, slabs = lax.axis_size("grp"), lax.axis_size("slab")
    points = grain_ids.shape[0]
    tiles = points // AVG
    grains = tiles
    per_device = owner_blocks.shape[0] // (groups * slabs)
    blk = grains // per_device
    slots = per_device + 1
    chips = slabs // CORES

    ids = grain_ids.reshape(tiles, AVG)
    quads = orientation.reshape(4, tiles, AVG).transpose(1, 0, 2).reshape(4 * tiles, AVG)
    in_hbm = [pltpu.with_memory_space_constraint(x, pltpu.HBM) for x in (ids, quads, stress)]
    anywhere = pl.BlockSpec(memory_space=pl.ANY)
    vmem = pl.BlockSpec(memory_space=pltpu.VMEM)
    hbm = pl.BlockSpec(memory_space=pltpu.HBM)
    params = pltpu.CompilerParams(vmem_limit_bytes=20 << 20)

    cuts = [tiles * part // 8 for part in CUTS]
    windows = tiles // blk
    table, means, ids, q, s = pl.pallas_call(
        functools.partial(sum_kernel, cuts=cuts, blk=blk),
        out_shape=[
            jax.ShapeDtypeStruct((slots, 8, AVG), BF16),
            jax.ShapeDtypeStruct((windows, ROWS, AVG), F32),
            jax.ShapeDtypeStruct((tiles, AVG), jnp.int32),
            jax.ShapeDtypeStruct((4 * tiles, AVG), F32),
            jax.ShapeDtypeStruct((9, points), F32),
        ],
        in_specs=[hbm, hbm, hbm],
        out_specs=[vmem] * 5,
        scratch_shapes=[
            pltpu.VMEM((grains + AVG, AVG), F32),
            pltpu.SemaphoreType.DMA((3, len(cuts) - 1)),
        ],
        compiler_params=params,
        cost_estimate=pl.CostEstimate(
            flops=64 * points * ROWS, bytes_accessed=4 * points * ROWS, transcendentals=0
        ),
        name="sums",
    )(*in_hbm)
    on_chip = (ids, q, s, means)

    def look_up(begin, end, earlier):
        share = (end - begin) * points // windows
        return pl.pallas_call(
            functools.partial(fluctuation_kernel, begin=begin, end=end),
            out_shape=jax.ShapeDtypeStruct((COUNT, points), BF16),
            in_specs=[vmem] * 4 + [hbm] * len(earlier),
            out_specs=hbm,
            scratch_shapes=[pltpu.VMEM((COUNT, share), BF16), pltpu.SemaphoreType.DMA((end - begin,))],
            input_output_aliases={4: 0} if earlier else {},
            compiler_params=params,
            cost_estimate=pl.CostEstimate(
                flops=64 * share * ROWS, bytes_accessed=6 * share * ROWS, transcendentals=0
            ),
            name="fluctuation",
        )(*on_chip, *earlier)

    stages = [("grp", 1 << bit) for bit in range((groups - 1).bit_length())] + [("slab", 1)]
    held = table[None]
    fluctuation = []
    for stage, (axis, bit) in enumerate(stages):
        size = lax.axis_size(axis)
        other = lax.ppermute(held, axis, [(member, member ^ bit) for member in range(size)])
        begin, end = (windows * step // len(stages) for step in (stage, stage + 1))
        fluctuation = [look_up(begin, end, fluctuation)]
        other, fluctuation = lax.optimization_barrier((other, fluctuation))
        if axis == "grp":
            held = pl.pallas_call(
                functools.partial(stack_kernel, bit=bit),
                out_shape=jax.ShapeDtypeStruct((2, *held.shape), BF16),
                in_specs=[vmem, vmem],
                out_specs=vmem,
                compiler_params=params,
                name="stack",
            )(held, other).reshape(-1, slots, 8, AVG)
    sent = pl.pallas_call(
        route_kernel,
        out_shape=[jax.ShapeDtypeStruct((per_device + CORES, 8, AVG), BF16)] * chips,
        in_specs=[anywhere, vmem, vmem],
        out_specs=[vmem] * chips,
        scratch_shapes=[
            pltpu.VMEM((CORES, groups, slots, 8, AVG), BF16),
            pltpu.SMEM(owner_blocks.shape, jnp.int32),
            pltpu.SemaphoreType.DMA,
        ],
        compiler_params=params,
        name="route",
    )(owner_blocks, held, other)
    got = [sent[0]]
    for offset in reversed(range(1, chips)):
        moves = [
            (chip * CORES + core, (chip ^ offset) * CORES + core)
            for chip in range(chips)
            for core in range(CORES)
        ]
        got.insert(1, lax.ppermute(sent[offset], "slab", moves))
    grain_table, fluctuation = pl.pallas_call(
        functools.partial(place_kernel, groups=groups, chips=chips, blk=blk),
        out_shape=[
            jax.ShapeDtypeStruct((COUNT, grains), F32),
            jax.ShapeDtypeStruct((COUNT, points), BF16),
        ],
        in_specs=[anywhere] + [vmem] * (chips + 4) + [hbm],
        out_specs=[hbm, hbm],
        scratch_shapes=[
            pltpu.VMEM((chips, per_device + CORES, 8, AVG), BF16),
            pltpu.VMEM((slabs, 8, AVG), F32),
            pltpu.VMEM((COUNT, 2 * EDGE * AVG), BF16),
            pltpu.VMEM((COUNT, grains), F32),
            pltpu.SMEM(owner_blocks.shape, jnp.int32),
            pltpu.SemaphoreType.DMA((4,)),
        ],
        input_output_aliases={chips + 5: 1},
        compiler_params=params,
        name="place",
    )(owner_blocks, *reversed(got), *on_chip, *fluctuation)
    return (grain_table, fluctuation)


def solution(mesh):
    placed = (P(AXES), P(None, AXES), P(None, AXES), P())
    return jax.shard_map(
        local,
        mesh=mesh,
        in_specs=placed,
        out_specs=(P(None, AXES), P(None, AXES)),
        check_vma=False,
    )
```

```python
import functools

import jax
import jax.numpy as jnp
from jax import lax
from jax.experimental import pallas as pl
from jax.experimental.pallas import tpu as pltpu
from jax.sharding import PartitionSpec as P

AVG = 128
AXES = ("grp", "slab")
SUB = 8
WINDOW = 16
ROWS = 16
COUNT = 13
CORES = 2
CUTS = (0, 1, 2, 3, 4)
EDGE = 2
F32 = jnp.float32
BF16 = jnp.bfloat16


def window_sums(selector, values):
    high = values.astype(BF16)
    low = (values - high.astype(F32)).astype(BF16)
    both = jnp.concatenate([high, low], axis=0)
    return lax.dot_general(selector, both, (((1,), (1,)), ((), ())), preferred_element_type=F32)


def finish(total):
    row = lax.broadcasted_iota(jnp.int32, total.shape, 0)
    squares = jnp.sum(jnp.where(row < 4, total * total, 0.0), axis=0, keepdims=True)
    scale = jnp.where(row < 4, jnp.sqrt(squares), total[COUNT : COUNT + 1])
    return total / jnp.where(scale > 0.0, scale, 1.0)


def device_index():
    return lax.axis_index("grp") * lax.axis_size("slab") + lax.axis_index("slab")


def div_rem(x, n):
    if n & (n - 1) == 0:
        return x >> (n.bit_length() - 1), x & (n - 1)
    return lax.div(x, n), lax.rem(x, n)


def selection(ids_ref, first_tile, tiles, first_grain):
    grain_row = lax.broadcasted_iota(jnp.int32, (WINDOW, AVG), 0) + first_grain
    picks = []
    for tile in range(tiles):
        ids = jnp.broadcast_to(ids_ref[pl.ds(first_tile + tile, 1), :], (WINDOW, AVG))
        picks.append((ids == grain_row).astype(F32).astype(BF16))
    return jnp.concatenate(picks, axis=1)


def sum_kernel(
    ids_hbm, q_hbm, s_hbm, table_ref, window_ref, point_ref, ids_ref, q_ref, s_ref, acc_ref, sems, *, cuts, blk
):
    grains = ids_hbm.shape[0]
    tile_base = device_index() * grains
    chunks = list(zip(cuts[:-1], cuts[1:]))

    def copies(chunk):
        begin, end = chunks[chunk]
        rows, quads = slice(begin, end), slice(4 * begin, 4 * end)
        lanes = slice(begin * AVG, end * AVG)
        return (
            pltpu.make_async_copy(ids_hbm.at[rows], ids_ref.at[rows], sems.at[0, chunk]),
            pltpu.make_async_copy(q_hbm.at[quads], q_ref.at[quads], sems.at[1, chunk]),
            pltpu.make_async_copy(s_hbm.at[:, lanes], s_ref.at[:, lanes], sems.at[2, chunk]),
        )

    for chunk in range(len(chunks)):
        for copy in copies(chunk):
            copy.start()

    quaternion = lax.broadcasted_iota(jnp.int32, (8, AVG), 0) < 4
    ones = jnp.ones((ROWS - COUNT, SUB * AVG), F32)

    carry = jnp.zeros((SUB, 2 * ROWS), F32)
    for chunk, (begin, end) in enumerate(chunks):
        for copy in copies(chunk):
            copy.wait()
        for tile in range(begin, end, SUB):
            lanes = slice(tile * AVG, (tile + SUB) * AVG)
            q = jnp.concatenate([q_ref[4 * t : 4 * t + 4, :] for t in range(tile, tile + SUB)], axis=1)
            values = jnp.concatenate([q, s_ref[:, lanes], ones], axis=0)
            sums = window_sums(selection(ids_ref, tile, SUB, tile_base + tile - 1), values)
            acc_ref[tile : tile + SUB, : 2 * ROWS] = carry + sums[:SUB]
            carry = sums[SUB:]
            parts = [q_ref[pl.ds(4 * tile + c, SUB, stride=4), :] for c in range(4)]
            scale = lax.rsqrt(sum(part * part for part in parts))
            scales = [
                jnp.where(quaternion, jnp.broadcast_to(scale[t : t + 1], (8, AVG)), 1.0) for t in range(SUB)
            ]
            point_ref[:8, lanes] = values[:8] * jnp.concatenate(scales, axis=1)
            point_ref[8:, lanes] = values[8:]
    acc_ref[grains : grains + SUB, : 2 * ROWS] = carry
    blocks = [acc_ref[block * AVG : (block + 1) * AVG, :].T for block in range(grains // AVG + 1)]
    part = jnp.concatenate([block[:ROWS] + block[ROWS : 2 * ROWS] for block in blocks], axis=1)
    rounded = finish(part).astype(BF16).astype(F32)
    for index in range(window_ref.shape[0]):
        window_ref[index] = rounded[:, index * blk : index * blk + AVG]
    own = rounded[:, 1 : 1 + grains]
    half = lax.broadcasted_iota(jnp.int32, (8, AVG), 1) < blk
    for pair in range(grains // AVG):
        top = own[:8, pair * AVG : (pair + 1) * AVG]
        low = own[8:, pair * AVG : (pair + 1) * AVG]
        table_ref[2 * pair] = jnp.where(half, top, pltpu.roll(low, blk, 1)).astype(BF16)
        table_ref[2 * pair + 1] = jnp.where(half, pltpu.roll(top, blk, 1), low).astype(BF16)
    lane = lax.broadcasted_iota(jnp.int32, (ROWS, AVG), 1)
    ends = jnp.where(lane < 2, part[:, :AVG], pltpu.roll(part[:, grains:], 2, 1))
    high = ends.astype(BF16).astype(F32)
    mid = (ends - high).astype(BF16).astype(F32)
    rest = ends - high - mid
    pieces = jnp.where(lane < 4, high, jnp.where(lane < 8, pltpu.roll(mid, 4, 1), pltpu.roll(rest, 8, 1)))
    pieces = jnp.where(lane < 12, pieces, 0.0)
    table_ref[grains // blk] = jnp.where(half, pieces[:8], pltpu.roll(pieces[8:], blk, 1)).astype(BF16)


def fluctuation_kernel(
    ids_ref, point_ref, window_ref, out_hbm, edge_ids_ref, edge_point_ref, edge_window_ref, out_ref, sems
):
    windows = window_ref.shape[0]
    total = ids_ref.shape[0]
    tile_base = device_index() * total
    tiles = total // windows
    points = tiles * AVG

    def copy(window):
        lanes = pl.ds(window * points, points)
        return pltpu.make_async_copy(out_ref.at[:, lanes], out_hbm.at[:, lanes], sems.at[window])

    def step(window):
        table = window_ref[window]
        for sub in range(tiles // SUB):
            tile = window * tiles + sub * SUB
            lanes = pl.ds(tile * AVG, SUB * AVG)
            near = pltpu.roll(table, (AVG - sub * SUB) % AVG, 1)[:, :WINDOW].astype(BF16)
            picks = selection(ids_ref, tile, SUB, tile_base + tile - 1)
            means = jnp.dot(near, picks, preferred_element_type=F32)
            out_ref[:, lanes] = (point_ref[:, lanes] - means)[:COUNT].astype(BF16)
        copy(window).start()

    for window in range(windows):
        step(window)
    first, last = slice(0, EDGE), slice(total - EDGE, total)
    edge_ids_ref[:EDGE] = ids_ref[first]
    edge_ids_ref[EDGE:] = ids_ref[last]
    edge_point_ref[:, : EDGE * AVG] = point_ref[:, : EDGE * AVG]
    edge_point_ref[:, EDGE * AVG :] = point_ref[:, (total - EDGE) * AVG :]
    edge_window_ref[0] = window_ref[0]
    edge_window_ref[1] = pltpu.roll(window_ref[windows - 1], AVG - tiles + SUB, 1)
    for window in range(windows):
        copy(window).wait()


def source(me, offset, count):
    if count & (count - 1) == 0:
        return me ^ offset
    return (me + count - offset) % count


def target(me, offset, count):
    if count & (count - 1) == 0:
        return me ^ offset
    return (me + offset) % count


def stack_kernel(*refs):
    *held_refs, out_ref = refs
    for offset, ref in enumerate(held_refs):
        out_ref[source(lax.axis_index("grp"), offset, len(held_refs))] = ref[...]


def route_kernel(blocks_any, mine_ref, other_ref, *refs):
    *out_refs, held_ref, blocks_ref, sem = refs
    copy = pltpu.make_async_copy(blocks_any, blocks_ref, sem)
    copy.start()
    chips = len(out_refs)
    groups, slots = mine_ref.shape[:2]
    per_device = slots - 1
    slabs = chips * CORES
    group = lax.axis_index("grp")
    chip, core = div_rem(lax.axis_index("slab"), CORES)
    held_ref[core] = mine_ref[...]
    held_ref[1 - core] = other_ref[...]
    step = AVG // 2 // groups
    lane = lax.broadcasted_iota(jnp.int32, (8, AVG), 1) & (AVG // 2 - 1)
    for owner_core in range(CORES):
        ends = held_ref[owner_core, 0, per_device].astype(F32)
        for owner_group in range(1, groups):
            rolled = pltpu.roll(held_ref[owner_core, owner_group, per_device].astype(F32), owner_group * step, 1)
            ends = jnp.where(lane >= owner_group * step, rolled, ends)
        for out_ref in out_refs:
            out_ref[per_device + owner_core] = ends.astype(BF16)
    copy.wait()
    for offset, out_ref in enumerate(out_refs):
        wanted = (group * slabs + target(chip, offset, chips) * CORES + core) * per_device
        for slot in range(per_device):
            owner, index = div_rem(blocks_ref[wanted + slot], per_device)
            owner_group, owner_slab = div_rem(owner, slabs)
            out_ref[slot] = held_ref[div_rem(owner_slab, CORES)[1], owner_group, index]


def place_kernel(blocks_any, *refs, groups, chips, blk):
    (*got_refs, edge_ids_ref, edge_point_ref, edge_window_ref, _, table_hbm, fluctuation_hbm, held_ref, ends_ref,
     edge_ref, table_ref, blocks_ref, sems) = refs
    blocks_copy = pltpu.make_async_copy(blocks_any, blocks_ref, sems.at[3])
    blocks_copy.start()
    slots = got_refs[0].shape[0]
    per_device = slots - CORES
    slabs = chips * CORES
    devices = groups * slabs
    grains = table_ref.shape[1]
    step = AVG // 2 // groups
    device = device_index()
    chip = div_rem(lax.axis_index("slab"), CORES)[0]
    lane = lax.broadcasted_iota(jnp.int32, (8, AVG), 1)
    half = lane < blk

    for offset, ref in enumerate(reversed(got_refs)):
        owner_chip = source(chip, offset, chips)
        held_ref[owner_chip] = ref[...]
        for core in range(CORES):
            piece = ref[per_device + core].astype(F32)
            piece = piece + pltpu.roll(piece, AVG - 4, 1) + pltpu.roll(piece, AVG - 8, 1)
            ends_ref[owner_chip * CORES + core] = piece

    def ends(owner, column, lane):
        group, slab = div_rem(jnp.clip(owner, 0, devices - 1), slabs)
        moved = pltpu.roll(ends_ref[slab], (lane - column - step * group + 2 * AVG) & (AVG - 1), 1)
        return jnp.where((owner >= 0) & (owner < devices), moved, 0.0)

    def unfold(value):
        return jnp.concatenate([value, pltpu.roll(value, blk, 1)], axis=0)

    lane_half = lane & (blk - 1)
    others = jnp.where(lane_half < 2, ends(device - 1, 2, 0), ends(device + 1, 0, 2))
    shared = finish(unfold(ends(device, 0, 0) + others))
    wide_lane = lax.broadcasted_iota(jnp.int32, (ROWS, AVG), 1)
    first = jnp.where(wide_lane < 2, shared, edge_window_ref[0])
    in_last = (wide_lane >= SUB) & (wide_lane < SUB + 2)
    last = jnp.where(in_last, pltpu.roll(shared, SUB - 2, 1), edge_window_ref[1])
    width = EDGE * AVG
    total = fluctuation_hbm.shape[1]
    first_grain = device * grains - 1
    copies = []
    for end, (table, grain, begin) in enumerate(
        ((first, first_grain, 0), (last, first_grain + grains - SUB, total - width))
    ):
        lanes = slice(end * width, (end + 1) * width)
        picks = selection(edge_ids_ref, end * EDGE, EDGE, grain)
        means = jnp.dot(table[:, :WINDOW].astype(BF16), picks, preferred_element_type=F32)
        edge_ref[:, lanes] = (edge_point_ref[:, lanes] - means)[:COUNT].astype(BF16)
        copies.append(
            pltpu.make_async_copy(
                edge_ref.at[:, lanes], fluctuation_hbm.at[:, begin : begin + width], sems.at[end]
            )
        )
        copies[-1].start()

    blocks_copy.wait()
    tiles, columns = [], []
    sums = jnp.zeros((8, AVG), F32)
    for slot in range(per_device):
        owner, index = div_rem(blocks_ref[device * per_device + slot], per_device)
        owner_chip = div_rem(div_rem(owner, slabs)[1], CORES)[0]
        tiles.append(held_ref[owner_chip, slot].astype(F32))
        low = index == 0
        beside = jnp.where(low, owner - 1, owner + 1)
        both = ends(owner, jnp.where(low, 1, 2), slot) + ends(beside, jnp.where(low, 3, 0), slot)
        sums = jnp.where(lane_half == slot, both, sums)
        columns.append(jnp.where(low, 0, jnp.where(index == per_device - 1, blk - 1, 2 * AVG)))
    repaired = finish(unfold(sums))
    repaired = jnp.where(half, repaired[:8], pltpu.roll(repaired[8:], blk, 1))
    for slot in range(per_device):
        moved = pltpu.roll(repaired, (columns[slot] - slot + AVG) & (AVG - 1), 1)
        tiles[slot] = jnp.where(lane_half == columns[slot], moved, tiles[slot])
    for pair in range(per_device // 2):
        first, second = tiles[2 * pair], tiles[2 * pair + 1]
        lanes = slice(pair * AVG, (pair + 1) * AVG)
        table_ref[:8, lanes] = jnp.where(half, first, pltpu.roll(second, blk, 1))
        table_ref[8:, lanes] = jnp.where(half, pltpu.roll(first, blk, 1), second)[: COUNT - 8]
    copies.append(pltpu.make_async_copy(table_ref, table_hbm, sems.at[2]))
    copies[-1].start()
    for copy in copies:
        copy.wait()


def local(grain_ids, orientation, stress, owner_blocks):
    groups, slabs = lax.axis_size("grp"), lax.axis_size("slab")
    points = grain_ids.shape[0]
    tiles = points // AVG
    grains = tiles
    per_device = owner_blocks.shape[0] // (groups * slabs)
    blk = grains // per_device
    slots = per_device + 1
    chips = slabs // CORES

    ids = grain_ids.reshape(tiles, AVG)
    quads = orientation.reshape(4, tiles, AVG).transpose(1, 0, 2).reshape(4 * tiles, AVG)
    in_hbm = [pltpu.with_memory_space_constraint(x, pltpu.HBM) for x in (ids, quads, stress)]
    anywhere = pl.BlockSpec(memory_space=pl.ANY)
    vmem = pl.BlockSpec(memory_space=pltpu.VMEM)
    hbm = pl.BlockSpec(memory_space=pltpu.HBM)
    params = pltpu.CompilerParams(vmem_limit_bytes=20 << 20)

    cuts = [tiles * part // CUTS[-1] for part in CUTS]
    table, windows, point = pl.pallas_call(
        functools.partial(sum_kernel, cuts=cuts, blk=blk),
        out_shape=[
            jax.ShapeDtypeStruct((slots, 8, AVG), BF16),
            jax.ShapeDtypeStruct((tiles // blk, ROWS, AVG), F32),
            jax.ShapeDtypeStruct((ROWS, points), F32),
        ],
        in_specs=[hbm, hbm, hbm],
        out_specs=[vmem, vmem, vmem],
        scratch_shapes=[
            pltpu.VMEM((tiles, AVG), jnp.int32),
            pltpu.VMEM((4 * tiles, AVG), F32),
            pltpu.VMEM((9, points), F32),
            pltpu.VMEM((grains + AVG, AVG), F32),
            pltpu.SemaphoreType.DMA((3, len(cuts) - 1)),
        ],
        compiler_params=params,
        cost_estimate=pl.CostEstimate(
            flops=64 * points * ROWS, bytes_accessed=4 * points * ROWS, transcendentals=0
        ),
        name="sums",
    )(*in_hbm)

    held = [table]
    for offset in range(1, groups):
        moves = [(g, int(target(g, offset, groups))) for g in range(groups)]
        held.append(lax.ppermute(table, "grp", moves))

    fluctuation, edge_ids, edge_point, edge_windows = pl.pallas_call(
        fluctuation_kernel,
        out_shape=[
            jax.ShapeDtypeStruct((COUNT, points), BF16),
            jax.ShapeDtypeStruct((2 * EDGE, AVG), jnp.int32),
            jax.ShapeDtypeStruct((ROWS, 2 * EDGE * AVG), F32),
            jax.ShapeDtypeStruct((2, ROWS, AVG), F32),
        ],
        in_specs=[vmem, vmem, vmem],
        out_specs=[hbm, vmem, vmem, vmem],
        scratch_shapes=[
            pltpu.VMEM((COUNT, points), BF16),
            pltpu.SemaphoreType.DMA((tiles // blk,)),
        ],
        compiler_params=params,
        cost_estimate=pl.CostEstimate(
            flops=64 * points * ROWS, bytes_accessed=6 * points * ROWS, transcendentals=0
        ),
        name="fluctuation",
    )(ids, point, windows)

    held, edge_ids = lax.optimization_barrier((held, edge_ids))
    mine = pl.pallas_call(
        stack_kernel,
        out_shape=jax.ShapeDtypeStruct((groups, slots, 8, AVG), BF16),
        in_specs=[vmem] * groups,
        out_specs=vmem,
        compiler_params=params,
        name="stack",
    )(*held)
    other = lax.ppermute(mine, "slab", [(s, s ^ 1) for s in range(slabs)])
    sent = pl.pallas_call(
        route_kernel,
        out_shape=[jax.ShapeDtypeStruct((per_device + CORES, 8, AVG), BF16)] * chips,
        in_specs=[anywhere, vmem, vmem],
        out_specs=[vmem] * chips,
        scratch_shapes=[
            pltpu.VMEM((CORES, groups, slots, 8, AVG), BF16),
            pltpu.SMEM(owner_blocks.shape, jnp.int32),
            pltpu.SemaphoreType.DMA,
        ],
        compiler_params=params,
        name="route",
    )(owner_blocks, mine, other)
    got = [sent[0]]
    for offset in reversed(range(1, chips)):
        moves = [
            (chip * CORES + core, int(target(chip, offset, chips)) * CORES + core)
            for chip in range(chips)
            for core in range(CORES)
        ]
        got.insert(1, lax.ppermute(sent[offset], "slab", moves))
    grain_table, fluctuation = pl.pallas_call(
        functools.partial(place_kernel, groups=groups, chips=chips, blk=blk),
        out_shape=[
            jax.ShapeDtypeStruct((COUNT, grains), F32),
            jax.ShapeDtypeStruct((COUNT, points), BF16),
        ],
        in_specs=[anywhere] + [vmem] * (chips + 3) + [hbm],
        out_specs=[hbm, hbm],
        scratch_shapes=[
            pltpu.VMEM((chips, per_device + CORES, 8, AVG), BF16),
            pltpu.VMEM((slabs, 8, AVG), F32),
            pltpu.VMEM((COUNT, 2 * EDGE * AVG), BF16),
            pltpu.VMEM((COUNT, grains), F32),
            pltpu.SMEM(owner_blocks.shape, jnp.int32),
            pltpu.SemaphoreType.DMA((4,)),
        ],
        input_output_aliases={chips + 4: 1},
        compiler_params=params,
        name="place",
    )(owner_blocks, *reversed(got), edge_ids, edge_point, edge_windows, fluctuation)
    return (grain_table, fluctuation)


def solution(mesh):
    placed = (P(AXES), P(None, AXES), P(None, AXES), P())
    return jax.shard_map(
        local,
        mesh=mesh,
        in_specs=placed,
        out_specs=(P(None, AXES), P(None, AXES)),
        check_vma=False,
    )
```

```python
import functools

import jax
import jax.numpy as jnp
from jax import lax
from jax.experimental import pallas as pl
from jax.experimental.pallas import tpu as pltpu
from jax.sharding import PartitionSpec as P

AVG = 128
AXES = ("grp", "slab")
SUB = 8
WINDOW = 16
ROWS = 16
COUNT = 13
CORES = 2
CUTS = (0, 1, 2, 3, 4)
EDGE = 2
F32 = jnp.float32
BF16 = jnp.bfloat16


def window_sums(selector, values):
    high = values.astype(BF16)
    low = (values - high.astype(F32)).astype(BF16)
    both = jnp.concatenate([high, low], axis=0)
    return lax.dot_general(selector, both, (((1,), (1,)), ((), ())), preferred_element_type=F32)


def finish(total):
    row = lax.broadcasted_iota(jnp.int32, total.shape, 0)
    squares = jnp.sum(jnp.where(row < 4, total * total, 0.0), axis=0, keepdims=True)
    scale = jnp.where(row < 4, jnp.sqrt(squares), total[COUNT : COUNT + 1])
    return total / jnp.where(scale > 0.0, scale, 1.0)


def device_index():
    return lax.axis_index("grp") * lax.axis_size("slab") + lax.axis_index("slab")


def div_rem(x, n):
    if n & (n - 1) == 0:
        return x >> (n.bit_length() - 1), x & (n - 1)
    return lax.div(x, n), lax.rem(x, n)


def selection(ids_ref, first_tile, tiles, first_grain):
    grain_row = lax.broadcasted_iota(jnp.int32, (WINDOW, AVG), 0) + first_grain
    picks = []
    for tile in range(tiles):
        ids = jnp.broadcast_to(ids_ref[pl.ds(first_tile + tile, 1), :], (WINDOW, AVG))
        picks.append((ids == grain_row).astype(F32).astype(BF16))
    return jnp.concatenate(picks, axis=1)


def sum_kernel(
    ids_hbm, q_hbm, s_hbm, blocks_any, table_ref, window_ref, point_ref, blocks_ref, ids_ref, q_ref, s_ref, acc_ref,
    sems, blocks_sem, *, cuts, blk,
):
    grains = ids_hbm.shape[0]
    tile_base = device_index() * grains
    chunks = list(zip(cuts[:-1], cuts[1:]))

    def copies(chunk):
        begin, end = chunks[chunk]
        rows, quads = slice(begin, end), slice(4 * begin, 4 * end)
        lanes = slice(begin * AVG, end * AVG)
        return (
            pltpu.make_async_copy(ids_hbm.at[rows], ids_ref.at[rows], sems.at[0, chunk]),
            pltpu.make_async_copy(q_hbm.at[quads], q_ref.at[quads], sems.at[1, chunk]),
            pltpu.make_async_copy(s_hbm.at[:, lanes], s_ref.at[:, lanes], sems.at[2, chunk]),
        )

    for chunk in range(len(chunks)):
        for copy in copies(chunk):
            copy.start()
    blocks_copy = pltpu.make_async_copy(blocks_any, blocks_ref, blocks_sem)
    blocks_copy.start()

    quaternion = lax.broadcasted_iota(jnp.int32, (8, AVG), 0) < 4
    ones = jnp.ones((ROWS - COUNT, SUB * AVG), F32)

    carry = jnp.zeros((SUB, 2 * ROWS), F32)
    for chunk, (begin, end) in enumerate(chunks):
        for copy in copies(chunk):
            copy.wait()
        for tile in range(begin, end, SUB):
            lanes = slice(tile * AVG, (tile + SUB) * AVG)
            q = jnp.concatenate([q_ref[4 * t : 4 * t + 4, :] for t in range(tile, tile + SUB)], axis=1)
            values = jnp.concatenate([q, s_ref[:, lanes], ones], axis=0)
            sums = window_sums(selection(ids_ref, tile, SUB, tile_base + tile - 1), values)
            acc_ref[tile : tile + SUB, : 2 * ROWS] = carry + sums[:SUB]
            carry = sums[SUB:]
            parts = [q_ref[pl.ds(4 * tile + c, SUB, stride=4), :] for c in range(4)]
            scale = lax.rsqrt(sum(part * part for part in parts))
            scales = [
                jnp.where(quaternion, jnp.broadcast_to(scale[t : t + 1], (8, AVG)), 1.0) for t in range(SUB)
            ]
            point_ref[:8, lanes] = values[:8] * jnp.concatenate(scales, axis=1)
            point_ref[8:, lanes] = values[8:]
    blocks_copy.wait()
    acc_ref[grains : grains + SUB, : 2 * ROWS] = carry
    blocks = [acc_ref[block * AVG : (block + 1) * AVG, :].T for block in range(grains // AVG + 1)]
    part = jnp.concatenate([block[:ROWS] + block[ROWS : 2 * ROWS] for block in blocks], axis=1)
    rounded = finish(part).astype(BF16).astype(F32)
    for index in range(window_ref.shape[0]):
        window_ref[index] = rounded[:, index * blk : index * blk + AVG]
    own = rounded[:, 1 : 1 + grains]
    half = lax.broadcasted_iota(jnp.int32, (8, AVG), 1) < blk
    for pair in range(grains // AVG):
        top = own[:8, pair * AVG : (pair + 1) * AVG]
        low = own[8:, pair * AVG : (pair + 1) * AVG]
        table_ref[2 * pair] = jnp.where(half, top, pltpu.roll(low, blk, 1)).astype(BF16)
        table_ref[2 * pair + 1] = jnp.where(half, pltpu.roll(top, blk, 1), low).astype(BF16)
    lane = lax.broadcasted_iota(jnp.int32, (ROWS, AVG), 1)
    ends = jnp.where(lane < 2, part[:, :AVG], pltpu.roll(part[:, grains:], 2, 1))
    high = ends.astype(BF16).astype(F32)
    mid = (ends - high).astype(BF16).astype(F32)
    rest = ends - high - mid
    pieces = jnp.where(lane < 4, high, jnp.where(lane < 8, pltpu.roll(mid, 4, 1), pltpu.roll(rest, 8, 1)))
    pieces = jnp.where(lane < 12, pieces, 0.0)
    table_ref[grains // blk] = jnp.where(half, pieces[:8], pltpu.roll(pieces[8:], blk, 1)).astype(BF16)


def fluctuation_kernel(
    ids_ref, point_ref, window_ref, out_hbm, edge_ids_ref, edge_point_ref, edge_window_ref, out_ref, sems
):
    windows = window_ref.shape[0]
    total = ids_ref.shape[0]
    tile_base = device_index() * total
    tiles = total // windows
    points = tiles * AVG

    def copy(window):
        lanes = pl.ds(window * points, points)
        return pltpu.make_async_copy(out_ref.at[:, lanes], out_hbm.at[:, lanes], sems.at[window])

    def step(window):
        table = window_ref[window]
        for sub in range(tiles // SUB):
            tile = window * tiles + sub * SUB
            lanes = pl.ds(tile * AVG, SUB * AVG)
            near = pltpu.roll(table, (AVG - sub * SUB) % AVG, 1)[:, :WINDOW].astype(BF16)
            picks = selection(ids_ref, tile, SUB, tile_base + tile - 1)
            means = jnp.dot(near, picks, preferred_element_type=F32)
            out_ref[:, lanes] = (point_ref[:, lanes] - means)[:COUNT].astype(BF16)
        copy(window).start()

    for window in range(windows):
        step(window)
    first, last = slice(0, EDGE), slice(total - EDGE, total)
    edge_ids_ref[:EDGE] = ids_ref[first]
    edge_ids_ref[EDGE:] = ids_ref[last]
    edge_point_ref[:, : EDGE * AVG] = point_ref[:, : EDGE * AVG]
    edge_point_ref[:, EDGE * AVG :] = point_ref[:, (total - EDGE) * AVG :]
    edge_window_ref[0] = window_ref[0]
    edge_window_ref[1] = pltpu.roll(window_ref[windows - 1], AVG - tiles + SUB, 1)
    for window in range(windows):
        copy(window).wait()


def source(me, offset, count):
    if count & (count - 1) == 0:
        return me ^ offset
    return (me + count - offset) % count


def target(me, offset, count):
    if count & (count - 1) == 0:
        return me ^ offset
    return (me + offset) % count


def stack_kernel(*refs):
    *held_refs, out_ref = refs
    for offset, ref in enumerate(held_refs):
        out_ref[source(lax.axis_index("grp"), offset, len(held_refs))] = ref[...]


def route_kernel(blocks_ref, mine_ref, other_ref, *refs):
    *out_refs, held_ref = refs
    chips = len(out_refs)
    groups, slots = mine_ref.shape[:2]
    per_device = slots - 1
    slabs = chips * CORES
    group = lax.axis_index("grp")
    chip, core = div_rem(lax.axis_index("slab"), CORES)
    held_ref[core] = mine_ref[...]
    held_ref[1 - core] = other_ref[...]
    step = AVG // 2 // groups
    lane = lax.broadcasted_iota(jnp.int32, (8, AVG), 1) & (AVG // 2 - 1)
    for owner_core in range(CORES):
        ends = held_ref[owner_core, 0, per_device].astype(F32)
        for owner_group in range(1, groups):
            rolled = pltpu.roll(held_ref[owner_core, owner_group, per_device].astype(F32), owner_group * step, 1)
            ends = jnp.where(lane >= owner_group * step, rolled, ends)
        for out_ref in out_refs:
            out_ref[per_device + owner_core] = ends.astype(BF16)
    for offset, out_ref in enumerate(out_refs):
        wanted = (group * slabs + target(chip, offset, chips) * CORES + core) * per_device
        for slot in range(per_device):
            owner, index = div_rem(blocks_ref[wanted + slot], per_device)
            owner_group, owner_slab = div_rem(owner, slabs)
            out_ref[slot] = held_ref[div_rem(owner_slab, CORES)[1], owner_group, index]


def place_kernel(blocks_ref, *refs, groups, chips, blk):
    (*got_refs, edge_ids_ref, edge_point_ref, edge_window_ref, _, table_hbm, fluctuation_hbm, held_ref, ends_ref,
     edge_ref, table_ref, sems) = refs
    slots = got_refs[0].shape[0]
    per_device = slots - CORES
    slabs = chips * CORES
    devices = groups * slabs
    grains = table_ref.shape[1]
    step = AVG // 2 // groups
    device = device_index()
    chip = div_rem(lax.axis_index("slab"), CORES)[0]
    lane = lax.broadcasted_iota(jnp.int32, (8, AVG), 1)
    half = lane < blk

    for offset, ref in enumerate(reversed(got_refs)):
        owner_chip = source(chip, offset, chips)
        held_ref[owner_chip] = ref[...]
        for core in range(CORES):
            piece = ref[per_device + core].astype(F32)
            piece = piece + pltpu.roll(piece, AVG - 4, 1) + pltpu.roll(piece, AVG - 8, 1)
            ends_ref[owner_chip * CORES + core] = piece

    def ends(owner, column, lane):
        group, slab = div_rem(jnp.clip(owner, 0, devices - 1), slabs)
        moved = pltpu.roll(ends_ref[slab], (lane - column - step * group + 2 * AVG) & (AVG - 1), 1)
        return jnp.where((owner >= 0) & (owner < devices), moved, 0.0)

    def unfold(value):
        return jnp.concatenate([value, pltpu.roll(value, blk, 1)], axis=0)

    lane_half = lane & (blk - 1)
    others = jnp.where(lane_half < 2, ends(device - 1, 2, 0), ends(device + 1, 0, 2))
    shared = finish(unfold(ends(device, 0, 0) + others))
    wide_lane = lax.broadcasted_iota(jnp.int32, (ROWS, AVG), 1)
    first = jnp.where(wide_lane < 2, shared, edge_window_ref[0])
    in_last = (wide_lane >= SUB) & (wide_lane < SUB + 2)
    last = jnp.where(in_last, pltpu.roll(shared, SUB - 2, 1), edge_window_ref[1])
    width = EDGE * AVG
    total = fluctuation_hbm.shape[1]
    first_grain = device * grains - 1
    copies = []
    for end, (table, grain, begin) in enumerate(
        ((first, first_grain, 0), (last, first_grain + grains - SUB, total - width))
    ):
        lanes = slice(end * width, (end + 1) * width)
        picks = selection(edge_ids_ref, end * EDGE, EDGE, grain)
        means = jnp.dot(table[:, :WINDOW].astype(BF16), picks, preferred_element_type=F32)
        edge_ref[:, lanes] = (edge_point_ref[:, lanes] - means)[:COUNT].astype(BF16)
        copies.append(
            pltpu.make_async_copy(
                edge_ref.at[:, lanes], fluctuation_hbm.at[:, begin : begin + width], sems.at[end]
            )
        )
        copies[-1].start()

    tiles, columns = [], []
    sums = jnp.zeros((8, AVG), F32)
    for slot in range(per_device):
        owner, index = div_rem(blocks_ref[device * per_device + slot], per_device)
        owner_chip = div_rem(div_rem(owner, slabs)[1], CORES)[0]
        tiles.append(held_ref[owner_chip, slot].astype(F32))
        low = index == 0
        beside = jnp.where(low, owner - 1, owner + 1)
        both = ends(owner, jnp.where(low, 1, 2), slot) + ends(beside, jnp.where(low, 3, 0), slot)
        sums = jnp.where(lane_half == slot, both, sums)
        columns.append(jnp.where(low, 0, jnp.where(index == per_device - 1, blk - 1, 2 * AVG)))
    repaired = finish(unfold(sums))
    repaired = jnp.where(half, repaired[:8], pltpu.roll(repaired[8:], blk, 1))
    for slot in range(per_device):
        moved = pltpu.roll(repaired, (columns[slot] - slot + AVG) & (AVG - 1), 1)
        tiles[slot] = jnp.where(lane_half == columns[slot], moved, tiles[slot])
    for pair in range(per_device // 2):
        first, second = tiles[2 * pair], tiles[2 * pair + 1]
        lanes = slice(pair * AVG, (pair + 1) * AVG)
        table_ref[:8, lanes] = jnp.where(half, first, pltpu.roll(second, blk, 1))
        table_ref[8:, lanes] = jnp.where(half, pltpu.roll(first, blk, 1), second)[: COUNT - 8]
    copies.append(pltpu.make_async_copy(table_ref, table_hbm, sems.at[2]))
    copies[-1].start()
    for copy in copies:
        copy.wait()


def local(grain_ids, orientation, stress, owner_blocks):
    groups, slabs = lax.axis_size("grp"), lax.axis_size("slab")
    points = grain_ids.shape[0]
    tiles = points // AVG
    grains = tiles
    per_device = owner_blocks.shape[0] // (groups * slabs)
    blk = grains // per_device
    slots = per_device + 1
    chips = slabs // CORES

    ids = grain_ids.reshape(tiles, AVG)
    quads = orientation.reshape(4, tiles, AVG).transpose(1, 0, 2).reshape(4 * tiles, AVG)
    in_hbm = [pltpu.with_memory_space_constraint(x, pltpu.HBM) for x in (ids, quads, stress)]
    anywhere = pl.BlockSpec(memory_space=pl.ANY)
    smem = pl.BlockSpec(memory_space=pltpu.SMEM)
    vmem = pl.BlockSpec(memory_space=pltpu.VMEM)
    hbm = pl.BlockSpec(memory_space=pltpu.HBM)
    params = pltpu.CompilerParams(vmem_limit_bytes=20 << 20)

    cuts = [tiles * part // CUTS[-1] for part in CUTS]
    table, windows, point, blocks = pl.pallas_call(
        functools.partial(sum_kernel, cuts=cuts, blk=blk),
        out_shape=[
            jax.ShapeDtypeStruct((slots, 8, AVG), BF16),
            jax.ShapeDtypeStruct((tiles // blk, ROWS, AVG), F32),
            jax.ShapeDtypeStruct((ROWS, points), F32),
            pltpu.SMEM(owner_blocks.shape, jnp.int32),
        ],
        in_specs=[hbm, hbm, hbm, anywhere],
        out_specs=[vmem, vmem, vmem, smem],
        scratch_shapes=[
            pltpu.VMEM((tiles, AVG), jnp.int32),
            pltpu.VMEM((4 * tiles, AVG), F32),
            pltpu.VMEM((9, points), F32),
            pltpu.VMEM((grains + AVG, AVG), F32),
            pltpu.SemaphoreType.DMA((3, len(cuts) - 1)),
            pltpu.SemaphoreType.DMA,
        ],
        compiler_params=params,
        cost_estimate=pl.CostEstimate(
            flops=64 * points * ROWS, bytes_accessed=4 * points * ROWS, transcendentals=0
        ),
        name="sums",
    )(*in_hbm, owner_blocks)
    blocks = pltpu.with_memory_space_constraint(blocks, pltpu.SMEM)

    held = [table]
    for offset in range(1, groups):
        moves = [(g, int(target(g, offset, groups))) for g in range(groups)]
        held.append(lax.ppermute(table, "grp", moves))

    fluctuation, edge_ids, edge_point, edge_windows = pl.pallas_call(
        fluctuation_kernel,
        out_shape=[
            jax.ShapeDtypeStruct((COUNT, points), BF16),
            jax.ShapeDtypeStruct((2 * EDGE, AVG), jnp.int32),
            jax.ShapeDtypeStruct((ROWS, 2 * EDGE * AVG), F32),
            jax.ShapeDtypeStruct((2, ROWS, AVG), F32),
        ],
        in_specs=[vmem, vmem, vmem],
        out_specs=[hbm, vmem, vmem, vmem],
        scratch_shapes=[
            pltpu.VMEM((COUNT, points), BF16),
            pltpu.SemaphoreType.DMA((tiles // blk,)),
        ],
        compiler_params=params,
        cost_estimate=pl.CostEstimate(
            flops=64 * points * ROWS, bytes_accessed=6 * points * ROWS, transcendentals=0
        ),
        name="fluctuation",
    )(ids, point, windows)

    held, edge_ids = lax.optimization_barrier((held, edge_ids))
    mine = pl.pallas_call(
        stack_kernel,
        out_shape=jax.ShapeDtypeStruct((groups, slots, 8, AVG), BF16),
        in_specs=[vmem] * groups,
        out_specs=vmem,
        compiler_params=params,
        name="stack",
    )(*held)
    other = lax.ppermute(mine, "slab", [(s, s ^ 1) for s in range(slabs)])
    sent = pl.pallas_call(
        route_kernel,
        out_shape=[jax.ShapeDtypeStruct((per_device + CORES, 8, AVG), BF16)] * chips,
        in_specs=[smem, vmem, vmem],
        out_specs=[vmem] * chips,
        scratch_shapes=[pltpu.VMEM((CORES, groups, slots, 8, AVG), BF16)],
        compiler_params=params,
        name="route",
    )(blocks, mine, other)
    got = [sent[0]]
    for offset in reversed(range(1, chips)):
        moves = [
            (chip * CORES + core, int(target(chip, offset, chips)) * CORES + core)
            for chip in range(chips)
            for core in range(CORES)
        ]
        got.insert(1, lax.ppermute(sent[offset], "slab", moves))
    grain_table, fluctuation = pl.pallas_call(
        functools.partial(place_kernel, groups=groups, chips=chips, blk=blk),
        out_shape=[
            jax.ShapeDtypeStruct((COUNT, grains), F32),
            jax.ShapeDtypeStruct((COUNT, points), BF16),
        ],
        in_specs=[smem] + [vmem] * (chips + 3) + [hbm],
        out_specs=[hbm, hbm],
        scratch_shapes=[
            pltpu.VMEM((chips, per_device + CORES, 8, AVG), BF16),
            pltpu.VMEM((slabs, 8, AVG), F32),
            pltpu.VMEM((COUNT, 2 * EDGE * AVG), BF16),
            pltpu.VMEM((COUNT, grains), F32),
            pltpu.SemaphoreType.DMA((3,)),
        ],
        input_output_aliases={chips + 4: 1},
        compiler_params=params,
        name="place",
    )(blocks, *reversed(got), edge_ids, edge_point, edge_windows, fluctuation)
    return (grain_table, fluctuation)


def solution(mesh):
    placed = (P(AXES), P(None, AXES), P(None, AXES), P())
    return jax.shard_map(
        local,
        mesh=mesh,
        in_specs=placed,
        out_specs=(P(None, AXES), P(None, AXES)),
        check_vma=False,
    )
```

```python
import functools

import jax
import jax.numpy as jnp
from jax import lax
from jax.experimental import pallas as pl
from jax.experimental.pallas import tpu as pltpu
from jax.sharding import PartitionSpec as P

AVG = 128
AXES = ("grp", "slab")
SUB = 8
WINDOW = 16
ROWS = 16
COUNT = 13
CORES = 2
CUTS = (0, 1, 2, 3, 4)
EDGE = 2
F32 = jnp.float32
BF16 = jnp.bfloat16


def window_sums(selector, values):
    high = values.astype(BF16)
    low = (values - high.astype(F32)).astype(BF16)
    both = jnp.concatenate([high, low], axis=0)
    return lax.dot_general(selector, both, (((1,), (1,)), ((), ())), preferred_element_type=F32)


def finish(total):
    row = lax.broadcasted_iota(jnp.int32, total.shape, 0)
    squares = jnp.sum(jnp.where(row < 4, total * total, 0.0), axis=0, keepdims=True)
    scale = jnp.where(row < 4, jnp.sqrt(squares), total[COUNT : COUNT + 1])
    return total / jnp.where(scale > 0.0, scale, 1.0)


def device_index():
    return lax.axis_index("grp") * lax.axis_size("slab") + lax.axis_index("slab")


def div_rem(x, n):
    if n & (n - 1) == 0:
        return x >> (n.bit_length() - 1), x & (n - 1)
    return lax.div(x, n), lax.rem(x, n)


def selection(ids_ref, first_tile, tiles, first_grain):
    grain_row = lax.broadcasted_iota(jnp.int32, (WINDOW, AVG), 0) + first_grain
    picks = []
    for tile in range(tiles):
        ids = jnp.broadcast_to(ids_ref[pl.ds(first_tile + tile, 1), :], (WINDOW, AVG))
        picks.append((ids == grain_row).astype(F32).astype(BF16))
    return jnp.concatenate(picks, axis=1)


def sum_kernel(
    ids_hbm, q_hbm, s_hbm, blocks_hbm, table_ref, window_ref, point_ref, blocks_ref, ids_ref, q_ref, s_ref, acc_ref,
    sems, blocks_sem, *, cuts, blk,
):
    grains = ids_hbm.shape[0]
    tile_base = device_index() * grains
    chunks = list(zip(cuts[:-1], cuts[1:]))

    def copies(chunk):
        begin, end = chunks[chunk]
        rows, quads = slice(begin, end), slice(4 * begin, 4 * end)
        lanes = slice(begin * AVG, end * AVG)
        return (
            pltpu.make_async_copy(ids_hbm.at[rows], ids_ref.at[rows], sems.at[0, chunk]),
            pltpu.make_async_copy(q_hbm.at[quads], q_ref.at[quads], sems.at[1, chunk]),
            pltpu.make_async_copy(s_hbm.at[:, lanes], s_ref.at[:, lanes], sems.at[2, chunk]),
        )

    for chunk in range(len(chunks)):
        for copy in copies(chunk):
            copy.start()
    blocks_copy = pltpu.make_async_copy(blocks_hbm, blocks_ref, blocks_sem)
    blocks_copy.start()

    quaternion = lax.broadcasted_iota(jnp.int32, (8, AVG), 0) < 4
    ones = jnp.ones((ROWS - COUNT, SUB * AVG), F32)

    carry = jnp.zeros((SUB, 2 * ROWS), F32)
    for chunk, (begin, end) in enumerate(chunks):
        for copy in copies(chunk):
            copy.wait()
        for tile in range(begin, end, SUB):
            lanes = slice(tile * AVG, (tile + SUB) * AVG)
            q = jnp.concatenate([q_ref[4 * t : 4 * t + 4, :] for t in range(tile, tile + SUB)], axis=1)
            values = jnp.concatenate([q, s_ref[:, lanes], ones], axis=0)
            sums = window_sums(selection(ids_ref, tile, SUB, tile_base + tile - 1), values)
            acc_ref[tile : tile + SUB, : 2 * ROWS] = carry + sums[:SUB]
            carry = sums[SUB:]
            parts = [q_ref[pl.ds(4 * tile + c, SUB, stride=4), :] for c in range(4)]
            scale = lax.rsqrt(sum(part * part for part in parts))
            scales = [
                jnp.where(quaternion, jnp.broadcast_to(scale[t : t + 1], (8, AVG)), 1.0) for t in range(SUB)
            ]
            point_ref[:8, lanes] = values[:8] * jnp.concatenate(scales, axis=1)
            point_ref[8:, lanes] = values[8:]
    blocks_copy.wait()
    acc_ref[grains : grains + SUB, : 2 * ROWS] = carry
    blocks = [acc_ref[block * AVG : (block + 1) * AVG, :].T for block in range(grains // AVG + 1)]
    part = jnp.concatenate([block[:ROWS] + block[ROWS : 2 * ROWS] for block in blocks], axis=1)
    rounded = finish(part).astype(BF16).astype(F32)
    for index in range(window_ref.shape[0]):
        window_ref[index] = rounded[:, index * blk : index * blk + AVG]
    own = rounded[:, 1 : 1 + grains]
    half = lax.broadcasted_iota(jnp.int32, (8, AVG), 1) < blk
    for pair in range(grains // AVG):
        top = own[:8, pair * AVG : (pair + 1) * AVG]
        low = own[8:, pair * AVG : (pair + 1) * AVG]
        table_ref[2 * pair] = jnp.where(half, top, pltpu.roll(low, blk, 1)).astype(BF16)
        table_ref[2 * pair + 1] = jnp.where(half, pltpu.roll(top, blk, 1), low).astype(BF16)
    lane = lax.broadcasted_iota(jnp.int32, (ROWS, AVG), 1)
    ends = jnp.where(lane < 2, part[:, :AVG], pltpu.roll(part[:, grains:], 2, 1))
    high = ends.astype(BF16).astype(F32)
    mid = (ends - high).astype(BF16).astype(F32)
    rest = ends - high - mid
    pieces = jnp.where(lane < 4, high, jnp.where(lane < 8, pltpu.roll(mid, 4, 1), pltpu.roll(rest, 8, 1)))
    pieces = jnp.where(lane < 12, pieces, 0.0)
    table_ref[grains // blk] = jnp.where(half, pieces[:8], pltpu.roll(pieces[8:], blk, 1)).astype(BF16)


def fluctuation_kernel(
    ids_ref, point_ref, window_ref, out_hbm, edge_ids_ref, edge_point_ref, edge_window_ref, out_ref, sems
):
    windows = window_ref.shape[0]
    total = ids_ref.shape[0]
    tile_base = device_index() * total
    tiles = total // windows
    points = tiles * AVG

    def copy(window):
        lanes = pl.ds(window * points, points)
        return pltpu.make_async_copy(out_ref.at[:, lanes], out_hbm.at[:, lanes], sems.at[window])

    def step(window):
        table = window_ref[window]
        for sub in range(tiles // SUB):
            tile = window * tiles + sub * SUB
            lanes = pl.ds(tile * AVG, SUB * AVG)
            near = pltpu.roll(table, (AVG - sub * SUB) % AVG, 1)[:, :WINDOW].astype(BF16)
            picks = selection(ids_ref, tile, SUB, tile_base + tile - 1)
            means = jnp.dot(near, picks, preferred_element_type=F32)
            out_ref[:, lanes] = (point_ref[:, lanes] - means)[:COUNT].astype(BF16)
        copy(window).start()

    for window in range(windows):
        step(window)
    first, last = slice(0, EDGE), slice(total - EDGE, total)
    edge_ids_ref[:EDGE] = ids_ref[first]
    edge_ids_ref[EDGE:] = ids_ref[last]
    edge_point_ref[:, : EDGE * AVG] = point_ref[:, : EDGE * AVG]
    edge_point_ref[:, EDGE * AVG :] = point_ref[:, (total - EDGE) * AVG :]
    edge_window_ref[0] = window_ref[0]
    edge_window_ref[1] = pltpu.roll(window_ref[windows - 1], AVG - tiles + SUB, 1)
    for window in range(windows):
        copy(window).wait()


def source(me, offset, count):
    if count & (count - 1) == 0:
        return me ^ offset
    return (me + count - offset) % count


def target(me, offset, count):
    if count & (count - 1) == 0:
        return me ^ offset
    return (me + offset) % count


def stack_kernel(*refs):
    *held_refs, out_ref = refs
    for offset, ref in enumerate(held_refs):
        out_ref[source(lax.axis_index("grp"), offset, len(held_refs))] = ref[...]


def route_kernel(blocks_ref, mine_ref, other_ref, *refs):
    *out_refs, held_ref = refs
    chips = len(out_refs)
    groups, slots = mine_ref.shape[:2]
    per_device = slots - 1
    slabs = chips * CORES
    group = lax.axis_index("grp")
    chip, core = div_rem(lax.axis_index("slab"), CORES)
    held_ref[core] = mine_ref[...]
    held_ref[1 - core] = other_ref[...]
    step = AVG // 2 // groups
    lane = lax.broadcasted_iota(jnp.int32, (8, AVG), 1) & (AVG // 2 - 1)
    for owner_core in range(CORES):
        ends = held_ref[owner_core, 0, per_device].astype(F32)
        for owner_group in range(1, groups):
            rolled = pltpu.roll(held_ref[owner_core, owner_group, per_device].astype(F32), owner_group * step, 1)
            ends = jnp.where(lane >= owner_group * step, rolled, ends)
        for out_ref in out_refs:
            out_ref[per_device + owner_core] = ends.astype(BF16)
    for offset, out_ref in enumerate(out_refs):
        wanted = (group * slabs + target(chip, offset, chips) * CORES + core) * per_device
        for slot in range(per_device):
            owner, index = div_rem(blocks_ref[wanted + slot], per_device)
            owner_group, owner_slab = div_rem(owner, slabs)
            out_ref[slot] = held_ref[div_rem(owner_slab, CORES)[1], owner_group, index]


def place_kernel(blocks_ref, *refs, groups, chips, blk):
    (*got_refs, edge_ids_ref, edge_point_ref, edge_window_ref, _, table_hbm, fluctuation_hbm, held_ref, ends_ref,
     edge_ref, table_ref, sems) = refs
    slots = got_refs[0].shape[0]
    per_device = slots - CORES
    slabs = chips * CORES
    devices = groups * slabs
    grains = table_ref.shape[1]
    step = AVG // 2 // groups
    device = device_index()
    chip = div_rem(lax.axis_index("slab"), CORES)[0]
    lane = lax.broadcasted_iota(jnp.int32, (8, AVG), 1)
    half = lane < blk

    for offset, ref in enumerate(reversed(got_refs)):
        owner_chip = source(chip, offset, chips)
        held_ref[owner_chip] = ref[...]
        for core in range(CORES):
            piece = ref[per_device + core].astype(F32)
            piece = piece + pltpu.roll(piece, AVG - 4, 1) + pltpu.roll(piece, AVG - 8, 1)
            ends_ref[owner_chip * CORES + core] = piece

    def ends(owner, column, lane):
        group, slab = div_rem(jnp.clip(owner, 0, devices - 1), slabs)
        moved = pltpu.roll(ends_ref[slab], (lane - column - step * group + 2 * AVG) & (AVG - 1), 1)
        return jnp.where((owner >= 0) & (owner < devices), moved, 0.0)

    def unfold(value):
        return jnp.concatenate([value, pltpu.roll(value, blk, 1)], axis=0)

    lane_half = lane & (blk - 1)
    others = jnp.where(lane_half < 2, ends(device - 1, 2, 0), ends(device + 1, 0, 2))
    shared = finish(unfold(ends(device, 0, 0) + others))
    wide_lane = lax.broadcasted_iota(jnp.int32, (ROWS, AVG), 1)
    first = jnp.where(wide_lane < 2, shared, edge_window_ref[0])
    in_last = (wide_lane >= SUB) & (wide_lane < SUB + 2)
    last = jnp.where(in_last, pltpu.roll(shared, SUB - 2, 1), edge_window_ref[1])
    width = EDGE * AVG
    total = fluctuation_hbm.shape[1]
    first_grain = device * grains - 1
    copies = []
    for end, (table, grain, begin) in enumerate(
        ((first, first_grain, 0), (last, first_grain + grains - SUB, total - width))
    ):
        lanes = slice(end * width, (end + 1) * width)
        picks = selection(edge_ids_ref, end * EDGE, EDGE, grain)
        means = jnp.dot(table[:, :WINDOW].astype(BF16), picks, preferred_element_type=F32)
        edge_ref[:, lanes] = (edge_point_ref[:, lanes] - means)[:COUNT].astype(BF16)
        copies.append(
            pltpu.make_async_copy(
                edge_ref.at[:, lanes], fluctuation_hbm.at[:, begin : begin + width], sems.at[end]
            )
        )
        copies[-1].start()

    tiles, columns = [], []
    sums = jnp.zeros((8, AVG), F32)
    for slot in range(per_device):
        owner, index = div_rem(blocks_ref[device * per_device + slot], per_device)
        owner_chip = div_rem(div_rem(owner, slabs)[1], CORES)[0]
        tiles.append(held_ref[owner_chip, slot].astype(F32))
        low = index == 0
        beside = jnp.where(low, owner - 1, owner + 1)
        both = ends(owner, jnp.where(low, 1, 2), slot) + ends(beside, jnp.where(low, 3, 0), slot)
        sums = jnp.where(lane_half == slot, both, sums)
        columns.append(jnp.where(low, 0, jnp.where(index == per_device - 1, blk - 1, 2 * AVG)))
    repaired = finish(unfold(sums))
    repaired = jnp.where(half, repaired[:8], pltpu.roll(repaired[8:], blk, 1))
    for slot in range(per_device):
        moved = pltpu.roll(repaired, (columns[slot] - slot + AVG) & (AVG - 1), 1)
        tiles[slot] = jnp.where(lane_half == columns[slot], moved, tiles[slot])
    for pair in range(per_device // 2):
        first, second = tiles[2 * pair], tiles[2 * pair + 1]
        lanes = slice(pair * AVG, (pair + 1) * AVG)
        table_ref[:8, lanes] = jnp.where(half, first, pltpu.roll(second, blk, 1))
        table_ref[8:, lanes] = jnp.where(half, pltpu.roll(first, blk, 1), second)[: COUNT - 8]
    copies.append(pltpu.make_async_copy(table_ref, table_hbm, sems.at[2]))
    copies[-1].start()
    for copy in copies:
        copy.wait()


def local(grain_ids, orientation, stress, owner_blocks):
    groups, slabs = lax.axis_size("grp"), lax.axis_size("slab")
    points = grain_ids.shape[0]
    tiles = points // AVG
    grains = tiles
    per_device = owner_blocks.shape[0] // (groups * slabs)
    blk = grains // per_device
    slots = per_device + 1
    chips = slabs // CORES

    ids = grain_ids.reshape(tiles, AVG)
    quads = orientation.reshape(4, tiles, AVG).transpose(1, 0, 2).reshape(4 * tiles, AVG)
    in_hbm = [pltpu.with_memory_space_constraint(x, pltpu.HBM) for x in (ids, quads, stress, owner_blocks)]
    smem = pl.BlockSpec(memory_space=pltpu.SMEM)
    vmem = pl.BlockSpec(memory_space=pltpu.VMEM)
    hbm = pl.BlockSpec(memory_space=pltpu.HBM)
    params = pltpu.CompilerParams(vmem_limit_bytes=20 << 20)

    cuts = [tiles * part // CUTS[-1] for part in CUTS]
    table, windows, point, blocks = pl.pallas_call(
        functools.partial(sum_kernel, cuts=cuts, blk=blk),
        out_shape=[
            jax.ShapeDtypeStruct((slots, 8, AVG), BF16),
            jax.ShapeDtypeStruct((tiles // blk, ROWS, AVG), F32),
            jax.ShapeDtypeStruct((ROWS, points), F32),
            pltpu.SMEM(owner_blocks.shape, jnp.int32),
        ],
        in_specs=[hbm] * 4,
        out_specs=[vmem, vmem, vmem, smem],
        scratch_shapes=[
            pltpu.VMEM((tiles, AVG), jnp.int32),
            pltpu.VMEM((4 * tiles, AVG), F32),
            pltpu.VMEM((9, points), F32),
            pltpu.VMEM((grains + AVG, AVG), F32),
            pltpu.SemaphoreType.DMA((3, len(cuts) - 1)),
            pltpu.SemaphoreType.DMA,
        ],
        compiler_params=params,
        cost_estimate=pl.CostEstimate(
            flops=64 * points * ROWS, bytes_accessed=4 * points * ROWS, transcendentals=0
        ),
        name="sums",
    )(*in_hbm)
    blocks = pltpu.with_memory_space_constraint(blocks, pltpu.SMEM)

    held = [table]
    for offset in range(1, groups):
        moves = [(g, int(target(g, offset, groups))) for g in range(groups)]
        held.append(lax.ppermute(table, "grp", moves))

    fluctuation, edge_ids, edge_point, edge_windows = pl.pallas_call(
        fluctuation_kernel,
        out_shape=[
            jax.ShapeDtypeStruct((COUNT, points), BF16),
            jax.ShapeDtypeStruct((2 * EDGE, AVG), jnp.int32),
            jax.ShapeDtypeStruct((ROWS, 2 * EDGE * AVG), F32),
            jax.ShapeDtypeStruct((2, ROWS, AVG), F32),
        ],
        in_specs=[vmem, vmem, vmem],
        out_specs=[hbm, vmem, vmem, vmem],
        scratch_shapes=[
            pltpu.VMEM((COUNT, points), BF16),
            pltpu.SemaphoreType.DMA((tiles // blk,)),
        ],
        compiler_params=params,
        cost_estimate=pl.CostEstimate(
            flops=64 * points * ROWS, bytes_accessed=6 * points * ROWS, transcendentals=0
        ),
        name="fluctuation",
    )(ids, point, windows)

    held, edge_ids = lax.optimization_barrier((held, edge_ids))
    mine = pl.pallas_call(
        stack_kernel,
        out_shape=jax.ShapeDtypeStruct((groups, slots, 8, AVG), BF16),
        in_specs=[vmem] * groups,
        out_specs=vmem,
        compiler_params=params,
        name="stack",
    )(*held)
    other = lax.ppermute(mine, "slab", [(s, s ^ 1) for s in range(slabs)])
    sent = pl.pallas_call(
        route_kernel,
        out_shape=[jax.ShapeDtypeStruct((per_device + CORES, 8, AVG), BF16)] * chips,
        in_specs=[smem, vmem, vmem],
        out_specs=[vmem] * chips,
        scratch_shapes=[pltpu.VMEM((CORES, groups, slots, 8, AVG), BF16)],
        compiler_params=params,
        name="route",
    )(blocks, mine, other)
    got = [sent[0]]
    for offset in reversed(range(1, chips)):
        moves = [
            (chip * CORES + core, int(target(chip, offset, chips)) * CORES + core)
            for chip in range(chips)
            for core in range(CORES)
        ]
        got.insert(1, lax.ppermute(sent[offset], "slab", moves))
    grain_table, fluctuation = pl.pallas_call(
        functools.partial(place_kernel, groups=groups, chips=chips, blk=blk),
        out_shape=[
            jax.ShapeDtypeStruct((COUNT, grains), F32),
            jax.ShapeDtypeStruct((COUNT, points), BF16),
        ],
        in_specs=[smem] + [vmem] * (chips + 3) + [hbm],
        out_specs=[hbm, hbm],
        scratch_shapes=[
            pltpu.VMEM((chips, per_device + CORES, 8, AVG), BF16),
            pltpu.VMEM((slabs, 8, AVG), F32),
            pltpu.VMEM((COUNT, 2 * EDGE * AVG), BF16),
            pltpu.VMEM((COUNT, grains), F32),
            pltpu.SemaphoreType.DMA((3,)),
        ],
        input_output_aliases={chips + 4: 1},
        compiler_params=params,
        name="place",
    )(blocks, *reversed(got), edge_ids, edge_point, edge_windows, fluctuation)
    return (grain_table, fluctuation)


def solution(mesh):
    placed = (P(AXES), P(None, AXES), P(None, AXES), P())
    return jax.shard_map(
        local,
        mesh=mesh,
        in_specs=placed,
        out_specs=(P(None, AXES), P(None, AXES)),
        check_vma=False,
    )
```

```python
import functools

import jax
import jax.numpy as jnp
from jax import lax
from jax.experimental import pallas as pl
from jax.experimental.pallas import tpu as pltpu
from jax.sharding import PartitionSpec as P

AVG = 128
AXES = ("grp", "slab")
SUB = 8
WINDOW = 16
ROWS = 16
COUNT = 13
CORES = 2
CUTS = (0, 1, 2, 3, 4)
EDGE = 2
F32 = jnp.float32
BF16 = jnp.bfloat16


def window_sums(selector, values):
    high = values.astype(BF16)
    low = (values - high.astype(F32)).astype(BF16)
    both = jnp.concatenate([high, low], axis=0)
    return lax.dot_general(selector, both, (((1,), (1,)), ((), ())), preferred_element_type=F32)


def finish(total):
    row = lax.broadcasted_iota(jnp.int32, total.shape, 0)
    squares = jnp.sum(jnp.where(row < 4, total * total, 0.0), axis=0, keepdims=True)
    scale = jnp.where(row < 4, jnp.sqrt(squares), total[COUNT : COUNT + 1])
    return total / jnp.where(scale > 0.0, scale, 1.0)


def device_index():
    return lax.axis_index("grp") * lax.axis_size("slab") + lax.axis_index("slab")


def div_rem(x, n):
    if n & (n - 1) == 0:
        return x >> (n.bit_length() - 1), x & (n - 1)
    return lax.div(x, n), lax.rem(x, n)


def selection(ids_ref, first_tile, tiles, first_grain):
    grain_row = lax.broadcasted_iota(jnp.int32, (WINDOW, AVG), 0) + first_grain
    picks = []
    for tile in range(tiles):
        ids = jnp.broadcast_to(ids_ref[pl.ds(first_tile + tile, 1), :], (WINDOW, AVG))
        picks.append((ids == grain_row).astype(F32).astype(BF16))
    return jnp.concatenate(picks, axis=1)


def sum_kernel(
    ids_hbm, q_hbm, s_hbm, blocks_hbm, table_ref, window_ref, point_ref, blocks_ref, ids_ref, q_ref, s_ref, acc_ref,
    sems, blocks_sem, *, cuts, blk,
):
    grains = ids_hbm.shape[0]
    tile_base = device_index() * grains
    chunks = list(zip(cuts[:-1], cuts[1:]))

    def copies(chunk):
        begin, end = chunks[chunk]
        rows, quads = slice(begin, end), slice(4 * begin, 4 * end)
        lanes = slice(begin * AVG, end * AVG)
        return (
            pltpu.make_async_copy(ids_hbm.at[rows], ids_ref.at[rows], sems.at[0, chunk]),
            pltpu.make_async_copy(q_hbm.at[quads], q_ref.at[quads], sems.at[1, chunk]),
            pltpu.make_async_copy(s_hbm.at[:, lanes], s_ref.at[:, lanes], sems.at[2, chunk]),
        )

    for chunk in range(len(chunks)):
        for copy in copies(chunk):
            copy.start()
    blocks_copy = pltpu.make_async_copy(blocks_hbm, blocks_ref, blocks_sem)
    blocks_copy.start()

    quaternion = lax.broadcasted_iota(jnp.int32, (8, AVG), 0) < 4
    ones = jnp.ones((ROWS - COUNT, SUB * AVG), F32)

    carry = jnp.zeros((SUB, 2 * ROWS), F32)
    for chunk, (begin, end) in enumerate(chunks):
        for copy in copies(chunk):
            copy.wait()
        for tile in range(begin, end, SUB):
            lanes = slice(tile * AVG, (tile + SUB) * AVG)
            q = jnp.concatenate([q_ref[4 * t : 4 * t + 4, :] for t in range(tile, tile + SUB)], axis=1)
            values = jnp.concatenate([q, s_ref[:, lanes], ones], axis=0)
            sums = window_sums(selection(ids_ref, tile, SUB, tile_base + tile - 1), values)
            acc_ref[tile : tile + SUB, : 2 * ROWS] = carry + sums[:SUB]
            carry = sums[SUB:]
            parts = [q_ref[pl.ds(4 * tile + c, SUB, stride=4), :] for c in range(4)]
            scale = lax.rsqrt(sum(part * part for part in parts))
            scales = [
                jnp.where(quaternion, jnp.broadcast_to(scale[t : t + 1], (8, AVG)), 1.0) for t in range(SUB)
            ]
            point_ref[:8, lanes] = values[:8] * jnp.concatenate(scales, axis=1)
            point_ref[8:, lanes] = values[8:]
    blocks_copy.wait()
    acc_ref[grains : grains + SUB, : 2 * ROWS] = carry
    blocks = [acc_ref[block * AVG : (block + 1) * AVG, :].T for block in range(grains // AVG + 1)]
    part = jnp.concatenate([block[:ROWS] + block[ROWS : 2 * ROWS] for block in blocks], axis=1)
    rounded = finish(part).astype(BF16).astype(F32)
    for index in range(window_ref.shape[0]):
        window_ref[index] = rounded[:, index * blk : index * blk + AVG]
    own = rounded[:, 1 : 1 + grains]
    half = lax.broadcasted_iota(jnp.int32, (8, AVG), 1) < blk
    for pair in range(grains // AVG):
        top = own[:8, pair * AVG : (pair + 1) * AVG]
        low = own[8:, pair * AVG : (pair + 1) * AVG]
        table_ref[2 * pair] = jnp.where(half, top, pltpu.roll(low, blk, 1)).astype(BF16)
        table_ref[2 * pair + 1] = jnp.where(half, pltpu.roll(top, blk, 1), low).astype(BF16)
    lane = lax.broadcasted_iota(jnp.int32, (ROWS, AVG), 1)
    ends = jnp.where(lane < 2, part[:, :AVG], pltpu.roll(part[:, grains:], 2, 1))
    high = ends.astype(BF16).astype(F32)
    mid = (ends - high).astype(BF16).astype(F32)
    rest = ends - high - mid
    pieces = jnp.where(lane < 4, high, jnp.where(lane < 8, pltpu.roll(mid, 4, 1), pltpu.roll(rest, 8, 1)))
    pieces = jnp.where(lane < 12, pieces, 0.0)
    table_ref[grains // blk] = jnp.where(half, pieces[:8], pltpu.roll(pieces[8:], blk, 1)).astype(BF16)


def fluctuation_kernel(ids_ref, point_ref, window_ref, *refs, begin, end):
    *_, out_hbm, out_ref, sems = refs
    total = ids_ref.shape[0]
    tile_base = device_index() * total
    tiles = total // window_ref.shape[0]
    points = tiles * AVG

    def copy(window):
        here = slice((window - begin) * points, (window - begin + 1) * points)
        there = slice(window * points, (window + 1) * points)
        return pltpu.make_async_copy(out_ref.at[:, here], out_hbm.at[:, there], sems.at[window - begin])

    for window in range(begin, end):
        table = window_ref[window]
        for sub in range(tiles // SUB):
            tile = window * tiles + sub * SUB
            lanes = slice(tile * AVG, (tile + SUB) * AVG)
            near = pltpu.roll(table, (AVG - sub * SUB) % AVG, 1)[:, :WINDOW].astype(BF16)
            means = jnp.dot(near, selection(ids_ref, tile, SUB, tile_base + tile - 1), preferred_element_type=F32)
            here = slice((tile - begin * tiles) * AVG, (tile - begin * tiles + SUB) * AVG)
            out_ref[:, here] = (point_ref[:, lanes] - means)[:COUNT].astype(BF16)
        copy(window).start()
    for window in range(begin, end):
        copy(window).wait()


def source(me, offset, count):
    if count & (count - 1) == 0:
        return me ^ offset
    return (me + count - offset) % count


def target(me, offset, count):
    if count & (count - 1) == 0:
        return me ^ offset
    return (me + offset) % count


def stack_kernel(*refs):
    *held_refs, out_ref = refs
    for offset, ref in enumerate(held_refs):
        out_ref[source(lax.axis_index("grp"), offset, len(held_refs))] = ref[...]


def route_kernel(blocks_ref, mine_ref, other_ref, *refs):
    *out_refs, held_ref = refs
    chips = len(out_refs)
    groups, slots = mine_ref.shape[:2]
    per_device = slots - 1
    slabs = chips * CORES
    group = lax.axis_index("grp")
    chip, core = div_rem(lax.axis_index("slab"), CORES)
    held_ref[core] = mine_ref[...]
    held_ref[1 - core] = other_ref[...]
    step = AVG // 2 // groups
    lane = lax.broadcasted_iota(jnp.int32, (8, AVG), 1) & (AVG // 2 - 1)
    for owner_core in range(CORES):
        ends = held_ref[owner_core, 0, per_device].astype(F32)
        for owner_group in range(1, groups):
            rolled = pltpu.roll(held_ref[owner_core, owner_group, per_device].astype(F32), owner_group * step, 1)
            ends = jnp.where(lane >= owner_group * step, rolled, ends)
        for out_ref in out_refs:
            out_ref[per_device + owner_core] = ends.astype(BF16)
    for offset, out_ref in enumerate(out_refs):
        wanted = (group * slabs + target(chip, offset, chips) * CORES + core) * per_device
        for slot in range(per_device):
            owner, index = div_rem(blocks_ref[wanted + slot], per_device)
            owner_group, owner_slab = div_rem(owner, slabs)
            out_ref[slot] = held_ref[div_rem(owner_slab, CORES)[1], owner_group, index]


def place_kernel(blocks_ref, *refs, groups, chips, blk):
    (*got_refs, ids_ref, point_ref, window_ref, _, table_hbm, fluctuation_hbm, held_ref, ends_ref,
     edge_ref, table_ref, sems) = refs
    slots = got_refs[0].shape[0]
    per_device = slots - CORES
    slabs = chips * CORES
    devices = groups * slabs
    grains = table_ref.shape[1]
    step = AVG // 2 // groups
    device = device_index()
    chip = div_rem(lax.axis_index("slab"), CORES)[0]
    lane = lax.broadcasted_iota(jnp.int32, (8, AVG), 1)
    half = lane < blk

    for offset, ref in enumerate(reversed(got_refs)):
        owner_chip = source(chip, offset, chips)
        held_ref[owner_chip] = ref[...]
        for core in range(CORES):
            piece = ref[per_device + core].astype(F32)
            piece = piece + pltpu.roll(piece, AVG - 4, 1) + pltpu.roll(piece, AVG - 8, 1)
            ends_ref[owner_chip * CORES + core] = piece

    def ends(owner, column, lane):
        group, slab = div_rem(jnp.clip(owner, 0, devices - 1), slabs)
        moved = pltpu.roll(ends_ref[slab], (lane - column - step * group + 2 * AVG) & (AVG - 1), 1)
        return jnp.where((owner >= 0) & (owner < devices), moved, 0.0)

    def unfold(value):
        return jnp.concatenate([value, pltpu.roll(value, blk, 1)], axis=0)

    lane_half = lane & (blk - 1)
    others = jnp.where(lane_half < 2, ends(device - 1, 2, 0), ends(device + 1, 0, 2))
    shared = finish(unfold(ends(device, 0, 0) + others))
    wide_lane = lax.broadcasted_iota(jnp.int32, (ROWS, AVG), 1)
    windows = window_ref.shape[0]
    first = jnp.where(wide_lane < 2, shared, window_ref[0])
    in_last = (wide_lane >= SUB) & (wide_lane < SUB + 2)
    last = pltpu.roll(window_ref[windows - 1], AVG - grains // windows + SUB, 1)
    last = jnp.where(in_last, pltpu.roll(shared, SUB - 2, 1), last)
    width = EDGE * AVG
    first_grain = device * grains - 1
    copies = []
    for end, (table, tile, grain) in enumerate(
        ((first, 0, first_grain), (last, grains - EDGE, first_grain + grains - SUB))
    ):
        lanes = slice(end * width, (end + 1) * width)
        points = slice(tile * AVG, tile * AVG + width)
        picks = selection(ids_ref, tile, EDGE, grain)
        means = jnp.dot(table[:, :WINDOW].astype(BF16), picks, preferred_element_type=F32)
        edge_ref[:, lanes] = (point_ref[:, points] - means)[:COUNT].astype(BF16)
        copies.append(
            pltpu.make_async_copy(
                edge_ref.at[:, lanes], fluctuation_hbm.at[:, points], sems.at[end]
            )
        )
        copies[-1].start()

    tiles, columns = [], []
    sums = jnp.zeros((8, AVG), F32)
    for slot in range(per_device):
        owner, index = div_rem(blocks_ref[device * per_device + slot], per_device)
        owner_chip = div_rem(div_rem(owner, slabs)[1], CORES)[0]
        tiles.append(held_ref[owner_chip, slot].astype(F32))
        low = index == 0
        beside = jnp.where(low, owner - 1, owner + 1)
        both = ends(owner, jnp.where(low, 1, 2), slot) + ends(beside, jnp.where(low, 3, 0), slot)
        sums = jnp.where(lane_half == slot, both, sums)
        columns.append(jnp.where(low, 0, jnp.where(index == per_device - 1, blk - 1, 2 * AVG)))
    repaired = finish(unfold(sums))
    repaired = jnp.where(half, repaired[:8], pltpu.roll(repaired[8:], blk, 1))
    for slot in range(per_device):
        moved = pltpu.roll(repaired, (columns[slot] - slot + AVG) & (AVG - 1), 1)
        tiles[slot] = jnp.where(lane_half == columns[slot], moved, tiles[slot])
    for pair in range(per_device // 2):
        first, second = tiles[2 * pair], tiles[2 * pair + 1]
        lanes = slice(pair * AVG, (pair + 1) * AVG)
        table_ref[:8, lanes] = jnp.where(half, first, pltpu.roll(second, blk, 1))
        table_ref[8:, lanes] = jnp.where(half, pltpu.roll(first, blk, 1), second)[: COUNT - 8]
    copies.append(pltpu.make_async_copy(table_ref, table_hbm, sems.at[2]))
    copies[-1].start()
    for copy in copies:
        copy.wait()


def local(grain_ids, orientation, stress, owner_blocks):
    groups, slabs = lax.axis_size("grp"), lax.axis_size("slab")
    points = grain_ids.shape[0]
    tiles = points // AVG
    grains = tiles
    per_device = owner_blocks.shape[0] // (groups * slabs)
    blk = grains // per_device
    slots = per_device + 1
    chips = slabs // CORES

    ids = grain_ids.reshape(tiles, AVG)
    quads = orientation.reshape(4, tiles, AVG).transpose(1, 0, 2).reshape(4 * tiles, AVG)
    in_hbm = [pltpu.with_memory_space_constraint(x, pltpu.HBM) for x in (ids, quads, stress, owner_blocks)]
    smem = pl.BlockSpec(memory_space=pltpu.SMEM)
    vmem = pl.BlockSpec(memory_space=pltpu.VMEM)
    hbm = pl.BlockSpec(memory_space=pltpu.HBM)
    params = pltpu.CompilerParams(vmem_limit_bytes=20 << 20)

    cuts = [tiles * part // CUTS[-1] for part in CUTS]
    table, windows, point, blocks, on_chip_ids = pl.pallas_call(
        functools.partial(sum_kernel, cuts=cuts, blk=blk),
        out_shape=[
            jax.ShapeDtypeStruct((slots, 8, AVG), BF16),
            jax.ShapeDtypeStruct((tiles // blk, ROWS, AVG), F32),
            jax.ShapeDtypeStruct((ROWS, points), F32),
            pltpu.SMEM(owner_blocks.shape, jnp.int32),
            jax.ShapeDtypeStruct((tiles, AVG), jnp.int32),
        ],
        in_specs=[hbm] * 4,
        out_specs=[vmem, vmem, vmem, smem, vmem],
        scratch_shapes=[
            pltpu.VMEM((4 * tiles, AVG), F32),
            pltpu.VMEM((9, points), F32),
            pltpu.VMEM((grains + AVG, AVG), F32),
            pltpu.SemaphoreType.DMA((3, len(cuts) - 1)),
            pltpu.SemaphoreType.DMA,
        ],
        compiler_params=params,
        cost_estimate=pl.CostEstimate(
            flops=64 * points * ROWS, bytes_accessed=4 * points * ROWS, transcendentals=0
        ),
        name="sums",
    )(*in_hbm)
    blocks = pltpu.with_memory_space_constraint(blocks, pltpu.SMEM)

    held = [table]
    for offset in range(1, groups):
        moves = [(g, int(target(g, offset, groups))) for g in range(groups)]
        held.append(lax.ppermute(table, "grp", moves))

    on_chip = (on_chip_ids, point, windows)
    count = tiles // blk

    def look_up(begin, end, earlier):
        share = (end - begin) * points // count
        return pl.pallas_call(
            functools.partial(fluctuation_kernel, begin=begin, end=end),
            out_shape=jax.ShapeDtypeStruct((COUNT, points), BF16),
            in_specs=[vmem] * 3 + [hbm] * len(earlier),
            out_specs=hbm,
            scratch_shapes=[pltpu.VMEM((COUNT, share), BF16), pltpu.SemaphoreType.DMA((end - begin,))],
            input_output_aliases={3: 0} if earlier else {},
            compiler_params=params,
            cost_estimate=pl.CostEstimate(
                flops=64 * share * ROWS, bytes_accessed=6 * share * ROWS, transcendentals=0
            ),
            name="fluctuation",
        )(*on_chip, *earlier)

    fluctuation = look_up(0, count // 2, [])
    held, fluctuation = lax.optimization_barrier((held, fluctuation))
    mine = pl.pallas_call(
        stack_kernel,
        out_shape=jax.ShapeDtypeStruct((groups, slots, 8, AVG), BF16),
        in_specs=[vmem] * groups,
        out_specs=vmem,
        compiler_params=params,
        name="stack",
    )(*held)
    other = lax.ppermute(mine, "slab", [(s, s ^ 1) for s in range(slabs)])
    fluctuation = look_up(count // 2, count, [fluctuation])
    other, fluctuation = lax.optimization_barrier((other, fluctuation))
    sent = pl.pallas_call(
        route_kernel,
        out_shape=[jax.ShapeDtypeStruct((per_device + CORES, 8, AVG), BF16)] * chips,
        in_specs=[smem, vmem, vmem],
        out_specs=[vmem] * chips,
        scratch_shapes=[pltpu.VMEM((CORES, groups, slots, 8, AVG), BF16)],
        compiler_params=params,
        name="route",
    )(blocks, mine, other)
    got = [sent[0]]
    for offset in reversed(range(1, chips)):
        moves = [
            (chip * CORES + core, int(target(chip, offset, chips)) * CORES + core)
            for chip in range(chips)
            for core in range(CORES)
        ]
        got.insert(1, lax.ppermute(sent[offset], "slab", moves))
    grain_table, fluctuation = pl.pallas_call(
        functools.partial(place_kernel, groups=groups, chips=chips, blk=blk),
        out_shape=[
            jax.ShapeDtypeStruct((COUNT, grains), F32),
            jax.ShapeDtypeStruct((COUNT, points), BF16),
        ],
        in_specs=[smem] + [vmem] * (chips + 3) + [hbm],
        out_specs=[hbm, hbm],
        scratch_shapes=[
            pltpu.VMEM((chips, per_device + CORES, 8, AVG), BF16),
            pltpu.VMEM((slabs, 8, AVG), F32),
            pltpu.VMEM((COUNT, 2 * EDGE * AVG), BF16),
            pltpu.VMEM((COUNT, grains), F32),
            pltpu.SemaphoreType.DMA((3,)),
        ],
        input_output_aliases={chips + 4: 1},
        compiler_params=params,
        name="place",
    )(blocks, *reversed(got), *on_chip, fluctuation)
    return (grain_table, fluctuation)


def solution(mesh):
    placed = (P(AXES), P(None, AXES), P(None, AXES), P())
    return jax.shard_map(
        local,
        mesh=mesh,
        in_specs=placed,
        out_specs=(P(None, AXES), P(None, AXES)),
        check_vma=False,
    )
```

```python
import functools

import jax
import jax.numpy as jnp
from jax import lax
from jax.experimental import pallas as pl
from jax.experimental.pallas import tpu as pltpu
from jax.sharding import PartitionSpec as P

AVG = 128
AXES = ("grp", "slab")
SUB = 8
WINDOW = 16
ROWS = 16
COUNT = 13
CORES = 2
CUTS = (0, 1, 2, 3, 4)
EDGE = 2
F32 = jnp.float32
BF16 = jnp.bfloat16


def window_sums(selector, values):
    high = values.astype(BF16)
    low = (values - high.astype(F32)).astype(BF16)
    both = jnp.concatenate([high, low], axis=0)
    return lax.dot_general(selector, both, (((1,), (1,)), ((), ())), preferred_element_type=F32)


def finish(total):
    row = lax.broadcasted_iota(jnp.int32, total.shape, 0)
    squares = jnp.sum(jnp.where(row < 4, total * total, 0.0), axis=0, keepdims=True)
    scale = jnp.where(row < 4, jnp.sqrt(squares), total[COUNT : COUNT + 1])
    return total / jnp.where(scale > 0.0, scale, 1.0)


def device_index():
    return lax.axis_index("grp") * lax.axis_size("slab") + lax.axis_index("slab")


def div_rem(x, n):
    if n & (n - 1) == 0:
        return x >> (n.bit_length() - 1), x & (n - 1)
    return lax.div(x, n), lax.rem(x, n)


def selection(ids_ref, first_tile, tiles, first_grain):
    grain_row = lax.broadcasted_iota(jnp.int32, (WINDOW, AVG), 0) + first_grain
    picks = []
    for tile in range(tiles):
        ids = jnp.broadcast_to(ids_ref[pl.ds(first_tile + tile, 1), :], (WINDOW, AVG))
        picks.append((ids == grain_row).astype(F32).astype(BF16))
    return jnp.concatenate(picks, axis=1)


def sum_kernel(
    ids_hbm, q_hbm, s_hbm, blocks_hbm, table_ref, window_ref, point_ref, blocks_ref, ids_ref, q_ref, s_ref, acc_ref,
    sems, blocks_sem, *, cuts, blk,
):
    grains = ids_hbm.shape[0]
    tile_base = device_index() * grains
    chunks = list(zip(cuts[:-1], cuts[1:]))

    def copies(chunk):
        begin, end = chunks[chunk]
        rows, quads = slice(begin, end), slice(4 * begin, 4 * end)
        lanes = slice(begin * AVG, end * AVG)
        return (
            pltpu.make_async_copy(ids_hbm.at[rows], ids_ref.at[rows], sems.at[0, chunk]),
            pltpu.make_async_copy(q_hbm.at[quads], q_ref.at[quads], sems.at[1, chunk]),
            pltpu.make_async_copy(s_hbm.at[:, lanes], s_ref.at[:, lanes], sems.at[2, chunk]),
        )

    for chunk in range(len(chunks)):
        for copy in copies(chunk):
            copy.start()
    blocks_copy = pltpu.make_async_copy(blocks_hbm, blocks_ref, blocks_sem)
    blocks_copy.start()

    quaternion = lax.broadcasted_iota(jnp.int32, (8, AVG), 0) < 4
    ones = jnp.ones((ROWS - COUNT, SUB * AVG), F32)

    carry = jnp.zeros((SUB, 2 * ROWS), F32)
    for chunk, (begin, end) in enumerate(chunks):
        for copy in copies(chunk):
            copy.wait()
        for tile in range(begin, end, SUB):
            lanes = slice(tile * AVG, (tile + SUB) * AVG)
            q = jnp.concatenate([q_ref[4 * t : 4 * t + 4, :] for t in range(tile, tile + SUB)], axis=1)
            values = jnp.concatenate([q, s_ref[:, lanes], ones], axis=0)
            sums = window_sums(selection(ids_ref, tile, SUB, tile_base + tile - 1), values)
            acc_ref[tile : tile + SUB, : 2 * ROWS] = carry + sums[:SUB]
            carry = sums[SUB:]
            parts = [q_ref[pl.ds(4 * tile + c, SUB, stride=4), :] for c in range(4)]
            scale = lax.rsqrt(sum(part * part for part in parts))
            scales = [
                jnp.where(quaternion, jnp.broadcast_to(scale[t : t + 1], (8, AVG)), 1.0) for t in range(SUB)
            ]
            point_ref[:8, lanes] = values[:8] * jnp.concatenate(scales, axis=1)
            point_ref[8:, lanes] = values[8:]
    blocks_copy.wait()
    acc_ref[grains : grains + SUB, : 2 * ROWS] = carry
    blocks = [acc_ref[block * AVG : (block + 1) * AVG, :].T for block in range(grains // AVG + 1)]
    part = jnp.concatenate([block[:ROWS] + block[ROWS : 2 * ROWS] for block in blocks], axis=1)
    rounded = finish(part).astype(BF16).astype(F32)
    for index in range(window_ref.shape[0]):
        window_ref[index] = rounded[:, index * blk : index * blk + AVG]
    own = rounded[:, 1 : 1 + grains]
    half = lax.broadcasted_iota(jnp.int32, (8, AVG), 1) < blk
    for pair in range(grains // AVG):
        top = own[:8, pair * AVG : (pair + 1) * AVG]
        low = own[8:, pair * AVG : (pair + 1) * AVG]
        table_ref[2 * pair] = jnp.where(half, top, pltpu.roll(low, blk, 1)).astype(BF16)
        table_ref[2 * pair + 1] = jnp.where(half, pltpu.roll(top, blk, 1), low).astype(BF16)
    lane = lax.broadcasted_iota(jnp.int32, (ROWS, AVG), 1)
    ends = jnp.where(lane < 2, part[:, :AVG], pltpu.roll(part[:, grains:], 2, 1))
    high = ends.astype(BF16).astype(F32)
    mid = (ends - high).astype(BF16).astype(F32)
    rest = ends - high - mid
    pieces = jnp.where(lane < 4, high, jnp.where(lane < 8, pltpu.roll(mid, 4, 1), pltpu.roll(rest, 8, 1)))
    pieces = jnp.where(lane < 12, pieces, 0.0)
    table_ref[grains // blk] = jnp.where(half, pieces[:8], pltpu.roll(pieces[8:], blk, 1)).astype(BF16)


def fluctuation_kernel(ids_ref, point_ref, window_ref, *refs, begin, end):
    *_, out_hbm, out_ref, sems = refs
    total = ids_ref.shape[0]
    tile_base = device_index() * total
    tiles = total // window_ref.shape[0]
    points = tiles * AVG

    def copy(window):
        here = slice((window - begin) * points, (window - begin + 1) * points)
        there = slice(window * points, (window + 1) * points)
        return pltpu.make_async_copy(out_ref.at[:, here], out_hbm.at[:, there], sems.at[window - begin])

    for window in range(begin, end):
        table = window_ref[window]
        for sub in range(tiles // SUB):
            tile = window * tiles + sub * SUB
            lanes = slice(tile * AVG, (tile + SUB) * AVG)
            near = pltpu.roll(table, (AVG - sub * SUB) % AVG, 1)[:, :WINDOW].astype(BF16)
            means = jnp.dot(near, selection(ids_ref, tile, SUB, tile_base + tile - 1), preferred_element_type=F32)
            here = slice((tile - begin * tiles) * AVG, (tile - begin * tiles + SUB) * AVG)
            out_ref[:, here] = (point_ref[:, lanes] - means)[:COUNT].astype(BF16)
        copy(window).start()
    for window in range(begin, end):
        copy(window).wait()


def source(me, offset, count):
    if count & (count - 1) == 0:
        return me ^ offset
    return (me + count - offset) % count


def target(me, offset, count):
    if count & (count - 1) == 0:
        return me ^ offset
    return (me + offset) % count


def stack_kernel(*refs):
    *held_refs, out_ref = refs
    for offset, ref in enumerate(held_refs):
        out_ref[source(lax.axis_index("grp"), offset, len(held_refs))] = ref[...]


def route_kernel(blocks_ref, mine_ref, other_ref, *refs):
    *out_refs, held_ref = refs
    chips = len(out_refs)
    groups, slots = mine_ref.shape[:2]
    per_device = slots - 1
    slabs = chips * CORES
    group = lax.axis_index("grp")
    chip, core = div_rem(lax.axis_index("slab"), CORES)
    held_ref[core] = mine_ref[...]
    held_ref[1 - core] = other_ref[...]
    step = AVG // 2 // groups
    lane = lax.broadcasted_iota(jnp.int32, (8, AVG), 1) & (AVG // 2 - 1)
    for owner_core in range(CORES):
        ends = held_ref[owner_core, 0, per_device].astype(F32)
        for owner_group in range(1, groups):
            rolled = pltpu.roll(held_ref[owner_core, owner_group, per_device].astype(F32), owner_group * step, 1)
            ends = jnp.where(lane >= owner_group * step, rolled, ends)
        for out_ref in out_refs:
            out_ref[per_device + owner_core] = ends.astype(BF16)
    for offset, out_ref in enumerate(out_refs):
        wanted = (group * slabs + target(chip, offset, chips) * CORES + core) * per_device
        for slot in range(per_device):
            owner, index = div_rem(blocks_ref[wanted + slot], per_device)
            owner_group, owner_slab = div_rem(owner, slabs)
            out_ref[slot] = held_ref[div_rem(owner_slab, CORES)[1], owner_group, index]


def place_kernel(blocks_ref, *refs, groups, chips, blk):
    (*got_refs, ids_ref, point_ref, window_ref, _, table_hbm, fluctuation_hbm, held_ref, ends_ref,
     edge_ref, table_ref, sems) = refs
    slots = got_refs[0].shape[0]
    per_device = slots - CORES
    slabs = chips * CORES
    devices = groups * slabs
    grains = table_ref.shape[1]
    step = AVG // 2 // groups
    device = device_index()
    chip = div_rem(lax.axis_index("slab"), CORES)[0]
    lane = lax.broadcasted_iota(jnp.int32, (8, AVG), 1)
    half = lane < blk

    for offset, ref in enumerate(reversed(got_refs)):
        owner_chip = source(chip, offset, chips)
        held_ref[owner_chip] = ref[...]
        for core in range(CORES):
            piece = ref[per_device + core].astype(F32)
            piece = piece + pltpu.roll(piece, AVG - 4, 1) + pltpu.roll(piece, AVG - 8, 1)
            ends_ref[owner_chip * CORES + core] = piece

    def ends(owner, column, lane):
        group, slab = div_rem(jnp.clip(owner, 0, devices - 1), slabs)
        moved = pltpu.roll(ends_ref[slab], (lane - column - step * group + 2 * AVG) & (AVG - 1), 1)
        return jnp.where((owner >= 0) & (owner < devices), moved, 0.0)

    def unfold(value):
        return jnp.concatenate([value, pltpu.roll(value, blk, 1)], axis=0)

    lane_half = lane & (blk - 1)
    others = jnp.where(lane_half < 2, ends(device - 1, 2, 0), ends(device + 1, 0, 2))
    shared = finish(unfold(ends(device, 0, 0) + others))
    wide_lane = lax.broadcasted_iota(jnp.int32, (ROWS, AVG), 1)
    windows = window_ref.shape[0]
    first = jnp.where(wide_lane < 2, shared, window_ref[0])
    in_last = (wide_lane >= SUB) & (wide_lane < SUB + 2)
    last = pltpu.roll(window_ref[windows - 1], AVG - grains // windows + SUB, 1)
    last = jnp.where(in_last, pltpu.roll(shared, SUB - 2, 1), last)
    width = EDGE * AVG
    first_grain = device * grains - 1
    copies = []
    for end, (table, tile, grain) in enumerate(
        ((first, 0, first_grain), (last, grains - EDGE, first_grain + grains - SUB))
    ):
        lanes = slice(end * width, (end + 1) * width)
        points = slice(tile * AVG, tile * AVG + width)
        picks = selection(ids_ref, tile, EDGE, grain)
        means = jnp.dot(table[:, :WINDOW].astype(BF16), picks, preferred_element_type=F32)
        edge_ref[:, lanes] = (point_ref[:, points] - means)[:COUNT].astype(BF16)
        copies.append(
            pltpu.make_async_copy(
                edge_ref.at[:, lanes], fluctuation_hbm.at[:, points], sems.at[end]
            )
        )
        copies[-1].start()

    tiles, columns = [], []
    sums = jnp.zeros((8, AVG), F32)
    for slot in range(per_device):
        owner, index = div_rem(blocks_ref[device * per_device + slot], per_device)
        owner_chip = div_rem(div_rem(owner, slabs)[1], CORES)[0]
        tiles.append(held_ref[owner_chip, slot].astype(F32))
        low = index == 0
        beside = jnp.where(low, owner - 1, owner + 1)
        both = ends(owner, jnp.where(low, 1, 2), slot) + ends(beside, jnp.where(low, 3, 0), slot)
        sums = jnp.where(lane_half == slot, both, sums)
        columns.append(jnp.where(low, 0, jnp.where(index == per_device - 1, blk - 1, 2 * AVG)))
    repaired = finish(unfold(sums))
    repaired = jnp.where(half, repaired[:8], pltpu.roll(repaired[8:], blk, 1))
    for slot in range(per_device):
        moved = pltpu.roll(repaired, (columns[slot] - slot + AVG) & (AVG - 1), 1)
        tiles[slot] = jnp.where(lane_half == columns[slot], moved, tiles[slot])
    for pair in range(per_device // 2):
        first, second = tiles[2 * pair], tiles[2 * pair + 1]
        lanes = slice(pair * AVG, (pair + 1) * AVG)
        table_ref[:8, lanes] = jnp.where(half, first, pltpu.roll(second, blk, 1))
        table_ref[8:, lanes] = jnp.where(half, pltpu.roll(first, blk, 1), second)[: COUNT - 8]
    copies.append(pltpu.make_async_copy(table_ref, table_hbm, sems.at[2]))
    copies[-1].start()
    for copy in copies:
        copy.wait()


def local(grain_ids, orientation, stress, owner_blocks):
    groups, slabs = lax.axis_size("grp"), lax.axis_size("slab")
    points = grain_ids.shape[0]
    tiles = points // AVG
    grains = tiles
    per_device = owner_blocks.shape[0] // (groups * slabs)
    blk = grains // per_device
    slots = per_device + 1
    chips = slabs // CORES

    ids = grain_ids.reshape(tiles, AVG)
    quads = orientation.reshape(4, tiles, AVG).transpose(1, 0, 2).reshape(4 * tiles, AVG)
    in_hbm = [pltpu.with_memory_space_constraint(x, pltpu.HBM) for x in (ids, quads, stress, owner_blocks)]
    smem = pl.BlockSpec(memory_space=pltpu.SMEM)
    vmem = pl.BlockSpec(memory_space=pltpu.VMEM)
    hbm = pl.BlockSpec(memory_space=pltpu.HBM)
    params = pltpu.CompilerParams(vmem_limit_bytes=20 << 20)

    cuts = [tiles * part // CUTS[-1] for part in CUTS]
    table, windows, point, blocks, on_chip_ids = pl.pallas_call(
        functools.partial(sum_kernel, cuts=cuts, blk=blk),
        out_shape=[
            jax.ShapeDtypeStruct((slots, 8, AVG), BF16),
            jax.ShapeDtypeStruct((tiles // blk, ROWS, AVG), F32),
            jax.ShapeDtypeStruct((ROWS, points), F32),
            pltpu.SMEM(owner_blocks.shape, jnp.int32),
            jax.ShapeDtypeStruct((tiles, AVG), jnp.int32),
        ],
        in_specs=[hbm] * 4,
        out_specs=[vmem, vmem, vmem, smem, vmem],
        scratch_shapes=[
            pltpu.VMEM((4 * tiles, AVG), F32),
            pltpu.VMEM((9, points), F32),
            pltpu.VMEM((grains + AVG, AVG), F32),
            pltpu.SemaphoreType.DMA((3, len(cuts) - 1)),
            pltpu.SemaphoreType.DMA,
        ],
        compiler_params=params,
        cost_estimate=pl.CostEstimate(
            flops=64 * points * ROWS, bytes_accessed=4 * points * ROWS, transcendentals=0
        ),
        name="sums",
    )(*in_hbm)
    blocks = pltpu.with_memory_space_constraint(blocks, pltpu.SMEM)

    held = [table]
    for offset in range(1, groups):
        moves = [(g, int(target(g, offset, groups))) for g in range(groups)]
        held.append(lax.ppermute(table, "grp", moves))

    on_chip = (on_chip_ids, point, windows)
    count = tiles // blk

    def look_up(begin, end, earlier):
        share = (end - begin) * points // count
        return pl.pallas_call(
            functools.partial(fluctuation_kernel, begin=begin, end=end),
            out_shape=jax.ShapeDtypeStruct((COUNT, points), BF16),
            in_specs=[vmem] * 3 + [hbm] * len(earlier),
            out_specs=hbm,
            scratch_shapes=[pltpu.VMEM((COUNT, share), BF16), pltpu.SemaphoreType.DMA((end - begin,))],
            input_output_aliases={3: 0} if earlier else {},
            compiler_params=params,
            cost_estimate=pl.CostEstimate(
                flops=64 * share * ROWS, bytes_accessed=6 * share * ROWS, transcendentals=0
            ),
            name="fluctuation",
        )(*on_chip, *earlier)

    fluctuation = look_up(0, count // 2, [])
    held, fluctuation = lax.optimization_barrier((held, fluctuation))
    mine = pl.pallas_call(
        stack_kernel,
        out_shape=jax.ShapeDtypeStruct((groups, slots, 8, AVG), BF16),
        in_specs=[vmem] * groups,
        out_specs=vmem,
        compiler_params=params,
        name="stack",
    )(*held)
    other = lax.ppermute(mine, "slab", [(s, s ^ 1) for s in range(slabs)])
    sent = pl.pallas_call(
        route_kernel,
        out_shape=[jax.ShapeDtypeStruct((per_device + CORES, 8, AVG), BF16)] * chips,
        in_specs=[smem, vmem, vmem],
        out_specs=[vmem] * chips,
        scratch_shapes=[pltpu.VMEM((CORES, groups, slots, 8, AVG), BF16)],
        compiler_params=params,
        name="route",
    )(blocks, mine, other)
    sent, fluctuation = lax.optimization_barrier((sent, fluctuation))
    fluctuation = look_up(count // 2, count, [fluctuation])
    got = [sent[0]]
    for offset in reversed(range(1, chips)):
        moves = [
            (chip * CORES + core, int(target(chip, offset, chips)) * CORES + core)
            for chip in range(chips)
            for core in range(CORES)
        ]
        got.insert(1, lax.ppermute(sent[offset], "slab", moves))
    grain_table, fluctuation = pl.pallas_call(
        functools.partial(place_kernel, groups=groups, chips=chips, blk=blk),
        out_shape=[
            jax.ShapeDtypeStruct((COUNT, grains), F32),
            jax.ShapeDtypeStruct((COUNT, points), BF16),
        ],
        in_specs=[smem] + [vmem] * (chips + 3) + [hbm],
        out_specs=[hbm, hbm],
        scratch_shapes=[
            pltpu.VMEM((chips, per_device + CORES, 8, AVG), BF16),
            pltpu.VMEM((slabs, 8, AVG), F32),
            pltpu.VMEM((COUNT, 2 * EDGE * AVG), BF16),
            pltpu.VMEM((COUNT, grains), F32),
            pltpu.SemaphoreType.DMA((3,)),
        ],
        input_output_aliases={chips + 4: 1},
        compiler_params=params,
        name="place",
    )(blocks, *reversed(got), *on_chip, fluctuation)
    return (grain_table, fluctuation)


def solution(mesh):
    placed = (P(AXES), P(None, AXES), P(None, AXES), P())
    return jax.shard_map(
        local,
        mesh=mesh,
        in_specs=placed,
        out_specs=(P(None, AXES), P(None, AXES)),
        check_vma=False,
    )
```

```python
import functools

import jax
import jax.numpy as jnp
from jax import lax
from jax.experimental import pallas as pl
from jax.experimental.pallas import tpu as pltpu
from jax.sharding import PartitionSpec as P

AVG = 128
AXES = ("grp", "slab")
SUB = 8
WINDOW = 16
ROWS = 16
COUNT = 13
CORES = 2
CUTS = (0, 1, 2, 3, 4)
EDGE = 2
F32 = jnp.float32
BF16 = jnp.bfloat16


def window_sums(selector, values):
    high = values.astype(BF16)
    low = (values - high.astype(F32)).astype(BF16)
    both = jnp.concatenate([high, low], axis=0)
    return lax.dot_general(selector, both, (((1,), (1,)), ((), ())), preferred_element_type=F32)


def finish(total):
    row = lax.broadcasted_iota(jnp.int32, total.shape, 0)
    squares = jnp.sum(jnp.where(row < 4, total * total, 0.0), axis=0, keepdims=True)
    scale = jnp.where(row < 4, jnp.sqrt(squares), total[COUNT : COUNT + 1])
    return total / jnp.where(scale > 0.0, scale, 1.0)


def device_index():
    return lax.axis_index("grp") * lax.axis_size("slab") + lax.axis_index("slab")


def div_rem(x, n):
    if n & (n - 1) == 0:
        return x >> (n.bit_length() - 1), x & (n - 1)
    return lax.div(x, n), lax.rem(x, n)


def selection(ids_ref, first_tile, tiles, first_grain):
    grain_row = lax.broadcasted_iota(jnp.int32, (WINDOW, AVG), 0) + first_grain
    picks = []
    for tile in range(tiles):
        ids = jnp.broadcast_to(ids_ref[pl.ds(first_tile + tile, 1), :], (WINDOW, AVG))
        picks.append((ids == grain_row).astype(F32).astype(BF16))
    return jnp.concatenate(picks, axis=1)


def sum_kernel(
    ids_hbm, q_hbm, s_hbm, blocks_hbm, table_ref, window_ref, point_ref, blocks_ref, ids_ref, q_ref, s_ref, acc_ref,
    sems, blocks_sem, *, cuts, blk,
):
    grains = ids_hbm.shape[0]
    tile_base = device_index() * grains
    chunks = list(zip(cuts[:-1], cuts[1:]))

    def copies(chunk):
        begin, end = chunks[chunk]
        rows, quads = slice(begin, end), slice(4 * begin, 4 * end)
        lanes = slice(begin * AVG, end * AVG)
        return (
            pltpu.make_async_copy(ids_hbm.at[rows], ids_ref.at[rows], sems.at[0, chunk]),
            pltpu.make_async_copy(q_hbm.at[quads], q_ref.at[quads], sems.at[1, chunk]),
            pltpu.make_async_copy(s_hbm.at[:, lanes], s_ref.at[:, lanes], sems.at[2, chunk]),
        )

    for chunk in range(len(chunks)):
        for copy in copies(chunk):
            copy.start()
    blocks_copy = pltpu.make_async_copy(blocks_hbm, blocks_ref, blocks_sem)
    blocks_copy.start()

    quaternion = lax.broadcasted_iota(jnp.int32, (8, AVG), 0) < 4
    ones = jnp.ones((ROWS - COUNT, SUB * AVG), F32)

    carry = jnp.zeros((SUB, 2 * ROWS), F32)
    for chunk, (begin, end) in enumerate(chunks):
        for copy in copies(chunk):
            copy.wait()
        for tile in range(begin, end, SUB):
            lanes = slice(tile * AVG, (tile + SUB) * AVG)
            q = jnp.concatenate([q_ref[4 * t : 4 * t + 4, :] for t in range(tile, tile + SUB)], axis=1)
            values = jnp.concatenate([q, s_ref[:, lanes], ones], axis=0)
            sums = window_sums(selection(ids_ref, tile, SUB, tile_base + tile - 1), values)
            acc_ref[tile : tile + SUB, : 2 * ROWS] = carry + sums[:SUB]
            carry = sums[SUB:]
            parts = [q_ref[pl.ds(4 * tile + c, SUB, stride=4), :] for c in range(4)]
            scale = lax.rsqrt(sum(part * part for part in parts))
            scales = [
                jnp.where(quaternion, jnp.broadcast_to(scale[t : t + 1], (8, AVG)), 1.0) for t in range(SUB)
            ]
            point_ref[:8, lanes] = values[:8] * jnp.concatenate(scales, axis=1)
            point_ref[8:, lanes] = values[8:]
    blocks_copy.wait()
    acc_ref[grains : grains + SUB, : 2 * ROWS] = carry
    blocks = [acc_ref[block * AVG : (block + 1) * AVG, :].T for block in range(grains // AVG + 1)]
    part = jnp.concatenate([block[:ROWS] + block[ROWS : 2 * ROWS] for block in blocks], axis=1)
    rounded = finish(part).astype(BF16).astype(F32)
    for index in range(window_ref.shape[0]):
        window_ref[index] = rounded[:, index * blk : index * blk + AVG]
    own = rounded[:, 1 : 1 + grains]
    half = lax.broadcasted_iota(jnp.int32, (8, AVG), 1) < blk
    for pair in range(grains // AVG):
        top = own[:8, pair * AVG : (pair + 1) * AVG]
        low = own[8:, pair * AVG : (pair + 1) * AVG]
        table_ref[2 * pair] = jnp.where(half, top, pltpu.roll(low, blk, 1)).astype(BF16)
        table_ref[2 * pair + 1] = jnp.where(half, pltpu.roll(top, blk, 1), low).astype(BF16)
    lane = lax.broadcasted_iota(jnp.int32, (ROWS, AVG), 1)
    ends = jnp.where(lane < 2, part[:, :AVG], pltpu.roll(part[:, grains:], 2, 1))
    high = ends.astype(BF16).astype(F32)
    mid = (ends - high).astype(BF16).astype(F32)
    rest = ends - high - mid
    pieces = jnp.where(lane < 4, high, jnp.where(lane < 8, pltpu.roll(mid, 4, 1), pltpu.roll(rest, 8, 1)))
    pieces = jnp.where(lane < 12, pieces, 0.0)
    table_ref[grains // blk] = jnp.where(half, pieces[:8], pltpu.roll(pieces[8:], blk, 1)).astype(BF16)


def fluctuation_kernel(ids_ref, point_ref, window_ref, *refs, begin, end):
    *_, out_hbm, out_ref, sems = refs
    total = ids_ref.shape[0]
    tile_base = device_index() * total
    tiles = total // window_ref.shape[0]
    points = tiles * AVG

    def copy(window):
        here = slice((window - begin) * points, (window - begin + 1) * points)
        there = slice(window * points, (window + 1) * points)
        return pltpu.make_async_copy(out_ref.at[:, here], out_hbm.at[:, there], sems.at[window - begin])

    for window in range(begin, end):
        table = window_ref[window]
        for sub in range(tiles // SUB):
            tile = window * tiles + sub * SUB
            lanes = slice(tile * AVG, (tile + SUB) * AVG)
            near = pltpu.roll(table, (AVG - sub * SUB) % AVG, 1)[:, :WINDOW].astype(BF16)
            means = jnp.dot(near, selection(ids_ref, tile, SUB, tile_base + tile - 1), preferred_element_type=F32)
            here = slice((tile - begin * tiles) * AVG, (tile - begin * tiles + SUB) * AVG)
            out_ref[:, here] = (point_ref[:, lanes] - means)[:COUNT].astype(BF16)
        copy(window).start()
    for window in range(begin, end):
        copy(window).wait()


def source(me, offset, count):
    if count & (count - 1) == 0:
        return me ^ offset
    return (me + count - offset) % count


def target(me, offset, count):
    if count & (count - 1) == 0:
        return me ^ offset
    return (me + offset) % count


def stack_kernel(*refs):
    *held_refs, out_ref = refs
    for offset, ref in enumerate(held_refs):
        out_ref[source(lax.axis_index("grp"), offset, len(held_refs))] = ref[...]


def route_kernel(blocks_ref, mine_ref, other_ref, *refs):
    *out_refs, held_ref = refs
    chips = len(out_refs)
    groups, slots = mine_ref.shape[:2]
    per_device = slots - 1
    slabs = chips * CORES
    group = lax.axis_index("grp")
    chip, core = div_rem(lax.axis_index("slab"), CORES)
    held_ref[core] = mine_ref[...]
    held_ref[1 - core] = other_ref[...]
    step = AVG // 2 // groups
    lane = lax.broadcasted_iota(jnp.int32, (8, AVG), 1) & (AVG // 2 - 1)
    for owner_core in range(CORES):
        ends = held_ref[owner_core, 0, per_device].astype(F32)
        for owner_group in range(1, groups):
            rolled = pltpu.roll(held_ref[owner_core, owner_group, per_device].astype(F32), owner_group * step, 1)
            ends = jnp.where(lane >= owner_group * step, rolled, ends)
        for out_ref in out_refs:
            out_ref[per_device + owner_core] = ends.astype(BF16)
    for offset, out_ref in enumerate(out_refs):
        wanted = (group * slabs + target(chip, offset, chips) * CORES + core) * per_device
        for slot in range(per_device):
            owner, index = div_rem(blocks_ref[wanted + slot], per_device)
            owner_group, owner_slab = div_rem(owner, slabs)
            out_ref[slot] = held_ref[div_rem(owner_slab, CORES)[1], owner_group, index]


def place_kernel(blocks_ref, *refs, groups, chips, blk):
    (*got_refs, ids_ref, point_ref, window_ref, _, table_hbm, fluctuation_hbm, held_ref, ends_ref,
     edge_ref, table_ref, sems) = refs
    slots = got_refs[0].shape[0]
    per_device = slots - CORES
    slabs = chips * CORES
    devices = groups * slabs
    grains = table_ref.shape[1]
    step = AVG // 2 // groups
    device = device_index()
    chip = div_rem(lax.axis_index("slab"), CORES)[0]
    lane = lax.broadcasted_iota(jnp.int32, (8, AVG), 1)
    half = lane < blk

    for offset, ref in enumerate(reversed(got_refs)):
        owner_chip = source(chip, offset, chips)
        held_ref[owner_chip] = ref[...]
        for core in range(CORES):
            piece = ref[per_device + core].astype(F32)
            piece = piece + pltpu.roll(piece, AVG - 4, 1) + pltpu.roll(piece, AVG - 8, 1)
            ends_ref[owner_chip * CORES + core] = piece

    def ends(owner, column, lane):
        group, slab = div_rem(jnp.clip(owner, 0, devices - 1), slabs)
        moved = pltpu.roll(ends_ref[slab], (lane - column - step * group + 2 * AVG) & (AVG - 1), 1)
        return jnp.where((owner >= 0) & (owner < devices), moved, 0.0)

    def unfold(value):
        return jnp.concatenate([value, pltpu.roll(value, blk, 1)], axis=0)

    lane_half = lane & (blk - 1)
    others = jnp.where(lane_half < 2, ends(device - 1, 2, 0), ends(device + 1, 0, 2))
    shared = finish(unfold(ends(device, 0, 0) + others))
    wide_lane = lax.broadcasted_iota(jnp.int32, (ROWS, AVG), 1)
    windows = window_ref.shape[0]
    first = jnp.where(wide_lane < 2, shared, window_ref[0])
    in_last = (wide_lane >= SUB) & (wide_lane < SUB + 2)
    last = pltpu.roll(window_ref[windows - 1], AVG - grains // windows + SUB, 1)
    last = jnp.where(in_last, pltpu.roll(shared, SUB - 2, 1), last)
    width = EDGE * AVG
    first_grain = device * grains - 1
    copies = []
    for end, (table, tile, grain) in enumerate(
        ((first, 0, first_grain), (last, grains - EDGE, first_grain + grains - SUB))
    ):
        lanes = slice(end * width, (end + 1) * width)
        points = slice(tile * AVG, tile * AVG + width)
        picks = selection(ids_ref, tile, EDGE, grain)
        means = jnp.dot(table[:, :WINDOW].astype(BF16), picks, preferred_element_type=F32)
        edge_ref[:, lanes] = (point_ref[:, points] - means)[:COUNT].astype(BF16)
        copies.append(
            pltpu.make_async_copy(
                edge_ref.at[:, lanes], fluctuation_hbm.at[:, points], sems.at[end]
            )
        )

    tiles, columns = [], []
    sums = jnp.zeros((8, AVG), F32)
    for slot in range(per_device):
        owner, index = div_rem(blocks_ref[device * per_device + slot], per_device)
        owner_chip = div_rem(div_rem(owner, slabs)[1], CORES)[0]
        tiles.append(held_ref[owner_chip, slot].astype(F32))
        low = index == 0
        beside = jnp.where(low, owner - 1, owner + 1)
        both = ends(owner, jnp.where(low, 1, 2), slot) + ends(beside, jnp.where(low, 3, 0), slot)
        sums = jnp.where(lane_half == slot, both, sums)
        columns.append(jnp.where(low, 0, jnp.where(index == per_device - 1, blk - 1, 2 * AVG)))
    repaired = finish(unfold(sums))
    repaired = jnp.where(half, repaired[:8], pltpu.roll(repaired[8:], blk, 1))
    for slot in range(per_device):
        moved = pltpu.roll(repaired, (columns[slot] - slot + AVG) & (AVG - 1), 1)
        tiles[slot] = jnp.where(lane_half == columns[slot], moved, tiles[slot])
    for pair in range(per_device // 2):
        first, second = tiles[2 * pair], tiles[2 * pair + 1]
        lanes = slice(pair * AVG, (pair + 1) * AVG)
        table_ref[:8, lanes] = jnp.where(half, first, pltpu.roll(second, blk, 1))
        table_ref[8:, lanes] = jnp.where(half, pltpu.roll(first, blk, 1), second)[: COUNT - 8]
    copies.insert(0, pltpu.make_async_copy(table_ref, table_hbm, sems.at[2]))
    for copy in copies:
        copy.start()
    for copy in copies:
        copy.wait()


def local(grain_ids, orientation, stress, owner_blocks):
    groups, slabs = lax.axis_size("grp"), lax.axis_size("slab")
    points = grain_ids.shape[0]
    tiles = points // AVG
    grains = tiles
    per_device = owner_blocks.shape[0] // (groups * slabs)
    blk = grains // per_device
    slots = per_device + 1
    chips = slabs // CORES

    ids = grain_ids.reshape(tiles, AVG)
    quads = orientation.reshape(4, tiles, AVG).transpose(1, 0, 2).reshape(4 * tiles, AVG)
    in_hbm = [pltpu.with_memory_space_constraint(x, pltpu.HBM) for x in (ids, quads, stress, owner_blocks)]
    smem = pl.BlockSpec(memory_space=pltpu.SMEM)
    vmem = pl.BlockSpec(memory_space=pltpu.VMEM)
    hbm = pl.BlockSpec(memory_space=pltpu.HBM)
    params = pltpu.CompilerParams(vmem_limit_bytes=20 << 20)

    cuts = [tiles * part // CUTS[-1] for part in CUTS]
    table, windows, point, blocks, on_chip_ids = pl.pallas_call(
        functools.partial(sum_kernel, cuts=cuts, blk=blk),
        out_shape=[
            jax.ShapeDtypeStruct((slots, 8, AVG), BF16),
            jax.ShapeDtypeStruct((tiles // blk, ROWS, AVG), F32),
            jax.ShapeDtypeStruct((ROWS, points), F32),
            pltpu.SMEM(owner_blocks.shape, jnp.int32),
            jax.ShapeDtypeStruct((tiles, AVG), jnp.int32),
        ],
        in_specs=[hbm] * 4,
        out_specs=[vmem, vmem, vmem, smem, vmem],
        scratch_shapes=[
            pltpu.VMEM((4 * tiles, AVG), F32),
            pltpu.VMEM((9, points), F32),
            pltpu.VMEM((grains + AVG, AVG), F32),
            pltpu.SemaphoreType.DMA((3, len(cuts) - 1)),
            pltpu.SemaphoreType.DMA,
        ],
        compiler_params=params,
        cost_estimate=pl.CostEstimate(
            flops=64 * points * ROWS, bytes_accessed=4 * points * ROWS, transcendentals=0
        ),
        name="sums",
    )(*in_hbm)
    blocks = pltpu.with_memory_space_constraint(blocks, pltpu.SMEM)

    held = [table]
    for offset in range(1, groups):
        moves = [(g, int(target(g, offset, groups))) for g in range(groups)]
        held.append(lax.ppermute(table, "grp", moves))

    on_chip = (on_chip_ids, point, windows)
    count = tiles // blk

    def look_up(begin, end, earlier):
        share = (end - begin) * points // count
        return pl.pallas_call(
            functools.partial(fluctuation_kernel, begin=begin, end=end),
            out_shape=jax.ShapeDtypeStruct((COUNT, points), BF16),
            in_specs=[vmem] * 3 + [hbm] * len(earlier),
            out_specs=hbm,
            scratch_shapes=[pltpu.VMEM((COUNT, share), BF16), pltpu.SemaphoreType.DMA((end - begin,))],
            input_output_aliases={3: 0} if earlier else {},
            compiler_params=params,
            cost_estimate=pl.CostEstimate(
                flops=64 * share * ROWS, bytes_accessed=6 * share * ROWS, transcendentals=0
            ),
            name="fluctuation",
        )(*on_chip, *earlier)

    fluctuation = look_up(0, count // 2, [])
    held, fluctuation = lax.optimization_barrier((held, fluctuation))
    mine = pl.pallas_call(
        stack_kernel,
        out_shape=jax.ShapeDtypeStruct((groups, slots, 8, AVG), BF16),
        in_specs=[vmem] * groups,
        out_specs=vmem,
        compiler_params=params,
        name="stack",
    )(*held)
    other = lax.ppermute(mine, "slab", [(s, s ^ 1) for s in range(slabs)])
    sent = pl.pallas_call(
        route_kernel,
        out_shape=[jax.ShapeDtypeStruct((per_device + CORES, 8, AVG), BF16)] * chips,
        in_specs=[smem, vmem, vmem],
        out_specs=[vmem] * chips,
        scratch_shapes=[pltpu.VMEM((CORES, groups, slots, 8, AVG), BF16)],
        compiler_params=params,
        name="route",
    )(blocks, mine, other)
    sent, fluctuation = lax.optimization_barrier((sent, fluctuation))
    fluctuation = look_up(count // 2, count, [fluctuation])
    got = [sent[0]]
    for offset in reversed(range(1, chips)):
        moves = [
            (chip * CORES + core, int(target(chip, offset, chips)) * CORES + core)
            for chip in range(chips)
            for core in range(CORES)
        ]
        got.insert(1, lax.ppermute(sent[offset], "slab", moves))
    grain_table, fluctuation = pl.pallas_call(
        functools.partial(place_kernel, groups=groups, chips=chips, blk=blk),
        out_shape=[
            jax.ShapeDtypeStruct((COUNT, grains), F32),
            jax.ShapeDtypeStruct((COUNT, points), BF16),
        ],
        in_specs=[smem] + [vmem] * (chips + 3) + [hbm],
        out_specs=[hbm, hbm],
        scratch_shapes=[
            pltpu.VMEM((chips, per_device + CORES, 8, AVG), BF16),
            pltpu.VMEM((slabs, 8, AVG), F32),
            pltpu.VMEM((COUNT, 2 * EDGE * AVG), BF16),
            pltpu.VMEM((COUNT, grains), F32),
            pltpu.SemaphoreType.DMA((3,)),
        ],
        input_output_aliases={chips + 4: 1},
        compiler_params=params,
        name="place",
    )(blocks, *reversed(got), *on_chip, fluctuation)
    return (grain_table, fluctuation)


def solution(mesh):
    placed = (P(AXES), P(None, AXES), P(None, AXES), P())
    return jax.shard_map(
        local,
        mesh=mesh,
        in_specs=placed,
        out_specs=(P(None, AXES), P(None, AXES)),
        check_vma=False,
    )
```

```python
import functools

import jax
import jax.numpy as jnp
from jax import lax
from jax.experimental import pallas as pl
from jax.experimental.pallas import tpu as pltpu
from jax.sharding import PartitionSpec as P

AVG = 128
AXES = ("grp", "slab")
SUB = 8
WINDOW = 16
ROWS = 16
COUNT = 13
CORES = 2
CUTS = (0, 1, 2, 3, 4)
EDGE = 2
F32 = jnp.float32
BF16 = jnp.bfloat16


def window_sums(selector, values):
    high = values.astype(BF16)
    low = (values - high.astype(F32)).astype(BF16)
    both = jnp.concatenate([high, low], axis=0)
    return lax.dot_general(selector, both, (((1,), (1,)), ((), ())), preferred_element_type=F32)


def finish(total):
    row = lax.broadcasted_iota(jnp.int32, total.shape, 0)
    squares = jnp.sum(jnp.where(row < 4, total * total, 0.0), axis=0, keepdims=True)
    scale = jnp.where(row < 4, jnp.sqrt(squares), total[COUNT : COUNT + 1])
    return total / jnp.where(scale > 0.0, scale, 1.0)


def device_index():
    return lax.axis_index("grp") * lax.axis_size("slab") + lax.axis_index("slab")


def div_rem(x, n):
    if n & (n - 1) == 0:
        return x >> (n.bit_length() - 1), x & (n - 1)
    return lax.div(x, n), lax.rem(x, n)


def selection(ids_ref, first_tile, tiles, first_grain):
    grain_row = lax.broadcasted_iota(jnp.int32, (WINDOW, AVG), 0) + first_grain
    picks = []
    for tile in range(tiles):
        ids = jnp.broadcast_to(ids_ref[pl.ds(first_tile + tile, 1), :], (WINDOW, AVG))
        picks.append((ids == grain_row).astype(F32).astype(BF16))
    return jnp.concatenate(picks, axis=1)


def sum_kernel(
    ids_hbm, q_hbm, s_hbm, blocks_hbm, table_ref, window_ref, point_ref, blocks_ref, ids_ref, q_ref, s_ref, acc_ref,
    sems, blocks_sem, *, cuts, blk,
):
    grains = ids_hbm.shape[0]
    tile_base = device_index() * grains
    chunks = list(zip(cuts[:-1], cuts[1:]))

    def copies(chunk):
        begin, end = chunks[chunk]
        rows, quads = slice(begin, end), slice(4 * begin, 4 * end)
        lanes = slice(begin * AVG, end * AVG)
        return (
            pltpu.make_async_copy(ids_hbm.at[rows], ids_ref.at[rows], sems.at[0, chunk]),
            pltpu.make_async_copy(q_hbm.at[quads], q_ref.at[quads], sems.at[1, chunk]),
            pltpu.make_async_copy(s_hbm.at[:, lanes], s_ref.at[:, lanes], sems.at[2, chunk]),
        )

    for chunk in range(len(chunks)):
        for copy in copies(chunk):
            copy.start()
    blocks_copy = pltpu.make_async_copy(blocks_hbm, blocks_ref, blocks_sem)
    blocks_copy.start()

    quaternion = lax.broadcasted_iota(jnp.int32, (8, AVG), 0) < 4
    ones = jnp.ones((ROWS - COUNT, SUB * AVG), F32)

    carry = jnp.zeros((SUB, 2 * ROWS), F32)
    for chunk, (begin, end) in enumerate(chunks):
        for copy in copies(chunk):
            copy.wait()
        for tile in range(begin, end, SUB):
            lanes = slice(tile * AVG, (tile + SUB) * AVG)
            q = jnp.concatenate([q_ref[4 * t : 4 * t + 4, :] for t in range(tile, tile + SUB)], axis=1)
            values = jnp.concatenate([q, s_ref[:, lanes], ones], axis=0)
            sums = window_sums(selection(ids_ref, tile, SUB, tile_base + tile - 1), values)
            acc_ref[tile : tile + SUB, : 2 * ROWS] = carry + sums[:SUB]
            carry = sums[SUB:]
            parts = [q_ref[pl.ds(4 * tile + c, SUB, stride=4), :] for c in range(4)]
            scale = lax.rsqrt(sum(part * part for part in parts))
            scales = [
                jnp.where(quaternion, jnp.broadcast_to(scale[t : t + 1], (8, AVG)), 1.0) for t in range(SUB)
            ]
            point_ref[:8, lanes] = values[:8] * jnp.concatenate(scales, axis=1)
            point_ref[8:, lanes] = values[8:]
    blocks_copy.wait()
    acc_ref[grains : grains + SUB, : 2 * ROWS] = carry
    blocks = [acc_ref[block * AVG : (block + 1) * AVG, :].T for block in range(grains // AVG + 1)]
    part = jnp.concatenate([block[:ROWS] + block[ROWS : 2 * ROWS] for block in blocks], axis=1)
    rounded = finish(part).astype(BF16).astype(F32)
    for index in range(window_ref.shape[0]):
        window_ref[index] = rounded[:, index * blk : index * blk + AVG]
    own = rounded[:, 1 : 1 + grains]
    half = lax.broadcasted_iota(jnp.int32, (8, AVG), 1) < blk
    for pair in range(grains // AVG):
        top = own[:8, pair * AVG : (pair + 1) * AVG]
        low = own[8:, pair * AVG : (pair + 1) * AVG]
        table_ref[2 * pair] = jnp.where(half, top, pltpu.roll(low, blk, 1)).astype(BF16)
        table_ref[2 * pair + 1] = jnp.where(half, pltpu.roll(top, blk, 1), low).astype(BF16)
    lane = lax.broadcasted_iota(jnp.int32, (ROWS, AVG), 1)
    ends = jnp.where(lane < 2, part[:, :AVG], pltpu.roll(part[:, grains:], 2, 1))
    high = ends.astype(BF16).astype(F32)
    mid = (ends - high).astype(BF16).astype(F32)
    rest = ends - high - mid
    pieces = jnp.where(lane < 4, high, jnp.where(lane < 8, pltpu.roll(mid, 4, 1), pltpu.roll(rest, 8, 1)))
    pieces = jnp.where(lane < 12, pieces, 0.0)
    table_ref[grains // blk] = jnp.where(half, pieces[:8], pltpu.roll(pieces[8:], blk, 1)).astype(BF16)


def fluctuation_kernel(ids_ref, point_ref, window_ref, *refs, begin, end):
    *_, out_hbm, out_ref, sems = refs
    total = ids_ref.shape[0]
    tile_base = device_index() * total
    tiles = total // window_ref.shape[0]
    points = tiles * AVG

    def copy(window):
        here = slice((window - begin) * points, (window - begin + 1) * points)
        there = slice(window * points, (window + 1) * points)
        return pltpu.make_async_copy(out_ref.at[:, here], out_hbm.at[:, there], sems.at[window - begin])

    for window in range(begin, end):
        table = window_ref[window]
        for sub in range(tiles // SUB):
            tile = window * tiles + sub * SUB
            lanes = slice(tile * AVG, (tile + SUB) * AVG)
            near = pltpu.roll(table, (AVG - sub * SUB) % AVG, 1)[:, :WINDOW].astype(BF16)
            means = jnp.dot(near, selection(ids_ref, tile, SUB, tile_base + tile - 1), preferred_element_type=F32)
            here = slice((tile - begin * tiles) * AVG, (tile - begin * tiles + SUB) * AVG)
            out_ref[:, here] = (point_ref[:, lanes] - means)[:COUNT].astype(BF16)
        copy(window).start()
    for window in range(begin, end):
        copy(window).wait()


def source(me, offset, count):
    if count & (count - 1) == 0:
        return me ^ offset
    return (me + count - offset) % count


def target(me, offset, count):
    if count & (count - 1) == 0:
        return me ^ offset
    return (me + offset) % count


def pair_kernel(mine_ref, other_ref, out_ref):
    core = div_rem(lax.axis_index("slab"), CORES)[1]
    out_ref[core] = mine_ref[...]
    out_ref[1 - core] = other_ref[...]


def route_kernel(blocks_ref, *refs, groups):
    pair_refs, (*out_refs, held_ref) = refs[:groups], refs[groups:]
    chips = len(out_refs)
    per_device = held_ref.shape[2] - 1
    slabs = chips * CORES
    group = lax.axis_index("grp")
    chip, core = div_rem(lax.axis_index("slab"), CORES)
    for offset, ref in enumerate(pair_refs):
        held_ref[source(group, offset, groups)] = ref[...]
    step = AVG // 2 // groups
    lane = lax.broadcasted_iota(jnp.int32, (8, AVG), 1) & (AVG // 2 - 1)
    for owner_core in range(CORES):
        ends = held_ref[0, owner_core, per_device].astype(F32)
        for owner_group in range(1, groups):
            rolled = pltpu.roll(held_ref[owner_group, owner_core, per_device].astype(F32), owner_group * step, 1)
            ends = jnp.where(lane >= owner_group * step, rolled, ends)
        for out_ref in out_refs:
            out_ref[per_device + owner_core] = ends.astype(BF16)
    for offset, out_ref in enumerate(out_refs):
        wanted = (group * slabs + target(chip, offset, chips) * CORES + core) * per_device
        for slot in range(per_device):
            owner, index = div_rem(blocks_ref[wanted + slot], per_device)
            owner_group, owner_slab = div_rem(owner, slabs)
            out_ref[slot] = held_ref[owner_group, div_rem(owner_slab, CORES)[1], index]


def place_kernel(blocks_ref, *refs, groups, chips, blk):
    (*got_refs, ids_ref, point_ref, window_ref, _, table_hbm, fluctuation_hbm, held_ref, ends_ref,
     edge_ref, table_ref, sems) = refs
    slots = got_refs[0].shape[0]
    per_device = slots - CORES
    slabs = chips * CORES
    devices = groups * slabs
    grains = table_ref.shape[1]
    step = AVG // 2 // groups
    device = device_index()
    chip = div_rem(lax.axis_index("slab"), CORES)[0]
    lane = lax.broadcasted_iota(jnp.int32, (8, AVG), 1)
    half = lane < blk

    for offset, ref in enumerate(reversed(got_refs)):
        owner_chip = source(chip, offset, chips)
        held_ref[owner_chip] = ref[...]
        for core in range(CORES):
            piece = ref[per_device + core].astype(F32)
            piece = piece + pltpu.roll(piece, AVG - 4, 1) + pltpu.roll(piece, AVG - 8, 1)
            ends_ref[owner_chip * CORES + core] = piece

    def ends(owner, column, lane):
        group, slab = div_rem(jnp.clip(owner, 0, devices - 1), slabs)
        moved = pltpu.roll(ends_ref[slab], (lane - column - step * group + 2 * AVG) & (AVG - 1), 1)
        return jnp.where((owner >= 0) & (owner < devices), moved, 0.0)

    def unfold(value):
        return jnp.concatenate([value, pltpu.roll(value, blk, 1)], axis=0)

    lane_half = lane & (blk - 1)
    others = jnp.where(lane_half < 2, ends(device - 1, 2, 0), ends(device + 1, 0, 2))
    shared = finish(unfold(ends(device, 0, 0) + others))
    wide_lane = lax.broadcasted_iota(jnp.int32, (ROWS, AVG), 1)
    windows = window_ref.shape[0]
    first = jnp.where(wide_lane < 2, shared, window_ref[0])
    in_last = (wide_lane >= SUB) & (wide_lane < SUB + 2)
    last = pltpu.roll(window_ref[windows - 1], AVG - grains // windows + SUB, 1)
    last = jnp.where(in_last, pltpu.roll(shared, SUB - 2, 1), last)
    width = EDGE * AVG
    first_grain = device * grains - 1
    copies = []
    for end, (table, tile, grain) in enumerate(
        ((first, 0, first_grain), (last, grains - EDGE, first_grain + grains - SUB))
    ):
        lanes = slice(end * width, (end + 1) * width)
        points = slice(tile * AVG, tile * AVG + width)
        picks = selection(ids_ref, tile, EDGE, grain)
        means = jnp.dot(table[:, :WINDOW].astype(BF16), picks, preferred_element_type=F32)
        edge_ref[:, lanes] = (point_ref[:, points] - means)[:COUNT].astype(BF16)
        copies.append(
            pltpu.make_async_copy(
                edge_ref.at[:, lanes], fluctuation_hbm.at[:, points], sems.at[end]
            )
        )

    tiles, columns = [], []
    sums = jnp.zeros((8, AVG), F32)
    for slot in range(per_device):
        owner, index = div_rem(blocks_ref[device * per_device + slot], per_device)
        owner_chip = div_rem(div_rem(owner, slabs)[1], CORES)[0]
        tiles.append(held_ref[owner_chip, slot].astype(F32))
        low = index == 0
        beside = jnp.where(low, owner - 1, owner + 1)
        both = ends(owner, jnp.where(low, 1, 2), slot) + ends(beside, jnp.where(low, 3, 0), slot)
        sums = jnp.where(lane_half == slot, both, sums)
        columns.append(jnp.where(low, 0, jnp.where(index == per_device - 1, blk - 1, 2 * AVG)))
    repaired = finish(unfold(sums))
    repaired = jnp.where(half, repaired[:8], pltpu.roll(repaired[8:], blk, 1))
    for slot in range(per_device):
        moved = pltpu.roll(repaired, (columns[slot] - slot + AVG) & (AVG - 1), 1)
        tiles[slot] = jnp.where(lane_half == columns[slot], moved, tiles[slot])
    for pair in range(per_device // 2):
        first, second = tiles[2 * pair], tiles[2 * pair + 1]
        lanes = slice(pair * AVG, (pair + 1) * AVG)
        table_ref[:8, lanes] = jnp.where(half, first, pltpu.roll(second, blk, 1))
        table_ref[8:, lanes] = jnp.where(half, pltpu.roll(first, blk, 1), second)[: COUNT - 8]
    copies.insert(0, pltpu.make_async_copy(table_ref, table_hbm, sems.at[2]))
    for copy in copies:
        copy.start()
    for copy in copies:
        copy.wait()


def local(grain_ids, orientation, stress, owner_blocks):
    groups, slabs = lax.axis_size("grp"), lax.axis_size("slab")
    points = grain_ids.shape[0]
    tiles = points // AVG
    grains = tiles
    per_device = owner_blocks.shape[0] // (groups * slabs)
    blk = grains // per_device
    slots = per_device + 1
    chips = slabs // CORES

    ids = grain_ids.reshape(tiles, AVG)
    quads = orientation.reshape(4, tiles, AVG).transpose(1, 0, 2).reshape(4 * tiles, AVG)
    in_hbm = [pltpu.with_memory_space_constraint(x, pltpu.HBM) for x in (ids, quads, stress, owner_blocks)]
    smem = pl.BlockSpec(memory_space=pltpu.SMEM)
    vmem = pl.BlockSpec(memory_space=pltpu.VMEM)
    hbm = pl.BlockSpec(memory_space=pltpu.HBM)
    params = pltpu.CompilerParams(vmem_limit_bytes=20 << 20)

    cuts = [tiles * part // CUTS[-1] for part in CUTS]
    table, windows, point, blocks, on_chip_ids = pl.pallas_call(
        functools.partial(sum_kernel, cuts=cuts, blk=blk),
        out_shape=[
            jax.ShapeDtypeStruct((slots, 8, AVG), BF16),
            jax.ShapeDtypeStruct((tiles // blk, ROWS, AVG), F32),
            jax.ShapeDtypeStruct((ROWS, points), F32),
            pltpu.SMEM(owner_blocks.shape, jnp.int32),
            jax.ShapeDtypeStruct((tiles, AVG), jnp.int32),
        ],
        in_specs=[hbm] * 4,
        out_specs=[vmem, vmem, vmem, smem, vmem],
        scratch_shapes=[
            pltpu.VMEM((4 * tiles, AVG), F32),
            pltpu.VMEM((9, points), F32),
            pltpu.VMEM((grains + AVG, AVG), F32),
            pltpu.SemaphoreType.DMA((3, len(cuts) - 1)),
            pltpu.SemaphoreType.DMA,
        ],
        compiler_params=params,
        cost_estimate=pl.CostEstimate(
            flops=64 * points * ROWS, bytes_accessed=4 * points * ROWS, transcendentals=0
        ),
        name="sums",
    )(*in_hbm)
    blocks = pltpu.with_memory_space_constraint(blocks, pltpu.SMEM)

    other = lax.ppermute(table, "slab", [(s, s ^ 1) for s in range(slabs)])
    pair = pl.pallas_call(
        pair_kernel,
        out_shape=jax.ShapeDtypeStruct((CORES, slots, 8, AVG), BF16),
        in_specs=[vmem, vmem],
        out_specs=vmem,
        compiler_params=params,
        name="pair",
    )(table, other)
    held = [pair]
    for offset in range(1, groups):
        moves = [(g, int(target(g, offset, groups))) for g in range(groups)]
        held.append(lax.ppermute(pair, "grp", moves))

    on_chip = (on_chip_ids, point, windows)
    count = tiles // blk

    def look_up(begin, end, earlier):
        share = (end - begin) * points // count
        return pl.pallas_call(
            functools.partial(fluctuation_kernel, begin=begin, end=end),
            out_shape=jax.ShapeDtypeStruct((COUNT, points), BF16),
            in_specs=[vmem] * 3 + [hbm] * len(earlier),
            out_specs=hbm,
            scratch_shapes=[pltpu.VMEM((COUNT, share), BF16), pltpu.SemaphoreType.DMA((end - begin,))],
            input_output_aliases={3: 0} if earlier else {},
            compiler_params=params,
            cost_estimate=pl.CostEstimate(
                flops=64 * share * ROWS, bytes_accessed=6 * share * ROWS, transcendentals=0
            ),
            name="fluctuation",
        )(*on_chip, *earlier)

    fluctuation = look_up(0, count // 2, [])
    held, fluctuation = lax.optimization_barrier((held, fluctuation))
    sent = pl.pallas_call(
        functools.partial(route_kernel, groups=groups),
        out_shape=[jax.ShapeDtypeStruct((per_device + CORES, 8, AVG), BF16)] * chips,
        in_specs=[smem] + [vmem] * groups,
        out_specs=[vmem] * chips,
        scratch_shapes=[pltpu.VMEM((groups, CORES, slots, 8, AVG), BF16)],
        compiler_params=params,
        name="route",
    )(blocks, *held)
    sent, fluctuation = lax.optimization_barrier((sent, fluctuation))
    fluctuation = look_up(count // 2, count, [fluctuation])
    got = [sent[0]]
    for offset in reversed(range(1, chips)):
        moves = [
            (chip * CORES + core, int(target(chip, offset, chips)) * CORES + core)
            for chip in range(chips)
            for core in range(CORES)
        ]
        got.insert(1, lax.ppermute(sent[offset], "slab", moves))
    grain_table, fluctuation = pl.pallas_call(
        functools.partial(place_kernel, groups=groups, chips=chips, blk=blk),
        out_shape=[
            jax.ShapeDtypeStruct((COUNT, grains), F32),
            jax.ShapeDtypeStruct((COUNT, points), BF16),
        ],
        in_specs=[smem] + [vmem] * (chips + 3) + [hbm],
        out_specs=[hbm, hbm],
        scratch_shapes=[
            pltpu.VMEM((chips, per_device + CORES, 8, AVG), BF16),
            pltpu.VMEM((slabs, 8, AVG), F32),
            pltpu.VMEM((COUNT, 2 * EDGE * AVG), BF16),
            pltpu.VMEM((COUNT, grains), F32),
            pltpu.SemaphoreType.DMA((3,)),
        ],
        input_output_aliases={chips + 4: 1},
        compiler_params=params,
        name="place",
    )(blocks, *reversed(got), *on_chip, fluctuation)
    return (grain_table, fluctuation)


def solution(mesh):
    placed = (P(AXES), P(None, AXES), P(None, AXES), P())
    return jax.shard_map(
        local,
        mesh=mesh,
        in_specs=placed,
        out_specs=(P(None, AXES), P(None, AXES)),
        check_vma=False,
    )
```

```python
import functools

import jax
import jax.numpy as jnp
from jax import lax
from jax.experimental import pallas as pl
from jax.experimental.pallas import tpu as pltpu
from jax.sharding import PartitionSpec as P

AVG = 128
AXES = ("grp", "slab")
SUB = 8
WINDOW = 16
ROWS = 16
COUNT = 13
CORES = 2
CUTS = (0, 1, 2, 3, 4)
EDGE = 2
F32 = jnp.float32
BF16 = jnp.bfloat16


def window_sums(selector, values):
    high = values.astype(BF16)
    low = (values - high.astype(F32)).astype(BF16)
    both = jnp.concatenate([high, low], axis=0)
    return lax.dot_general(selector, both, (((1,), (1,)), ((), ())), preferred_element_type=F32)


def finish(total):
    row = lax.broadcasted_iota(jnp.int32, total.shape, 0)
    squares = jnp.sum(jnp.where(row < 4, total * total, 0.0), axis=0, keepdims=True)
    scale = jnp.where(row < 4, jnp.sqrt(squares), total[COUNT : COUNT + 1])
    return total / jnp.where(scale > 0.0, scale, 1.0)


def device_index():
    return lax.axis_index("grp") * lax.axis_size("slab") + lax.axis_index("slab")


def div_rem(x, n):
    if n & (n - 1) == 0:
        return x >> (n.bit_length() - 1), x & (n - 1)
    return lax.div(x, n), lax.rem(x, n)


def selection(ids_ref, first_tile, tiles, first_grain):
    grain_row = lax.broadcasted_iota(jnp.int32, (WINDOW, AVG), 0) + first_grain
    picks = []
    for tile in range(tiles):
        ids = jnp.broadcast_to(ids_ref[pl.ds(first_tile + tile, 1), :], (WINDOW, AVG))
        picks.append((ids == grain_row).astype(F32).astype(BF16))
    return jnp.concatenate(picks, axis=1)


def sum_kernel(
    ids_hbm, q_hbm, s_hbm, blocks_hbm, table_ref, window_ref, point_ref, blocks_ref, ids_ref, q_ref, s_ref, acc_ref,
    sems, blocks_sem, *, cuts, blk,
):
    grains = ids_hbm.shape[0]
    tile_base = device_index() * grains
    chunks = list(zip(cuts[:-1], cuts[1:]))

    def copies(chunk):
        begin, end = chunks[chunk]
        rows, quads = slice(begin, end), slice(4 * begin, 4 * end)
        lanes = slice(begin * AVG, end * AVG)
        return (
            pltpu.make_async_copy(ids_hbm.at[rows], ids_ref.at[rows], sems.at[0, chunk]),
            pltpu.make_async_copy(q_hbm.at[quads], q_ref.at[quads], sems.at[1, chunk]),
            pltpu.make_async_copy(s_hbm.at[:, lanes], s_ref.at[:, lanes], sems.at[2, chunk]),
        )

    for chunk in range(len(chunks)):
        for copy in copies(chunk):
            copy.start()
    blocks_copy = pltpu.make_async_copy(blocks_hbm, blocks_ref, blocks_sem)
    blocks_copy.start()

    quaternion = lax.broadcasted_iota(jnp.int32, (8, AVG), 0) < 4
    ones = jnp.ones((ROWS - COUNT, SUB * AVG), F32)

    carry = jnp.zeros((SUB, 2 * ROWS), F32)
    for chunk, (begin, end) in enumerate(chunks):
        for copy in copies(chunk):
            copy.wait()
        for tile in range(begin, end, SUB):
            lanes = slice(tile * AVG, (tile + SUB) * AVG)
            q = jnp.concatenate([q_ref[4 * t : 4 * t + 4, :] for t in range(tile, tile + SUB)], axis=1)
            values = jnp.concatenate([q, s_ref[:, lanes], ones], axis=0)
            sums = window_sums(selection(ids_ref, tile, SUB, tile_base + tile - 1), values)
            acc_ref[tile : tile + SUB, : 2 * ROWS] = carry + sums[:SUB]
            carry = sums[SUB:]
            parts = [q_ref[pl.ds(4 * tile + c, SUB, stride=4), :] for c in range(4)]
            scale = lax.rsqrt(sum(part * part for part in parts))
            scales = [
                jnp.where(quaternion, jnp.broadcast_to(scale[t : t + 1], (8, AVG)), 1.0) for t in range(SUB)
            ]
            point_ref[:8, lanes] = values[:8] * jnp.concatenate(scales, axis=1)
            point_ref[8:, lanes] = values[8:]
    blocks_copy.wait()
    acc_ref[grains : grains + SUB, : 2 * ROWS] = carry
    blocks = [acc_ref[block * AVG : (block + 1) * AVG, :].T for block in range(grains // AVG + 1)]
    part = jnp.concatenate([block[:ROWS] + block[ROWS : 2 * ROWS] for block in blocks], axis=1)
    rounded = finish(part).astype(BF16).astype(F32)
    for index in range(window_ref.shape[0]):
        window_ref[index] = rounded[:, index * blk : index * blk + AVG]
    own = rounded[:, 1 : 1 + grains]
    half = lax.broadcasted_iota(jnp.int32, (8, AVG), 1) < blk
    for pair in range(grains // AVG):
        top = own[:8, pair * AVG : (pair + 1) * AVG]
        low = own[8:, pair * AVG : (pair + 1) * AVG]
        table_ref[2 * pair] = jnp.where(half, top, pltpu.roll(low, blk, 1)).astype(BF16)
        table_ref[2 * pair + 1] = jnp.where(half, pltpu.roll(top, blk, 1), low).astype(BF16)
    lane = lax.broadcasted_iota(jnp.int32, (ROWS, AVG), 1)
    ends = jnp.where(lane < 2, part[:, :AVG], pltpu.roll(part[:, grains:], 2, 1))
    high = ends.astype(BF16).astype(F32)
    mid = (ends - high).astype(BF16).astype(F32)
    rest = ends - high - mid
    pieces = jnp.where(lane < 4, high, jnp.where(lane < 8, pltpu.roll(mid, 4, 1), pltpu.roll(rest, 8, 1)))
    pieces = jnp.where(lane < 12, pieces, 0.0)
    table_ref[grains // blk] = jnp.where(half, pieces[:8], pltpu.roll(pieces[8:], blk, 1)).astype(BF16)


def fluctuation_kernel(ids_ref, point_ref, window_ref, *refs, begin, end):
    *_, out_hbm, out_ref, sems = refs
    total = ids_ref.shape[0]
    tile_base = device_index() * total
    tiles = total // window_ref.shape[0]
    points = tiles * AVG

    def copy(window):
        here = slice((window - begin) * points, (window - begin + 1) * points)
        there = slice(window * points, (window + 1) * points)
        return pltpu.make_async_copy(out_ref.at[:, here], out_hbm.at[:, there], sems.at[window - begin])

    for window in range(begin, end):
        table = window_ref[window]
        for sub in range(tiles // SUB):
            tile = window * tiles + sub * SUB
            lanes = slice(tile * AVG, (tile + SUB) * AVG)
            near = pltpu.roll(table, (AVG - sub * SUB) % AVG, 1)[:, :WINDOW].astype(BF16)
            means = jnp.dot(near, selection(ids_ref, tile, SUB, tile_base + tile - 1), preferred_element_type=F32)
            here = slice((tile - begin * tiles) * AVG, (tile - begin * tiles + SUB) * AVG)
            out_ref[:, here] = (point_ref[:, lanes] - means)[:COUNT].astype(BF16)
        copy(window).start()
    for window in range(begin, end):
        copy(window).wait()


def source(me, offset, count):
    if count & (count - 1) == 0:
        return me ^ offset
    return (me + count - offset) % count


def target(me, offset, count):
    if count & (count - 1) == 0:
        return me ^ offset
    return (me + offset) % count


def pair_kernel(mine_ref, other_ref, out_ref):
    core = div_rem(lax.axis_index("slab"), CORES)[1]
    out_ref[core] = mine_ref[...]
    out_ref[1 - core] = other_ref[...]


def route_kernel(blocks_ref, *refs, groups):
    pair_refs, (*out_refs, held_ref) = refs[:groups], refs[groups:]
    chips = len(out_refs)
    per_device = held_ref.shape[2] - 1
    slabs = chips * CORES
    group = lax.axis_index("grp")
    chip, core = div_rem(lax.axis_index("slab"), CORES)
    for offset, ref in enumerate(pair_refs):
        held_ref[source(group, offset, groups)] = ref[...]
    step = AVG // 2 // groups
    lane = lax.broadcasted_iota(jnp.int32, (8, AVG), 1) & (AVG // 2 - 1)
    for owner_core in range(CORES):
        ends = held_ref[0, owner_core, per_device].astype(F32)
        for owner_group in range(1, groups):
            rolled = pltpu.roll(held_ref[owner_group, owner_core, per_device].astype(F32), owner_group * step, 1)
            ends = jnp.where(lane >= owner_group * step, rolled, ends)
        for out_ref in out_refs:
            out_ref[per_device + owner_core] = ends.astype(BF16)
    for offset, out_ref in enumerate(out_refs):
        wanted = (group * slabs + target(chip, offset, chips) * CORES + core) * per_device
        for slot in range(per_device):
            owner, index = div_rem(blocks_ref[wanted + slot], per_device)
            owner_group, owner_slab = div_rem(owner, slabs)
            out_ref[slot] = held_ref[owner_group, div_rem(owner_slab, CORES)[1], index]


def place_kernel(blocks_ref, *refs, groups, chips, blk):
    (*got_refs, ids_ref, point_ref, window_ref, _, table_hbm, fluctuation_hbm, held_ref, ends_ref,
     edge_ref, table_ref, sems) = refs
    slots = got_refs[0].shape[0]
    per_device = slots - CORES
    slabs = chips * CORES
    devices = groups * slabs
    grains = table_ref.shape[1]
    step = AVG // 2 // groups
    device = device_index()
    chip = div_rem(lax.axis_index("slab"), CORES)[0]
    lane = lax.broadcasted_iota(jnp.int32, (8, AVG), 1)
    half = lane < blk

    for offset, ref in enumerate(reversed(got_refs)):
        owner_chip = source(chip, offset, chips)
        held_ref[owner_chip] = ref[...]
        for core in range(CORES):
            piece = ref[per_device + core].astype(F32)
            piece = piece + pltpu.roll(piece, AVG - 4, 1) + pltpu.roll(piece, AVG - 8, 1)
            ends_ref[owner_chip * CORES + core] = piece

    def ends(owner, column, lane):
        group, slab = div_rem(jnp.clip(owner, 0, devices - 1), slabs)
        moved = pltpu.roll(ends_ref[slab], (lane - column - step * group + 2 * AVG) & (AVG - 1), 1)
        return jnp.where((owner >= 0) & (owner < devices), moved, 0.0)

    def unfold(value):
        return jnp.concatenate([value, pltpu.roll(value, blk, 1)], axis=0)

    lane_half = lane & (blk - 1)
    others = jnp.where(lane_half < 2, ends(device - 1, 2, 0), ends(device + 1, 0, 2))
    shared = finish(unfold(ends(device, 0, 0) + others))
    wide_lane = lax.broadcasted_iota(jnp.int32, (ROWS, AVG), 1)
    windows = window_ref.shape[0]
    first = jnp.where(wide_lane < 2, shared, window_ref[0])
    in_last = (wide_lane >= SUB) & (wide_lane < SUB + 2)
    last = pltpu.roll(window_ref[windows - 1], AVG - grains // windows + SUB, 1)
    last = jnp.where(in_last, pltpu.roll(shared, SUB - 2, 1), last)
    width = EDGE * AVG
    first_grain = device * grains - 1
    copies = []
    for end, (table, tile, grain) in enumerate(
        ((first, 0, first_grain), (last, grains - EDGE, first_grain + grains - SUB))
    ):
        lanes = slice(end * width, (end + 1) * width)
        points = slice(tile * AVG, tile * AVG + width)
        picks = selection(ids_ref, tile, EDGE, grain)
        means = jnp.dot(table[:, :WINDOW].astype(BF16), picks, preferred_element_type=F32)
        edge_ref[:, lanes] = (point_ref[:, points] - means)[:COUNT].astype(BF16)
        copies.append(
            pltpu.make_async_copy(
                edge_ref.at[:, lanes], fluctuation_hbm.at[:, points], sems.at[end]
            )
        )

    tiles, columns = [], []
    sums = jnp.zeros((8, AVG), F32)
    for slot in range(per_device):
        owner, index = div_rem(blocks_ref[device * per_device + slot], per_device)
        owner_chip = div_rem(div_rem(owner, slabs)[1], CORES)[0]
        tiles.append(held_ref[owner_chip, slot].astype(F32))
        low = index == 0
        beside = jnp.where(low, owner - 1, owner + 1)
        both = ends(owner, jnp.where(low, 1, 2), slot) + ends(beside, jnp.where(low, 3, 0), slot)
        sums = jnp.where(lane_half == slot, both, sums)
        columns.append(jnp.where(low, 0, jnp.where(index == per_device - 1, blk - 1, 2 * AVG)))
    repaired = finish(unfold(sums))
    repaired = jnp.where(half, repaired[:8], pltpu.roll(repaired[8:], blk, 1))
    for slot in range(per_device):
        moved = pltpu.roll(repaired, (columns[slot] - slot + AVG) & (AVG - 1), 1)
        tiles[slot] = jnp.where(lane_half == columns[slot], moved, tiles[slot])
    for pair in range(per_device // 2):
        first, second = tiles[2 * pair], tiles[2 * pair + 1]
        lanes = slice(pair * AVG, (pair + 1) * AVG)
        table_ref[:8, lanes] = jnp.where(half, first, pltpu.roll(second, blk, 1))
        table_ref[8:, lanes] = jnp.where(half, pltpu.roll(first, blk, 1), second)[: COUNT - 8]
    copies.insert(0, pltpu.make_async_copy(table_ref, table_hbm, sems.at[2]))
    for copy in copies:
        copy.start()
    for copy in copies:
        copy.wait()


def local(grain_ids, orientation, stress, owner_blocks):
    groups, slabs = lax.axis_size("grp"), lax.axis_size("slab")
    points = grain_ids.shape[0]
    tiles = points // AVG
    grains = tiles
    per_device = owner_blocks.shape[0] // (groups * slabs)
    blk = grains // per_device
    slots = per_device + 1
    chips = slabs // CORES

    ids = grain_ids.reshape(tiles, AVG)
    quads = orientation.reshape(4, tiles, AVG).transpose(1, 0, 2).reshape(4 * tiles, AVG)
    in_hbm = [pltpu.with_memory_space_constraint(x, pltpu.HBM) for x in (ids, quads, stress, owner_blocks)]
    smem = pl.BlockSpec(memory_space=pltpu.SMEM)
    vmem = pl.BlockSpec(memory_space=pltpu.VMEM)
    hbm = pl.BlockSpec(memory_space=pltpu.HBM)
    params = pltpu.CompilerParams(vmem_limit_bytes=20 << 20)

    cuts = [tiles * part // CUTS[-1] for part in CUTS]
    table, windows, point, blocks, on_chip_ids = pl.pallas_call(
        functools.partial(sum_kernel, cuts=cuts, blk=blk),
        out_shape=[
            jax.ShapeDtypeStruct((slots, 8, AVG), BF16),
            jax.ShapeDtypeStruct((tiles // blk, ROWS, AVG), F32),
            jax.ShapeDtypeStruct((ROWS, points), F32),
            pltpu.SMEM(owner_blocks.shape, jnp.int32),
            jax.ShapeDtypeStruct((tiles, AVG), jnp.int32),
        ],
        in_specs=[hbm] * 4,
        out_specs=[vmem, vmem, vmem, smem, vmem],
        scratch_shapes=[
            pltpu.VMEM((4 * tiles, AVG), F32),
            pltpu.VMEM((9, points), F32),
            pltpu.VMEM((grains + AVG, AVG), F32),
            pltpu.SemaphoreType.DMA((3, len(cuts) - 1)),
            pltpu.SemaphoreType.DMA,
        ],
        compiler_params=params,
        cost_estimate=pl.CostEstimate(
            flops=64 * points * ROWS, bytes_accessed=4 * points * ROWS, transcendentals=0
        ),
        name="sums",
    )(*in_hbm)
    blocks = pltpu.with_memory_space_constraint(blocks, pltpu.SMEM)

    other = lax.ppermute(table, "slab", [(s, s ^ 1) for s in range(slabs)])
    pair = pl.pallas_call(
        pair_kernel,
        out_shape=jax.ShapeDtypeStruct((CORES, slots, 8, AVG), BF16),
        in_specs=[vmem, vmem],
        out_specs=vmem,
        compiler_params=params,
        name="pair",
    )(table, other)
    held = [pair]
    for offset in range(1, groups):
        moves = [(g, int(target(g, offset, groups))) for g in range(groups)]
        held.append(lax.ppermute(pair, "grp", moves))

    on_chip = (on_chip_ids, point, windows)
    count = tiles // blk

    def look_up(begin, end, on_chip):
        share = (end - begin) * points // count
        return pl.pallas_call(
            functools.partial(fluctuation_kernel, begin=begin, end=end),
            out_shape=jax.ShapeDtypeStruct((COUNT, points), BF16),
            in_specs=[vmem] * 3,
            out_specs=hbm,
            scratch_shapes=[pltpu.VMEM((COUNT, share), BF16), pltpu.SemaphoreType.DMA((end - begin,))],
            compiler_params=params,
            cost_estimate=pl.CostEstimate(
                flops=64 * share * ROWS, bytes_accessed=6 * share * ROWS, transcendentals=0
            ),
            name="fluctuation",
        )(*on_chip)

    sent = pl.pallas_call(
        functools.partial(route_kernel, groups=groups),
        out_shape=[jax.ShapeDtypeStruct((per_device + CORES, 8, AVG), BF16)] * chips,
        in_specs=[smem] + [vmem] * groups,
        out_specs=[vmem] * chips,
        scratch_shapes=[pltpu.VMEM((groups, CORES, slots, 8, AVG), BF16)],
        compiler_params=params,
        name="route",
    )(blocks, *held)
    on_chip, sent = lax.optimization_barrier((on_chip, sent))
    fluctuation = look_up(0, count, on_chip)
    got = [sent[0]]
    for offset in reversed(range(1, chips)):
        moves = [
            (chip * CORES + core, int(target(chip, offset, chips)) * CORES + core)
            for chip in range(chips)
            for core in range(CORES)
        ]
        got.insert(1, lax.ppermute(sent[offset], "slab", moves))
    grain_table, fluctuation = pl.pallas_call(
        functools.partial(place_kernel, groups=groups, chips=chips, blk=blk),
        out_shape=[
            jax.ShapeDtypeStruct((COUNT, grains), F32),
            jax.ShapeDtypeStruct((COUNT, points), BF16),
        ],
        in_specs=[smem] + [vmem] * (chips + 3) + [hbm],
        out_specs=[hbm, hbm],
        scratch_shapes=[
            pltpu.VMEM((chips, per_device + CORES, 8, AVG), BF16),
            pltpu.VMEM((slabs, 8, AVG), F32),
            pltpu.VMEM((COUNT, 2 * EDGE * AVG), BF16),
            pltpu.VMEM((COUNT, grains), F32),
            pltpu.SemaphoreType.DMA((3,)),
        ],
        input_output_aliases={chips + 4: 1},
        compiler_params=params,
        name="place",
    )(blocks, *reversed(got), *on_chip, fluctuation)
    return (grain_table, fluctuation)


def solution(mesh):
    placed = (P(AXES), P(None, AXES), P(None, AXES), P())
    return jax.shard_map(
        local,
        mesh=mesh,
        in_specs=placed,
        out_specs=(P(None, AXES), P(None, AXES)),
        check_vma=False,
    )
```

```python
import functools

import jax
import jax.numpy as jnp
from jax import lax
from jax.experimental import pallas as pl
from jax.experimental.pallas import tpu as pltpu
from jax.sharding import PartitionSpec as P

AVG = 128
AXES = ("grp", "slab")
SUB = 8
WINDOW = 16
ROWS = 16
COUNT = 13
CORES = 2
CUTS = (0, 1, 2, 3, 4)
EDGE = 2
F32 = jnp.float32
BF16 = jnp.bfloat16


def window_sums(selector, values):
    high = values.astype(BF16)
    low = (values - high.astype(F32)).astype(BF16)
    both = jnp.concatenate([high, low], axis=0)
    return lax.dot_general(selector, both, (((1,), (1,)), ((), ())), preferred_element_type=F32)


def finish(total):
    row = lax.broadcasted_iota(jnp.int32, total.shape, 0)
    squares = jnp.sum(jnp.where(row < 4, total * total, 0.0), axis=0, keepdims=True)
    scale = jnp.where(row < 4, jnp.sqrt(squares), total[COUNT : COUNT + 1])
    return total / jnp.where(scale > 0.0, scale, 1.0)


def device_index():
    return lax.axis_index("grp") * lax.axis_size("slab") + lax.axis_index("slab")


def div_rem(x, n):
    if n & (n - 1) == 0:
        return x >> (n.bit_length() - 1), x & (n - 1)
    return lax.div(x, n), lax.rem(x, n)


def selection(ids_ref, first_tile, tiles, first_grain):
    grain_row = lax.broadcasted_iota(jnp.int32, (WINDOW, AVG), 0) + first_grain
    picks = []
    for tile in range(tiles):
        ids = jnp.broadcast_to(ids_ref[pl.ds(first_tile + tile, 1), :], (WINDOW, AVG))
        picks.append((ids == grain_row).astype(F32).astype(BF16))
    return jnp.concatenate(picks, axis=1)


def sum_kernel(
    ids_hbm, q_hbm, s_hbm, blocks_hbm, table_ref, window_ref, point_ref, blocks_ref, ids_ref, q_ref, s_ref, acc_ref,
    sems, blocks_sem, *, cuts, blk,
):
    grains = ids_hbm.shape[0]
    tile_base = device_index() * grains
    chunks = list(zip(cuts[:-1], cuts[1:]))

    def copies(chunk):
        begin, end = chunks[chunk]
        rows, quads = slice(begin, end), slice(4 * begin, 4 * end)
        lanes = slice(begin * AVG, end * AVG)
        return (
            pltpu.make_async_copy(ids_hbm.at[rows], ids_ref.at[rows], sems.at[0, chunk]),
            pltpu.make_async_copy(q_hbm.at[quads], q_ref.at[quads], sems.at[1, chunk]),
            pltpu.make_async_copy(s_hbm.at[:, lanes], s_ref.at[:, lanes], sems.at[2, chunk]),
        )

    for chunk in range(len(chunks)):
        for copy in copies(chunk):
            copy.start()
    blocks_copy = pltpu.make_async_copy(blocks_hbm, blocks_ref, blocks_sem)
    blocks_copy.start()

    quaternion = lax.broadcasted_iota(jnp.int32, (8, AVG), 0) < 4
    ones = jnp.ones((ROWS - COUNT, SUB * AVG), F32)

    carry = jnp.zeros((SUB, 2 * ROWS), F32)
    for chunk, (begin, end) in enumerate(chunks):
        for copy in copies(chunk):
            copy.wait()
        for tile in range(begin, end, SUB):
            lanes = slice(tile * AVG, (tile + SUB) * AVG)
            q = jnp.concatenate([q_ref[4 * t : 4 * t + 4, :] for t in range(tile, tile + SUB)], axis=1)
            values = jnp.concatenate([q, s_ref[:, lanes], ones], axis=0)
            sums = window_sums(selection(ids_ref, tile, SUB, tile_base + tile - 1), values)
            acc_ref[tile : tile + SUB, : 2 * ROWS] = carry + sums[:SUB]
            carry = sums[SUB:]
            parts = [q_ref[pl.ds(4 * tile + c, SUB, stride=4), :] for c in range(4)]
            scale = lax.rsqrt(sum(part * part for part in parts))
            scales = [
                jnp.where(quaternion, jnp.broadcast_to(scale[t : t + 1], (8, AVG)), 1.0) for t in range(SUB)
            ]
            point_ref[:8, lanes] = values[:8] * jnp.concatenate(scales, axis=1)
            point_ref[8:, lanes] = values[8:]
    blocks_copy.wait()
    acc_ref[grains : grains + SUB, : 2 * ROWS] = carry
    blocks = [acc_ref[block * AVG : (block + 1) * AVG, :].T for block in range(grains // AVG + 1)]
    part = jnp.concatenate([block[:ROWS] + block[ROWS : 2 * ROWS] for block in blocks], axis=1)
    rounded = finish(part).astype(BF16).astype(F32)
    for index in range(window_ref.shape[0]):
        window_ref[index] = rounded[:, index * blk : index * blk + AVG]
    own = rounded[:, 1 : 1 + grains]
    half = lax.broadcasted_iota(jnp.int32, (8, AVG), 1) < blk
    for pair in range(grains // AVG):
        top = own[:8, pair * AVG : (pair + 1) * AVG]
        low = own[8:, pair * AVG : (pair + 1) * AVG]
        table_ref[2 * pair] = jnp.where(half, top, pltpu.roll(low, blk, 1)).astype(BF16)
        table_ref[2 * pair + 1] = jnp.where(half, pltpu.roll(top, blk, 1), low).astype(BF16)
    lane = lax.broadcasted_iota(jnp.int32, (ROWS, AVG), 1)
    ends = jnp.where(lane < 2, part[:, :AVG], pltpu.roll(part[:, grains:], 2, 1))
    high = ends.astype(BF16).astype(F32)
    mid = (ends - high).astype(BF16).astype(F32)
    rest = ends - high - mid
    pieces = jnp.where(lane < 4, high, jnp.where(lane < 8, pltpu.roll(mid, 4, 1), pltpu.roll(rest, 8, 1)))
    pieces = jnp.where(lane < 12, pieces, 0.0)
    table_ref[grains // blk] = jnp.where(half, pieces[:8], pltpu.roll(pieces[8:], blk, 1)).astype(BF16)


def fluctuation_kernel(ids_ref, point_ref, window_ref, *refs, begin, end):
    *_, out_hbm, out_ref, sems = refs
    total = ids_ref.shape[0]
    tile_base = device_index() * total
    tiles = total // window_ref.shape[0]
    points = tiles * AVG

    def copy(window):
        here = slice((window - begin) * points, (window - begin + 1) * points)
        there = slice(window * points, (window + 1) * points)
        return pltpu.make_async_copy(out_ref.at[:, here], out_hbm.at[:, there], sems.at[window - begin])

    for window in range(begin, end):
        table = window_ref[window]
        for sub in range(tiles // SUB):
            tile = window * tiles + sub * SUB
            lanes = slice(tile * AVG, (tile + SUB) * AVG)
            near = pltpu.roll(table, (AVG - sub * SUB) % AVG, 1)[:, :WINDOW].astype(BF16)
            means = jnp.dot(near, selection(ids_ref, tile, SUB, tile_base + tile - 1), preferred_element_type=F32)
            here = slice((tile - begin * tiles) * AVG, (tile - begin * tiles + SUB) * AVG)
            out_ref[:, here] = (point_ref[:, lanes] - means)[:COUNT].astype(BF16)
        copy(window).start()
    for window in range(begin, end):
        copy(window).wait()


def source(me, offset, count):
    if count & (count - 1) == 0:
        return me ^ offset
    return (me + count - offset) % count


def target(me, offset, count):
    if count & (count - 1) == 0:
        return me ^ offset
    return (me + offset) % count


def stack_kernel(*refs):
    *held_refs, out_ref = refs
    for offset, ref in enumerate(held_refs):
        out_ref[source(lax.axis_index("grp"), offset, len(held_refs))] = ref[...]


def route_kernel(blocks_ref, mine_ref, other_ref, *refs):
    *out_refs, held_ref = refs
    chips = len(out_refs)
    groups, slots = mine_ref.shape[:2]
    per_device = slots - 1
    slabs = chips * CORES
    group = lax.axis_index("grp")
    chip, core = div_rem(lax.axis_index("slab"), CORES)
    held_ref[core] = mine_ref[...]
    held_ref[1 - core] = other_ref[...]
    step = AVG // 2 // groups
    lane = lax.broadcasted_iota(jnp.int32, (8, AVG), 1) & (AVG // 2 - 1)
    for owner_core in range(CORES):
        ends = held_ref[owner_core, 0, per_device].astype(F32)
        for owner_group in range(1, groups):
            rolled = pltpu.roll(held_ref[owner_core, owner_group, per_device].astype(F32), owner_group * step, 1)
            ends = jnp.where(lane >= owner_group * step, rolled, ends)
        for out_ref in out_refs:
            out_ref[per_device + owner_core] = ends.astype(BF16)
    for offset, out_ref in enumerate(out_refs):
        wanted = (group * slabs + target(chip, offset, chips) * CORES + core) * per_device
        for slot in range(per_device):
            owner, index = div_rem(blocks_ref[wanted + slot], per_device)
            owner_group, owner_slab = div_rem(owner, slabs)
            out_ref[slot] = held_ref[div_rem(owner_slab, CORES)[1], owner_group, index]


def transfer_order(chips):
    return [*range(2, chips), *range(1, min(chips, 2)), 0]


def place_kernel(blocks_ref, *refs, groups, chips, blk):
    (*got_refs, ids_ref, point_ref, window_ref, _, table_hbm, fluctuation_hbm, held_ref, ends_ref,
     edge_ref, table_ref, sems) = refs
    slots = got_refs[0].shape[0]
    per_device = slots - CORES
    slabs = chips * CORES
    devices = groups * slabs
    grains = table_ref.shape[1]
    step = AVG // 2 // groups
    device = device_index()
    chip = div_rem(lax.axis_index("slab"), CORES)[0]
    lane = lax.broadcasted_iota(jnp.int32, (8, AVG), 1)
    half = lane < blk

    for offset, ref in zip(transfer_order(chips), got_refs):
        owner_chip = source(chip, offset, chips)
        held_ref[owner_chip] = ref[...]
        for core in range(CORES):
            piece = ref[per_device + core].astype(F32)
            piece = piece + pltpu.roll(piece, AVG - 4, 1) + pltpu.roll(piece, AVG - 8, 1)
            ends_ref[owner_chip * CORES + core] = piece

    def ends(owner, column, lane):
        group, slab = div_rem(jnp.clip(owner, 0, devices - 1), slabs)
        moved = pltpu.roll(ends_ref[slab], (lane - column - step * group + 2 * AVG) & (AVG - 1), 1)
        return jnp.where((owner >= 0) & (owner < devices), moved, 0.0)

    def unfold(value):
        return jnp.concatenate([value, pltpu.roll(value, blk, 1)], axis=0)

    lane_half = lane & (blk - 1)
    others = jnp.where(lane_half < 2, ends(device - 1, 2, 0), ends(device + 1, 0, 2))
    shared = finish(unfold(ends(device, 0, 0) + others))
    wide_lane = lax.broadcasted_iota(jnp.int32, (ROWS, AVG), 1)
    windows = window_ref.shape[0]
    first = jnp.where(wide_lane < 2, shared, window_ref[0])
    in_last = (wide_lane >= SUB) & (wide_lane < SUB + 2)
    last = pltpu.roll(window_ref[windows - 1], AVG - grains // windows + SUB, 1)
    last = jnp.where(in_last, pltpu.roll(shared, SUB - 2, 1), last)
    width = EDGE * AVG
    first_grain = device * grains - 1
    copies = []
    for end, (table, tile, grain) in enumerate(
        ((first, 0, first_grain), (last, grains - EDGE, first_grain + grains - SUB))
    ):
        lanes = slice(end * width, (end + 1) * width)
        points = slice(tile * AVG, tile * AVG + width)
        picks = selection(ids_ref, tile, EDGE, grain)
        means = jnp.dot(table[:, :WINDOW].astype(BF16), picks, preferred_element_type=F32)
        edge_ref[:, lanes] = (point_ref[:, points] - means)[:COUNT].astype(BF16)
        copies.append(
            pltpu.make_async_copy(
                edge_ref.at[:, lanes], fluctuation_hbm.at[:, points], sems.at[end]
            )
        )

    tiles, columns = [], []
    sums = jnp.zeros((8, AVG), F32)
    for slot in range(per_device):
        owner, index = div_rem(blocks_ref[device * per_device + slot], per_device)
        owner_chip = div_rem(div_rem(owner, slabs)[1], CORES)[0]
        tiles.append(held_ref[owner_chip, slot].astype(F32))
        low = index == 0
        beside = jnp.where(low, owner - 1, owner + 1)
        both = ends(owner, jnp.where(low, 1, 2), slot) + ends(beside, jnp.where(low, 3, 0), slot)
        sums = jnp.where(lane_half == slot, both, sums)
        columns.append(jnp.where(low, 0, jnp.where(index == per_device - 1, blk - 1, 2 * AVG)))
    repaired = finish(unfold(sums))
    repaired = jnp.where(half, repaired[:8], pltpu.roll(repaired[8:], blk, 1))
    for slot in range(per_device):
        moved = pltpu.roll(repaired, (columns[slot] - slot + AVG) & (AVG - 1), 1)
        tiles[slot] = jnp.where(lane_half == columns[slot], moved, tiles[slot])
    for pair in range(per_device // 2):
        first, second = tiles[2 * pair], tiles[2 * pair + 1]
        lanes = slice(pair * AVG, (pair + 1) * AVG)
        table_ref[:8, lanes] = jnp.where(half, first, pltpu.roll(second, blk, 1))
        table_ref[8:, lanes] = jnp.where(half, pltpu.roll(first, blk, 1), second)[: COUNT - 8]
    copies.insert(0, pltpu.make_async_copy(table_ref, table_hbm, sems.at[2]))
    for copy in copies:
        copy.start()
    for copy in copies:
        copy.wait()


def local(grain_ids, orientation, stress, owner_blocks):
    groups, slabs = lax.axis_size("grp"), lax.axis_size("slab")
    points = grain_ids.shape[0]
    tiles = points // AVG
    grains = tiles
    per_device = owner_blocks.shape[0] // (groups * slabs)
    blk = grains // per_device
    slots = per_device + 1
    chips = slabs // CORES

    ids = grain_ids.reshape(tiles, AVG)
    quads = orientation.reshape(4, tiles, AVG).transpose(1, 0, 2).reshape(4 * tiles, AVG)
    in_hbm = [pltpu.with_memory_space_constraint(x, pltpu.HBM) for x in (ids, quads, stress, owner_blocks)]
    smem = pl.BlockSpec(memory_space=pltpu.SMEM)
    vmem = pl.BlockSpec(memory_space=pltpu.VMEM)
    hbm = pl.BlockSpec(memory_space=pltpu.HBM)
    params = pltpu.CompilerParams(vmem_limit_bytes=20 << 20)

    cuts = [tiles * part // CUTS[-1] for part in CUTS]
    table, windows, point, blocks, on_chip_ids = pl.pallas_call(
        functools.partial(sum_kernel, cuts=cuts, blk=blk),
        out_shape=[
            jax.ShapeDtypeStruct((slots, 8, AVG), BF16),
            jax.ShapeDtypeStruct((tiles // blk, ROWS, AVG), F32),
            jax.ShapeDtypeStruct((ROWS, points), F32),
            pltpu.SMEM(owner_blocks.shape, jnp.int32),
            jax.ShapeDtypeStruct((tiles, AVG), jnp.int32),
        ],
        in_specs=[hbm] * 4,
        out_specs=[vmem, vmem, vmem, smem, vmem],
        scratch_shapes=[
            pltpu.VMEM((4 * tiles, AVG), F32),
            pltpu.VMEM((9, points), F32),
            pltpu.VMEM((grains + AVG, AVG), F32),
            pltpu.SemaphoreType.DMA((3, len(cuts) - 1)),
            pltpu.SemaphoreType.DMA,
        ],
        compiler_params=params,
        cost_estimate=pl.CostEstimate(
            flops=64 * points * ROWS, bytes_accessed=4 * points * ROWS, transcendentals=0
        ),
        name="sums",
    )(*in_hbm)
    blocks = pltpu.with_memory_space_constraint(blocks, pltpu.SMEM)

    held = [table]
    for offset in range(1, groups):
        moves = [(g, int(target(g, offset, groups))) for g in range(groups)]
        held.append(lax.ppermute(table, "grp", moves))

    on_chip = (on_chip_ids, point, windows)
    count = tiles // blk

    def look_up(begin, end, earlier):
        share = (end - begin) * points // count
        return pl.pallas_call(
            functools.partial(fluctuation_kernel, begin=begin, end=end),
            out_shape=jax.ShapeDtypeStruct((COUNT, points), BF16),
            in_specs=[vmem] * 3 + [hbm] * len(earlier),
            out_specs=hbm,
            scratch_shapes=[pltpu.VMEM((COUNT, share), BF16), pltpu.SemaphoreType.DMA((end - begin,))],
            input_output_aliases={3: 0} if earlier else {},
            compiler_params=params,
            cost_estimate=pl.CostEstimate(
                flops=64 * share * ROWS, bytes_accessed=6 * share * ROWS, transcendentals=0
            ),
            name="fluctuation",
        )(*on_chip, *earlier)

    fluctuation = look_up(0, count // 2, [])
    held, fluctuation = lax.optimization_barrier((held, fluctuation))
    mine = pl.pallas_call(
        stack_kernel,
        out_shape=jax.ShapeDtypeStruct((groups, slots, 8, AVG), BF16),
        in_specs=[vmem] * groups,
        out_specs=vmem,
        compiler_params=params,
        name="stack",
    )(*held)
    other = lax.ppermute(mine, "slab", [(s, s ^ 1) for s in range(slabs)])
    sent = pl.pallas_call(
        route_kernel,
        out_shape=[jax.ShapeDtypeStruct((per_device + CORES, 8, AVG), BF16)] * chips,
        in_specs=[smem, vmem, vmem],
        out_specs=[vmem] * chips,
        scratch_shapes=[pltpu.VMEM((CORES, groups, slots, 8, AVG), BF16)],
        compiler_params=params,
        name="route",
    )(blocks, mine, other)
    sent, fluctuation = lax.optimization_barrier((sent, fluctuation))
    fluctuation = look_up(count // 2, count, [fluctuation])
    got = [sent[0]]
    for offset in reversed(range(1, chips)):
        moves = [
            (chip * CORES + core, int(target(chip, offset, chips)) * CORES + core)
            for chip in range(chips)
            for core in range(CORES)
        ]
        got.insert(1, lax.ppermute(sent[offset], "slab", moves))
    grain_table, fluctuation = pl.pallas_call(
        functools.partial(place_kernel, groups=groups, chips=chips, blk=blk),
        out_shape=[
            jax.ShapeDtypeStruct((COUNT, grains), F32),
            jax.ShapeDtypeStruct((COUNT, points), BF16),
        ],
        in_specs=[smem] + [vmem] * (chips + 3) + [hbm],
        out_specs=[hbm, hbm],
        scratch_shapes=[
            pltpu.VMEM((chips, per_device + CORES, 8, AVG), BF16),
            pltpu.VMEM((slabs, 8, AVG), F32),
            pltpu.VMEM((COUNT, 2 * EDGE * AVG), BF16),
            pltpu.VMEM((COUNT, grains), F32),
            pltpu.SemaphoreType.DMA((3,)),
        ],
        input_output_aliases={chips + 4: 1},
        compiler_params=params,
        name="place",
    )(blocks, *(got[offset] for offset in transfer_order(chips)), *on_chip, fluctuation)
    return (grain_table, fluctuation)


def solution(mesh):
    placed = (P(AXES), P(None, AXES), P(None, AXES), P())
    return jax.shard_map(
        local,
        mesh=mesh,
        in_specs=placed,
        out_specs=(P(None, AXES), P(None, AXES)),
        check_vma=False,
    )
```
